256 devices in a mesh: gx: 8 (over y, core), yz: 32 (over x, z).
Axes of the slice: x: 4, y: 4, z: 8, core: 2. Of those that a mesh axis runs over, the one named last changes fastest.
Arguments:
- guess: float32 [64, 512, 512], P('gx', 'yz'), may hold values from -6 to 6
- rhs: float32 [64, 512, 512], P('gx', 'yz'), may hold values from -6 to 6
- alpha: float32 [64, 512, 512], P('gx', 'yz'), may hold values from 1 to 4
- beta: float32 [64, 512, 512], P('gx', 'yz'), may hold values from 0.25 to 1
Outputs:
- corrected: float32 [64, 512, 512], P('gx', 'yz')
- coarsest_rhs: float32 [16, 128, 128], P(None, 'yz')
The draws below stay inside these ranges and needn't reach their ends.
All inputs are finite; a program needn't handle non-finite values.
Results may differ from the reference program's by a relative error of at most 0.000068.
Values sent between devices are 32-bit elements; how exact they have to be, the bound alone decides.
A program may use at most 64 MiB of HBM per device.

```python
import math
import jax
import jax.numpy as jnp

DEGREE = 4
NX = 64
NY = 512
NZ = 512


def draw_rhs(key, part):
    values = jnp.clip(jax.random.normal(key, (NX, NY, NZ), jnp.float32), -5.0, 5.0)
    return values


def steps_of(own_key, shape, shards, low, largest):
    def one(dim, blocks):
        steps = jax.random.uniform(jax.random.fold_in(jax.random.fold_in(own_key, 6), dim), (blocks,), jnp.float32, low / len(shards), largest / len(shards))
        return jnp.repeat(jnp.exp(steps), shape[dim] // blocks).reshape((-1,) + (1,) * (len(shape) - dim - 1))

    factor_of = one(*shards[0])
    for cut in shards[1:]:
        factor_of = factor_of * one(*cut)
    return factor_of


def noise(key, dims, deviation, limit, split=(), kind=jnp.bfloat16):
    entries = jax.random.normal(key, dims, jnp.float32) * deviation
    if len(split) > 0:
        entries = steps_of(key, dims, split, -0.22, 0.18) * entries
    return jnp.clip(entries, min=-limit, max=limit).astype(kind)


def setup_inputs(seed: int = 0) -> dict:
    key_of = jax.random.split(jax.random.key(seed), 5)
    guess = noise(key_of[0], (NX, NY, NZ), 1.0, 6.0, ((0, 8), (1, 32)), jnp.float32)
    rhs = draw_rhs(jax.random.fold_in(key_of[4], 71), 0)
    alpha = jnp.clip(jnp.exp(math.log(4.0) - 1.3862944 * jax.random.uniform(key_of[2], (NX, NY, NZ), jnp.float32) ** steps_of(key_of[2], (NX, NY, NZ), ((0, 8), (1, 32)), -0.2, 0.2)), 1.0, 4.0)
    beta = jnp.clip(jnp.exp(math.log(1.0) - 1.3862944 * jax.random.uniform(key_of[3], (NX, NY, NZ), jnp.float32) ** steps_of(key_of[3], (NX, NY, NZ), ((0, 8), (1, 32)), -0.2, 0.2)), 0.25, 1.0)
    return {"guess": guess, "rhs": rhs, "alpha": alpha, "beta": beta}


THETA = 1.125
DELTA = 0.875


def cheb_terms():
    sigma = THETA / DELTA
    rho_prev = 1.0 / sigma
    terms = []
    for step in range(DEGREE - 1):
        rho_next = 1.0 / (2.0 * sigma - rho_prev)
        terms.append((rho_next * rho_prev, 2.0 * rho_next / DELTA))
        rho_prev = rho_next
    return terms


def zero_pad(field):
    return jnp.pad(field, 1)


def face_coeffs(beta, padded):
    return (0.5 * (beta + padded[2:, 1:-1, 1:-1]), 0.5 * (beta + padded[:-2, 1:-1, 1:-1]),
            0.5 * (beta + padded[1:-1, 2:, 1:-1]), 0.5 * (beta + padded[1:-1, :-2, 1:-1]),
            0.5 * (beta + padded[1:-1, 1:-1, 2:]), 0.5 * (beta + padded[1:-1, 1:-1, :-2]))


def operate(field, padded, alpha, faces, scale):
    terms = faces[0] * (field - padded[2:, 1:-1, 1:-1]) + faces[1] * (field - padded[:-2, 1:-1, 1:-1])
    terms = terms + faces[2] * (field - padded[1:-1, 2:, 1:-1]) + faces[3] * (field - padded[1:-1, :-2, 1:-1])
    terms = terms + faces[4] * (field - padded[1:-1, 1:-1, 2:]) + faces[5] * (field - padded[1:-1, 1:-1, :-2])
    return alpha * field + scale * terms


def smooth(start, source, alpha, faces, scale, pad_fn, from_zero):
    total = faces[0] + faces[1] + faces[2] + faces[3] + faces[4] + faces[5]
    inverse = 1.0 / (alpha + scale * total)
    if from_zero:
        resid = inverse * source
    else:
        resid = inverse * (source - operate(start, pad_fn(start), alpha, faces, scale))
    update = resid * (1.0 / THETA)
    field = start + update
    for first, second in cheb_terms():
        resid = inverse * (source - operate(field, pad_fn(field), alpha, faces, scale))
        update = first * update + second * resid
        field = field + update
    return field


def restrict(field):
    size_a, size_b, size_c = field.shape
    blocks = field.reshape(size_a // 2, 2, size_b // 2, 2, size_c // 2, 2)
    return jnp.sum(blocks, axis=(1, 3, 5)) * 0.125


def prolong(field):
    size_a, size_b, size_c = field.shape
    wide = jnp.broadcast_to(field[:, None, :, None, :, None], (size_a, 2, size_b, 2, size_c, 2))
    return wide.reshape(2 * size_a, 2 * size_b, 2 * size_c)


def reference(guess, rhs, alpha, beta):
    faces = face_coeffs(beta, zero_pad(beta))
    smoothed = smooth(guess, rhs, alpha, faces, 1.0, zero_pad, False)
    fine_resid = rhs - operate(smoothed, zero_pad(smoothed), alpha, faces, 1.0)
    coarse_rhs = restrict(fine_resid)
    coarse_alpha = restrict(alpha)
    coarse_beta = restrict(beta)
    coarse_faces = face_coeffs(coarse_beta, zero_pad(coarse_beta))
    coarse_x = smooth(jnp.zeros_like(coarse_rhs), coarse_rhs, coarse_alpha, coarse_faces, 0.25, zero_pad, True)
    coarse_resid = coarse_rhs - operate(coarse_x, zero_pad(coarse_x), coarse_alpha, coarse_faces, 0.25)
    return smoothed + prolong(coarse_x), restrict(coarse_resid)
```

```python
import functools

import jax
import jax.numpy as jnp
from jax import lax
from jax.experimental import pallas as pl
from jax.experimental.pallas import tpu as pltpu
from jax.sharding import PartitionSpec as P

DEGREE = 4
THETA = 1.125
DELTA = 0.875
MESH = pl.DeviceIdType.MESH
F32 = jnp.float32

NX, NY, NZ = 8, 16, 512
CX, CY, CZ = 4, 8, 256
ROUNDS = DEGREE + 1


def cheb_terms():
    sigma = THETA / DELTA
    rho_prev = 1.0 / sigma
    terms = []
    for _ in range(DEGREE - 1):
        rho_next = 1.0 / (2.0 * sigma - rho_prev)
        terms.append((rho_next * rho_prev, 2.0 * rho_next / DELTA))
        rho_prev = rho_next
    return terms


def lanes(shape):
    return lax.broadcasted_iota(jnp.int32, shape, 1)


def rows(shape):
    return lax.broadcasted_iota(jnp.int32, shape, 0)


def halve_z(field):
    count, width = field.shape
    lane = lanes((count, 128))
    even = jnp.where(lane < 64, 2 * lane, 2 * lane - 128)
    low = lane < 64
    tiles = []
    for t in range(width // 256):
        halves = []
        for h in range(2):
            part = field[:, (2 * t + h) * 128 : (2 * t + h + 1) * 128]
            part = part + pltpu.roll(part, 127, 1)
            halves.append(jnp.take_along_axis(part, even, axis=1))
        tiles.append(jnp.where(low, halves[0], halves[1]))
    return tiles[0] if len(tiles) == 1 else jnp.concatenate(tiles, axis=1)


def double_z(field):
    count, width = field.shape
    half = lanes((count, 128)) // 2
    tiles = []
    for t in range(width // 128):
        part = field[:, t * 128 : (t + 1) * 128]
        tiles.append(jnp.take_along_axis(part, half, axis=1))
        tiles.append(jnp.take_along_axis(part, half + 64, axis=1))
    return jnp.concatenate(tiles, axis=1)


def z_beside(field):
    width = field.shape[1]
    return pltpu.roll(field, width - 1, 1), pltpu.roll(field, 1, 1)


def y_beside(field, below, above):
    count = field.shape[0]
    row = rows(field.shape)
    up = jnp.where(row == count - 1, jnp.broadcast_to(above, field.shape), pltpu.roll(field, count - 1, 0))
    down = jnp.where(row == 0, jnp.broadcast_to(below, field.shape), pltpu.roll(field, 1, 0))
    return up, down


def kernel(
    guess_h, rhs_h, alpha_h, beta_h, out_ref, last_ref,
    gb, rhs, alpha, xs, ds, gs, diag, ws, hx, hy, sy, hx0, hy0, sy0,
    pair, wide, cab, cg, cw, cxs, cds, cdiag, coarsest,
    load_sem, sx_sem, rx_sem, sy_sem, ry_sem, sab_sem, rab_sem, sg_sem, rg_sem, sl_sem, rl_sem,
):
    gx = lax.axis_index("gx")
    yz = lax.axis_index("yz")
    ngx = lax.axis_size("gx")
    nyz = lax.axis_size("yz")

    def at(dx, dy):
        return (lax.rem(gx + ngx + dx, ngx), lax.rem(yz + nyz + dy, nyz))

    loads = []
    for k, (src, dst) in enumerate(
        ((guess_h, gb.at[0]), (beta_h, gb.at[1]), (alpha_h, alpha), (rhs_h, rhs))
    ):
        copy = pltpu.make_async_copy(src, dst, load_sem.at[k])
        copy.start()
        loads.append(copy)

    around = [(dx, dy) for dx in (-1, 0, 1) for dy in (-1, 0, 1) if (dx, dy) != (0, 0)]
    peers = [(dx, 0) for dx in range(1, 8)]
    greet = [at(dx, dy) for dx, dy in peers] + [at(dx, dy) for dx, dy in around if dy != 0]
    barrier = pltpu.get_barrier_semaphore()
    for device in greet:
        pl.semaphore_signal(barrier, inc=1, device_id=device, device_id_type=MESH)
    loads[0].wait()
    loads[1].wait()
    for f in range(2):
        for p in range(NX):
            sy0[0, f, p : p + 1, :] = gb[f, p, NY - 1 : NY, :]
            sy0[1, f, p : p + 1, :] = gb[f, p, 0:1, :]
    pl.semaphore_wait(barrier, len(greet))

    sent, done = [], []

    def send(src, dst, s_sem, r_sem, device):
        copy = pltpu.make_async_remote_copy(
            src_ref=src, dst_ref=dst, send_sem=s_sem, recv_sem=r_sem, device_id=device, device_id_type=MESH
        )
        copy.start()
        sent.append(copy)
        return copy

    waits = [
        send(sy0.at[0], hy0.at[0], sy_sem.at[0, 0], ry_sem.at[0, 0], at(0, 1)),
        send(sy0.at[1], hy0.at[1], sy_sem.at[0, 1], ry_sem.at[0, 1], at(0, -1)),
        send(gb.at[:, NX - 1], hx0.at[0], sx_sem.at[0, 0], rx_sem.at[0, 0], at(1, 0)),
        send(gb.at[:, 0], hx0.at[1], sx_sem.at[0, 1], rx_sem.at[0, 1], at(-1, 0)),
    ]

    loads[2].wait()
    loads[3].wait()

    def restrict_pair(first, second):
        both = first + second
        for t in range(4):
            pair[t] = both[:, t * 128 : (t + 1) * 128]
        summed = jnp.concatenate(
            [pair[t, pl.ds(0, CY, 2), :] + pair[t, pl.ds(1, CY, 2), :] for t in range(4)], axis=1
        )
        return halve_z(summed)

    for q in range(CX):
        cab[1, 1, 0, q] = 0.125 * restrict_pair(alpha[2 * q], alpha[2 * q + 1])
        cab[1, 1, 1, q] = 0.125 * restrict_pair(gb[1, 2 * q], gb[1, 2 * q + 1])
    ab_waits = [
        send(cab.at[1, 1], cab.at[1 - dx, 1 - dy], sab_sem.at[k], rab_sem.at[k], at(dx, dy))
        for k, (dx, dy) in enumerate(around)
    ]

    in_lo_x = (gx > 0).astype(F32)
    in_hi_x = (gx < ngx - 1).astype(F32)
    in_lo_y = (yz > 0).astype(F32)
    in_hi_y = (yz < nyz - 1).astype(F32)

    for copy in waits:
        copy.wait_recv()

    terms = [(None, 1.0 / THETA)] + cheb_terms()

    def spread(x_at, below, above, w):
        x = x_at(0)
        up, down = y_beside(x, below, above)
        right, left = z_beside(x)
        return (
            w(0) * x_at(1) + w(1) * x_at(-1) + w(2) * up + w(3) * down + w(4) * right + w(5) * left
        )

    lane = lanes((NY, NZ))
    row = rows((NY, NZ))
    for p in range(NX):
        b = gb[1, p]
        b_hi = gb[1, p + 1] if p < NX - 1 else hx0[1, 1] * in_hi_x
        b_lo = gb[1, p - 1] if p > 0 else hx0[0, 1] * in_lo_x
        b_up, b_down = y_beside(
            b, hy0[0, 1, p : p + 1, :] * in_lo_y, hy0[1, 1, p : p + 1, :] * in_hi_y
        )
        b_right, b_left = z_beside(b)
        b_right = jnp.where(lane == NZ - 1, 0.0, b_right)
        b_left = jnp.where(lane == 0, 0.0, b_left)
        faces = [0.5 * (b + other) for other in (b_hi, b_lo, b_up, b_down, b_right, b_left)]
        total = faces[0] + faces[1] + faces[2] + faces[3] + faces[4] + faces[5]
        whole = alpha[p] + total
        diag[p] = whole
        inverse = 1.0 / whole
        w = [inverse * face for face in faces]
        if p == NX - 1:
            w[0] = w[0] * in_hi_x
        if p == 0:
            w[1] = w[1] * in_lo_x
        w[2] = jnp.where(row == NY - 1, w[2] * in_hi_y, w[2])
        w[3] = jnp.where(row == 0, w[3] * in_lo_y, w[3])
        w[4] = jnp.where(lane == NZ - 1, 0.0, w[4])
        w[5] = jnp.where(lane == 0, 0.0, w[5])
        for e in range(6):
            ws[e, p] = w[e]
        g = inverse * rhs[p]
        gs[p] = g

        def x_at(step, p=p):
            if p + step < 0:
                return hx0[0, 0]
            if p + step >= NX:
                return hx0[1, 0]
            return gb[0, p + step]

        x = gb[0, p]
        resid = g - x + spread(x_at, hy0[0, 0, p : p + 1, :], hy0[1, 0, p : p + 1, :], lambda e: w[e])
        update = resid * (1.0 / THETA)
        ds[p] = update
        xs[0, p] = x + update

    def post(r, cur):
        for p in range(NX):
            sy[r, 0, p : p + 1, :] = xs[cur, p, NY - 1 : NY, :]
            sy[r, 1, p : p + 1, :] = xs[cur, p, 0:1, :]
        return [
            send(sy.at[r, 0], hy.at[r, 0], sy_sem.at[r + 1, 0], ry_sem.at[r + 1, 0], at(0, 1)),
            send(sy.at[r, 1], hy.at[r, 1], sy_sem.at[r + 1, 1], ry_sem.at[r + 1, 1], at(0, -1)),
            send(xs.at[cur, NX - 1], hx.at[r, 0], sx_sem.at[r + 1, 0], rx_sem.at[r + 1, 0], at(1, 0)),
            send(xs.at[cur, 0], hx.at[r, 1], sx_sem.at[r + 1, 1], rx_sem.at[r + 1, 1], at(-1, 0)),
        ]

    def residual(r, cur, p):
        def x_at(step):
            if p + step < 0:
                return hx[r, 0]
            if p + step >= NX:
                return hx[r, 1]
            return xs[cur, p + step]

        return (
            gs[p]
            - xs[cur, p]
            + spread(x_at, hy[r, 0, p : p + 1, :], hy[r, 1, p : p + 1, :], lambda e: ws[e, p])
        )

    slot_in_x = (in_lo_x, None, in_hi_x)
    slot_in_y = (in_lo_y, None, in_hi_y)

    def slot_mask(i, j):
        masks = [m for m in (slot_in_x[i], slot_in_y[j]) if m is not None]
        if not masks:
            return None
        return masks[0] if len(masks) == 1 else masks[0] * masks[1]

    def masked(value, i, j):
        mask = slot_mask(i, j)
        return value if mask is None else value * mask

    def coarse_y(get, i, q, j):
        here = get(i, j, q)
        below = get(i, j - 1, q)[CY - 1 : CY, :] if j > 0 else here[0:1, :]
        above = get(i, j + 1, q)[0:1, :] if j < 2 else here[CY - 1 : CY, :]
        return y_beside(here, below, above)

    def coarse_slots(depth):
        found = []
        for plane in range(-depth, CX + depth):
            beyond = max(-plane, plane - CX + 1, 0)
            i, q = (plane + CX) // CX, (plane + CX) % CX
            for j in (0, 1, 2) if beyond < depth else (1,):
                found.append((plane, i, q, j))
        return found

    def coarse_setup():
        clane = lanes((CY, CZ))

        def beta(i, j, q):
            return masked(cab[i, j, 1, q], i, j)

        for plane, i, q, j in coarse_slots(3):
            b = beta(i, j, q)
            hi, lo = plane + 1 + CX, plane - 1 + CX
            b_hi = beta(hi // CX, j, hi % CX)
            b_lo = beta(lo // CX, j, lo % CX)
            b_up, b_down = coarse_y(beta, i, q, j)
            b_right, b_left = z_beside(b)
            b_right = jnp.where(clane == CZ - 1, 0.0, b_right)
            b_left = jnp.where(clane == 0, 0.0, b_left)
            faces = [0.5 * (b + other) for other in (b_hi, b_lo, b_up, b_down, b_right, b_left)]
            total = faces[0] + faces[1] + faces[2] + faces[3] + faces[4] + faces[5]
            whole = cab[i, j, 0, q] + 0.25 * total
            if (i, j) == (1, 1):
                cdiag[q] = whole
            scale = masked(0.25 / whole, i, j)
            w = [scale * face for face in faces]
            w[4] = jnp.where(clane == CZ - 1, 0.0, w[4])
            w[5] = jnp.where(clane == 0, 0.0, w[5])
            for e in range(6):
                cw[e, i, j, q] = w[e]

    cur = 0
    for r in range(ROUNDS - 1):
        round_waits = post(r, cur)
        if r == 1:
            for copy in ab_waits:
                copy.wait_recv()
            coarse_setup()
        for copy in round_waits:
            copy.wait_recv()
        if r > 0:
            for copy in earlier:
                copy.wait_send()
                done.append(id(copy))
        earlier = round_waits[2:]
        if r < ROUNDS - 2:
            first, second = terms[r + 1]
            for p in range(NX):
                update = first * ds[p] + second * residual(r, cur, p)
                ds[p] = update
                xs[1 - cur, p] = xs[cur, p] + update
            cur = 1 - cur
        else:
            for q in range(CX):
                a = diag[2 * q] * residual(r, cur, 2 * q)
                b = diag[2 * q + 1] * residual(r, cur, 2 * q + 1)
                cg[1, 1, q] = 0.125 * restrict_pair(a, b) / cdiag[q]

    g_waits = [
        send(cg.at[1, 1], cg.at[1 - dx, 1 - dy], sg_sem.at[k], rg_sem.at[k], at(dx, dy))
        for k, (dx, dy) in enumerate(around)
    ]
    for copy in g_waits:
        copy.wait_recv()

    def coarse_g(i, j, q):
        return masked(cg[i, j, q], i, j)

    for plane, i, q, j in coarse_slots(4):
        update = coarse_g(i, j, q) * (1.0 / THETA)
        cxs[0, i, j, q] = update
        cds[i, j, q] = update

    def coarse_residual(now, plane, i, q, j):
        def get(i, j, q):
            return cxs[now, i, j, q]

        x = get(i, j, q)
        hi, lo = plane + 1 + CX, plane - 1 + CX
        up, down = coarse_y(get, i, q, j)
        right, left = z_beside(x)
        return (
            coarse_g(i, j, q) - x
            + cw[0, i, j, q] * get(hi // CX, j, hi % CX)
            + cw[1, i, j, q] * get(lo // CX, j, lo % CX)
            + cw[2, i, j, q] * up
            + cw[3, i, j, q] * down
            + cw[4, i, j, q] * right
            + cw[5, i, j, q] * left
        )

    now = 0
    for step, (first, second) in enumerate(cheb_terms()):
        for plane, i, q, j in coarse_slots(3 - step):
            update = first * cds[i, j, q] + second * coarse_residual(now, plane, i, q, j)
            cds[i, j, q] = update
            cxs[1 - now, i, j, q] = cxs[now, i, j, q] + update
        now = 1 - now

    quarter = []
    for q in range(CX):
        quarter.append(cdiag[q] * coarse_residual(now, q, 1, q, 1))
    for h in range(CX // 2):
        both = quarter[2 * h] + quarter[2 * h + 1]
        for t in range(2):
            pair[t, 0:CY, :] = both[:, t * 128 : (t + 1) * 128]
        summed = jnp.concatenate(
            [pair[t, pl.ds(0, CY // 2, 2), :] + pair[t, pl.ds(1, CY // 2, 2), :] for t in range(2)], axis=1
        )
        coarsest[0, h] = 0.125 * halve_z(summed)
    l_waits = [
        send(coarsest.at[0], coarsest.at[dx], sl_sem.at[dx], rl_sem.at[dx], at(dx, 0)) for dx in range(1, 8)
    ]

    for q in range(CX):
        fine = double_z(cxs[now, 1, 1, q])
        for t in range(4):
            part = fine[:, t * 128 : (t + 1) * 128]
            wide[t, pl.ds(0, CY, 2), :] = part
            wide[t, pl.ds(1, CY, 2), :] = part
        full = jnp.concatenate([wide[t] for t in range(4)], axis=1)
        for p in (2 * q, 2 * q + 1):
            out_ref[p] = xs[cur, p] + full

    for copy in l_waits:
        copy.wait_recv()
    for dx in range(8):
        owner = lax.rem(gx + ngx - dx, ngx)
        last_ref[pl.ds(2 * owner, 2)] = coarsest[dx]
    for copy in sent:
        if id(copy) not in done:
            copy.wait_send()


def on_device(guess, rhs, alpha, beta):
    vmem = pltpu.VMEM
    dma = pltpu.SemaphoreType.DMA
    fine = (NX, NY, NZ)
    scratch = [
        vmem((2, *fine), F32), vmem(fine, F32), vmem(fine, F32), vmem((2, *fine), F32), vmem(fine, F32),
        vmem(fine, F32), vmem(fine, F32), vmem((6, *fine), F32),
        vmem((ROUNDS - 1, 2, NY, NZ), F32), vmem((ROUNDS - 1, 2, NX, NZ), F32), vmem((ROUNDS - 1, 2, NX, NZ), F32),
        vmem((2, 2, NY, NZ), F32), vmem((2, 2, NX, NZ), F32), vmem((2, 2, NX, NZ), F32),
        vmem((4, NY, 128), F32), vmem((4, NY, 128), F32),
        vmem((3, 3, 2, CX, CY, CZ), F32), vmem((3, 3, CX, CY, CZ), F32), vmem((6, 3, 3, CX, CY, CZ), F32),
        vmem((2, 3, 3, CX, CY, CZ), F32), vmem((3, 3, CX, CY, CZ), F32), vmem((CX, CY, CZ), F32),
        vmem((8, 2, CY // 2, CZ // 2), F32),
        dma((4,)), dma((ROUNDS, 2)), dma((ROUNDS, 2)), dma((ROUNDS, 2)), dma((ROUNDS, 2)),
        dma((8,)), dma((8,)), dma((8,)), dma((8,)), dma((8,)), dma((8,)),
    ]
    return pl.pallas_call(
        kernel,
        out_shape=(
            jax.ShapeDtypeStruct(fine, F32),
            jax.ShapeDtypeStruct((16, CY // 2, CZ // 2), F32),
        ),
        in_specs=[pl.BlockSpec(memory_space=pltpu.HBM)] * 4,
        out_specs=(pl.BlockSpec(memory_space=vmem), pl.BlockSpec(memory_space=vmem)),
        scratch_shapes=scratch,
        compiler_params=pltpu.CompilerParams(
            collective_id=0, has_side_effects=True, vmem_limit_bytes=60 << 20
        ),
        name="vcycle",
    )(guess, rhs, alpha, beta)


def solution(mesh):
    placed = (P("gx", "yz", None),) * 4
    return jax.shard_map(
        on_device,
        mesh=mesh,
        in_specs=placed,
        out_specs=(P("gx", "yz", None), P(None, "yz", None)),
        check_vma=False,
    )
```

```python
import functools

import jax
import jax.numpy as jnp
from jax import lax
from jax.experimental import pallas as pl
from jax.experimental.pallas import tpu as pltpu
from jax.sharding import PartitionSpec as P

DEGREE = 4
THETA = 1.125
DELTA = 0.875
MESH = pl.DeviceIdType.MESH
F32 = jnp.float32

NX, NY, NZ = 8, 16, 512
CX, CY, CZ = 4, 8, 256
DEPTH = DEGREE + 1
PX, PY = DEPTH, 8
EX, EY = NX + 2 * DEPTH, NY + 2 * PY


def cheb_terms():
    sigma = THETA / DELTA
    rho_prev = 1.0 / sigma
    terms = []
    for _ in range(DEGREE - 1):
        rho_next = 1.0 / (2.0 * sigma - rho_prev)
        terms.append((rho_next * rho_prev, 2.0 * rho_next / DELTA))
        rho_prev = rho_next
    return terms


def lanes(shape):
    return lax.broadcasted_iota(jnp.int32, shape, 1)


def rows(shape):
    return lax.broadcasted_iota(jnp.int32, shape, 0)


def halve_z(field):
    count, width = field.shape
    lane = lanes((count, 128))
    even = jnp.where(lane < 64, 2 * lane, 2 * lane - 128)
    low = lane < 64
    tiles = []
    for t in range(width // 256):
        halves = []
        for h in range(2):
            part = field[:, (2 * t + h) * 128 : (2 * t + h + 1) * 128]
            part = part + pltpu.roll(part, 127, 1)
            halves.append(jnp.take_along_axis(part, even, axis=1))
        tiles.append(jnp.where(low, halves[0], halves[1]))
    return tiles[0] if len(tiles) == 1 else jnp.concatenate(tiles, axis=1)


def double_z(field):
    count, width = field.shape
    half = lanes((count, 128)) // 2
    tiles = []
    for t in range(width // 128):
        part = field[:, t * 128 : (t + 1) * 128]
        tiles.append(jnp.take_along_axis(part, half, axis=1))
        tiles.append(jnp.take_along_axis(part, half + 64, axis=1))
    return jnp.concatenate(tiles, axis=1)


def z_beside(field):
    width = field.shape[1]
    return pltpu.roll(field, width - 1, 1), pltpu.roll(field, 1, 1)


def y_beside(field, below, above):
    count = field.shape[0]
    row = rows(field.shape)
    up = jnp.where(row == count - 1, jnp.broadcast_to(above, field.shape), pltpu.roll(field, count - 1, 0))
    down = jnp.where(row == 0, jnp.broadcast_to(below, field.shape), pltpu.roll(field, 1, 0))
    return up, down


def tile_a(p):
    return 2 * p + (1 if p >= 4 else 0)


def tile_b(p):
    return 2 * p + (0 if p >= 4 else 1)


def kernel(
    guess_h, rhs_h, alpha_h, beta_h, out_ref, last_ref,
    xa, xb, be, al, rh, ds, gs, diag, ws, pk, rk, rc,
    pair, wide, cab, cg, cw, cxs, cds, cdiag, coarsest,
    load_sem, sx_sem, rx_sem, sy_sem, ry_sem, sc_sem, rc_sem, sab_sem, rab_sem, sg_sem, rg_sem, sl_sem, rl_sem,
):
    gx = lax.axis_index("gx")
    yz = lax.axis_index("yz")
    ngx = lax.axis_size("gx")
    nyz = lax.axis_size("yz")

    def at(dx, dy):
        return (lax.rem(gx + ngx + dx, ngx), lax.rem(yz + nyz + dy, nyz))

    around = [(dx, dy) for dx in (-1, 0, 1) for dy in (-1, 0, 1) if (dx, dy) != (0, 0)]
    peers = [(dx, 0) for dx in range(1, 8)]
    greet = [at(dx, dy) for dx, dy in peers] + [at(dx, dy) for dx, dy in around if dy != 0]
    barrier = pltpu.get_barrier_semaphore()
    for device in greet:
        pl.semaphore_signal(barrier, inc=1, device_id=device, device_id_type=MESH)

    own_x, own_y = pl.ds(PX, NX), pl.ds(PY, NY)
    loads = []
    for k, (src, dst) in enumerate(((guess_h, xa), (beta_h, be), (alpha_h, al), (rhs_h, rh))):
        copy = pltpu.make_async_copy(src, dst.at[own_x, own_y], load_sem.at[k])
        copy.start()
        loads.append(copy)
    for copy in loads:
        copy.wait()

    half = rows((8, NZ)) < 4

    def packed(first, second, side):
        moved = pltpu.roll(second, 4, 0)
        return jnp.where(half, moved, first) if side == 0 else jnp.where(half, first, moved)

    for side, start, fifth in ((0, PY + 8, PY + 11), (1, PY, PY + 4)):
        tile = pl.ds(start, 8)
        for p in range(NX):
            pk[side, tile_a(p)] = packed(xa[PX + p, tile, :], be[PX + p, tile, :], side)
            pk[side, tile_b(p)] = packed(al[PX + p, tile, :], rh[PX + p, tile, :], side)
            pk[side, 16, p : p + 1, :] = xa[PX + p, fifth : fifth + 1, :]
            pk[side, 17, p : p + 1, :] = be[PX + p, fifth : fifth + 1, :]
    pl.semaphore_wait(barrier, len(greet))

    sent = []

    def send(src, dst, s_sem, r_sem, device):
        copy = pltpu.make_async_remote_copy(
            src_ref=src, dst_ref=dst, send_sem=s_sem, recv_sem=r_sem, device_id=device, device_id_type=MESH
        )
        copy.start()
        sent.append(copy)
        return copy

    y_waits = [
        send(pk.at[side], rk.at[side], sy_sem.at[side], ry_sem.at[side], at(0, 1 - 2 * side)) for side in (0, 1)
    ]
    c_waits = []
    for sx in (0, 1):
        for sy in (0, 1):
            part = pl.ds(9, 7) if sx == 0 else pl.ds(0, 7)
            c_waits.append(
                send(
                    pk.at[sy, part], rc.at[sx, sy], sc_sem.at[sx, sy], rc_sem.at[sx, sy],
                    at(1 - 2 * sx, 1 - 2 * sy),
                )
            )
    x_waits = []
    for k, (src, dst, deep) in enumerate(
        ((guess_h, xa, DEPTH), (beta_h, be, DEPTH), (alpha_h, al, DEPTH - 1), (rhs_h, rh, DEPTH - 1))
    ):
        x_waits.append(
            send(
                src.at[pl.ds(NX - deep, deep)], dst.at[pl.ds(PX - deep, deep), own_y],
                sx_sem.at[k, 0], rx_sem.at[k, 0], at(1, 0),
            )
        )
        x_waits.append(
            send(
                src.at[pl.ds(0, deep)], dst.at[pl.ds(PX + NX, deep), own_y],
                sx_sem.at[k, 1], rx_sem.at[k, 1], at(-1, 0),
            )
        )

    def restrict_pair(first, second):
        both = first + second
        for t in range(4):
            pair[t] = both[:, t * 128 : (t + 1) * 128]
        summed = jnp.concatenate(
            [pair[t, pl.ds(0, CY, 2), :] + pair[t, pl.ds(1, CY, 2), :] for t in range(4)], axis=1
        )
        return halve_z(summed)

    for q in range(CX):
        one, two = PX + 2 * q, PX + 2 * q + 1
        cab[1, 1, 0, q] = 0.125 * restrict_pair(al[one, own_y, :], al[two, own_y, :])
        cab[1, 1, 1, q] = 0.125 * restrict_pair(be[one, own_y, :], be[two, own_y, :])
    ab_waits = [
        send(cab.at[1, 1], cab.at[1 - dx, 1 - dy], sab_sem.at[k], rab_sem.at[k], at(dx, dy))
        for k, (dx, dy) in enumerate(around)
    ]

    in_lo_x = (gx > 0).astype(F32)
    in_hi_x = (gx < ngx - 1).astype(F32)
    in_lo_y = (yz > 0).astype(F32)
    in_hi_y = (yz < nyz - 1).astype(F32)
    terms = cheb_terms()

    for copy in y_waits + c_waits + x_waits:
        copy.wait_recv()

    sub = rows((8, NZ))
    for side, start, fifth in ((0, 0, 3), (1, PY + NY, 4)):
        tile = pl.ds(start, 8)
        inside = in_lo_y if side == 0 else in_hi_y
        for p in range(NX):
            a = rk[side, tile_a(p)] * inside
            deep = rk[side, 16, p : p + 1, :] * inside
            xa[PX + p, tile, :] = jnp.where(sub == fifth, jnp.broadcast_to(deep, a.shape), a)
            deep = rk[side, 17, p : p + 1, :] * inside
            be[PX + p, tile, :] = jnp.where(sub == fifth, jnp.broadcast_to(deep, a.shape), pltpu.roll(a, 4, 0))
            b = rk[side, tile_b(p)]
            al[PX + p, tile, :] = b
            rh[PX + p, tile, :] = pltpu.roll(b, 4, 0)
        for sx in (0, 1):
            shift = 9 if sx == 0 else 0
            for p in range(4, 8) if sx == 0 else range(4):
                plane = PX + p - NX if sx == 0 else PX + p + NX
                a = rc[sx, side, tile_a(p) - shift] * inside
                xa[plane, tile, :] = a
                be[plane, tile, :] = pltpu.roll(a, 4, 0)
                if p not in (3, 4):
                    b = rc[sx, side, tile_b(p) - shift]
                    al[plane, tile, :] = b
                    rh[plane, tile, :] = pltpu.roll(b, 4, 0)

    for edge, start in ((gx == 0, 0), (gx == ngx - 1, PX + NX)):

        @pl.when(edge)
        def _(start=start):
            for plane in range(start, start + DEPTH):
                xa[plane] = jnp.zeros((EY, NZ), F32)
                be[plane] = jnp.zeros((EY, NZ), F32)

    def fine_blocks(deep):
        found = []
        for p in range(-deep, NX + deep):
            beyond = max(-p, p - NX + 1, 0)
            found.append((p, (0, EY) if beyond < deep else (PY, PY + NY)))
        return found

    def spread(x, x_at, span, w):
        if span == (0, EY):
            up, down = pltpu.roll(x, EY - 1, 0), pltpu.roll(x, 1, 0)
        else:
            up, down = y_beside(x, x_at(0, (PY - 1, PY)), x_at(0, (PY + NY, PY + NY + 1)))
        right, left = z_beside(x)
        return (
            w(0) * x_at(1, span) + w(1) * x_at(-1, span) + w(2) * up + w(3) * down + w(4) * right + w(5) * left
        )

    for p, span in fine_blocks(DEPTH - 1):
        lo, hi = span
        here = pl.ds(lo, hi - lo)
        shape = (hi - lo, NZ)
        lane = lanes(shape)
        b = be[PX + p, here, :]
        if span == (0, EY):
            b_up, b_down = pltpu.roll(b, EY - 1, 0), pltpu.roll(b, 1, 0)
        else:
            b_up, b_down = y_beside(b, be[PX + p, PY - 1 : PY, :], be[PX + p, PY + NY : PY + NY + 1, :])
        b_right, b_left = z_beside(b)
        b_right = jnp.where(lane == NZ - 1, 0.0, b_right)
        b_left = jnp.where(lane == 0, 0.0, b_left)
        faces = [
            0.5 * (b + other)
            for other in (be[PX + p + 1, here, :], be[PX + p - 1, here, :], b_up, b_down, b_right, b_left)
        ]
        total = faces[0] + faces[1] + faces[2] + faces[3] + faces[4] + faces[5]
        whole = al[PX + p, here, :] + total
        if 0 <= p < NX:
            diag[p] = whole[PY - lo : PY - lo + NY]
        inverse = 1.0 / whole
        if p < 0:
            inverse = inverse * in_lo_x
        if p >= NX:
            inverse = inverse * in_hi_x
        if span == (0, EY):
            row = rows(shape)
            inside = jnp.where(row < PY, in_lo_y, jnp.where(row >= PY + NY, in_hi_y, 1.0))
            inverse = inverse * inside
        w = [inverse * face for face in faces]
        w[4] = jnp.where(lane == NZ - 1, 0.0, w[4])
        w[5] = jnp.where(lane == 0, 0.0, w[5])
        for e in range(6):
            ws[e, PX + p, here, :] = w[e]
        g = inverse * rh[PX + p, here, :]
        gs[PX + p, here, :] = g
        x = xa[PX + p, here, :]
        resid = g - x + spread(x, lambda step, part: xa[PX + p + step, part[0] : part[1], :], span, lambda e: w[e])
        update = resid * (1.0 / THETA)
        ds[PX + p, here, :] = update
        xb[PX + p, here, :] = x + update

    def residual(cur, p, span):
        here = pl.ds(span[0], span[1] - span[0])
        x = cur[PX + p, here, :]
        return (
            gs[PX + p, here, :]
            - x
            + spread(
                x, lambda step, part: cur[PX + p + step, part[0] : part[1], :], span,
                lambda e: ws[e, PX + p, here, :],
            )
        )

    slot_in_x = (in_lo_x, None, in_hi_x)
    slot_in_y = (in_lo_y, None, in_hi_y)

    def slot_mask(i, j):
        masks = [m for m in (slot_in_x[i], slot_in_y[j]) if m is not None]
        if not masks:
            return None
        return masks[0] if len(masks) == 1 else masks[0] * masks[1]

    def masked(value, i, j):
        mask = slot_mask(i, j)
        return value if mask is None else value * mask

    def coarse_y(get, i, q, j):
        here = get(i, j, q)
        below = get(i, j - 1, q)[CY - 1 : CY, :] if j > 0 else here[0:1, :]
        above = get(i, j + 1, q)[0:1, :] if j < 2 else here[CY - 1 : CY, :]
        return y_beside(here, below, above)

    def coarse_slots(depth):
        found = []
        for plane in range(-depth, CX + depth):
            beyond = max(-plane, plane - CX + 1, 0)
            i, q = (plane + CX) // CX, (plane + CX) % CX
            for j in (0, 1, 2) if beyond < depth else (1,):
                found.append((plane, i, q, j))
        return found

    def coarse_setup(own_only):
        clane = lanes((CY, CZ))

        def beta(i, j, q):
            return masked(cab[i, j, 1, q], i, j)

        for plane, i, q, j in coarse_slots(0 if own_only else 3):
            b = beta(i, j, q)
            hi, lo = plane + 1 + CX, plane - 1 + CX
            b_hi = beta(hi // CX, j, hi % CX)
            b_lo = beta(lo // CX, j, lo % CX)
            b_up, b_down = coarse_y(beta, i, q, j)
            b_right, b_left = z_beside(b)
            b_right = jnp.where(clane == CZ - 1, 0.0, b_right)
            b_left = jnp.where(clane == 0, 0.0, b_left)
            faces = [0.5 * (b + other) for other in (b_hi, b_lo, b_up, b_down, b_right, b_left)]
            total = faces[0] + faces[1] + faces[2] + faces[3] + faces[4] + faces[5]
            whole = cab[i, j, 0, q] + 0.25 * total
            if own_only:
                cdiag[q] = whole
                continue
            scale = masked(0.25 / whole, i, j)
            w = [scale * face for face in faces]
            w[4] = jnp.where(clane == CZ - 1, 0.0, w[4])
            w[5] = jnp.where(clane == 0, 0.0, w[5])
            for e in range(6):
                cw[e, i, j, q] = w[e]

    cur, other = xb, xa
    for step, (first, second) in enumerate(terms):
        for p, span in fine_blocks(DEPTH - 2 - step):
            here = pl.ds(span[0], span[1] - span[0])
            update = first * ds[PX + p, here, :] + second * residual(cur, p, span)
            ds[PX + p, here, :] = update
            other[PX + p, here, :] = cur[PX + p, here, :] + update
        cur, other = other, cur
    own = (PY, PY + NY)
    for copy in ab_waits:
        copy.wait_recv()
    coarse_setup(True)
    for q in range(CX):
        a = diag[2 * q] * residual(cur, 2 * q, own)
        b = diag[2 * q + 1] * residual(cur, 2 * q + 1, own)
        cg[1, 1, q] = 0.125 * restrict_pair(a, b) / cdiag[q]

    g_waits = [
        send(cg.at[1, 1], cg.at[1 - dx, 1 - dy], sg_sem.at[k], rg_sem.at[k], at(dx, dy))
        for k, (dx, dy) in enumerate(around)
    ]
    coarse_setup(False)
    for copy in g_waits:
        copy.wait_recv()

    def coarse_g(i, j, q):
        return masked(cg[i, j, q], i, j)

    for plane, i, q, j in coarse_slots(4):
        update = coarse_g(i, j, q) * (1.0 / THETA)
        cxs[0, i, j, q] = update
        cds[i, j, q] = update

    def coarse_residual(now, plane, i, q, j):
        def get(i, j, q):
            return cxs[now, i, j, q]

        x = get(i, j, q)
        hi, lo = plane + 1 + CX, plane - 1 + CX
        up, down = coarse_y(get, i, q, j)
        right, left = z_beside(x)
        return (
            coarse_g(i, j, q) - x
            + cw[0, i, j, q] * get(hi // CX, j, hi % CX)
            + cw[1, i, j, q] * get(lo // CX, j, lo % CX)
            + cw[2, i, j, q] * up
            + cw[3, i, j, q] * down
            + cw[4, i, j, q] * right
            + cw[5, i, j, q] * left
        )

    now = 0
    for step, (first, second) in enumerate(cheb_terms()):
        for plane, i, q, j in coarse_slots(3 - step):
            update = first * cds[i, j, q] + second * coarse_residual(now, plane, i, q, j)
            cds[i, j, q] = update
            cxs[1 - now, i, j, q] = cxs[now, i, j, q] + update
        now = 1 - now

    quarter = []
    for q in range(CX):
        quarter.append(cdiag[q] * coarse_residual(now, q, 1, q, 1))
    for h in range(CX // 2):
        both = quarter[2 * h] + quarter[2 * h + 1]
        for t in range(2):
            pair[t, 0:CY, :] = both[:, t * 128 : (t + 1) * 128]
        summed = jnp.concatenate(
            [pair[t, pl.ds(0, CY // 2, 2), :] + pair[t, pl.ds(1, CY // 2, 2), :] for t in range(2)], axis=1
        )
        coarsest[0, h] = 0.125 * halve_z(summed)
    l_waits = [
        send(coarsest.at[0], coarsest.at[dx], sl_sem.at[dx], rl_sem.at[dx], at(dx, 0)) for dx in range(1, 8)
    ]

    for q in range(CX):
        fine = double_z(cxs[now, 1, 1, q])
        for t in range(4):
            part = fine[:, t * 128 : (t + 1) * 128]
            wide[t, pl.ds(0, CY, 2), :] = part
            wide[t, pl.ds(1, CY, 2), :] = part
        full = jnp.concatenate([wide[t] for t in range(4)], axis=1)
        for p in (2 * q, 2 * q + 1):
            out_ref[p] = cur[PX + p, own_y, :] + full

    for copy in l_waits:
        copy.wait_recv()
    for dx in range(8):
        owner = lax.rem(gx + ngx - dx, ngx)
        last_ref[pl.ds(2 * owner, 2)] = coarsest[dx]
    for copy in sent:
        copy.wait_send()


def on_device(guess, rhs, alpha, beta):
    vmem = pltpu.VMEM
    dma = pltpu.SemaphoreType.DMA
    fine = (NX, NY, NZ)
    wide = (EX, EY, NZ)
    scratch = [
        vmem(wide, F32), vmem(wide, F32), vmem(wide, F32), vmem(wide, F32), vmem(wide, F32), vmem(wide, F32),
        vmem(wide, F32), vmem(fine, F32), vmem((6, *wide), F32),
        vmem((2, 18, 8, NZ), F32), vmem((2, 18, 8, NZ), F32), vmem((2, 2, 7, 8, NZ), F32),
        vmem((4, NY, 128), F32), vmem((4, NY, 128), F32),
        vmem((3, 3, 2, CX, CY, CZ), F32), vmem((3, 3, CX, CY, CZ), F32), vmem((6, 3, 3, CX, CY, CZ), F32),
        vmem((2, 3, 3, CX, CY, CZ), F32), vmem((3, 3, CX, CY, CZ), F32), vmem((CX, CY, CZ), F32),
        vmem((8, 2, CY // 2, CZ // 2), F32),
        dma((4,)), dma((4, 2)), dma((4, 2)), dma((2,)), dma((2,)), dma((2, 2)), dma((2, 2)),
        dma((8,)), dma((8,)), dma((8,)), dma((8,)), dma((8,)), dma((8,)),
    ]
    placed = [pltpu.with_memory_space_constraint(x, pltpu.HBM) for x in (guess, rhs, alpha, beta)]
    return pl.pallas_call(
        kernel,
        out_shape=(
            jax.ShapeDtypeStruct(fine, F32),
            jax.ShapeDtypeStruct((16, CY // 2, CZ // 2), F32),
        ),
        in_specs=[pl.BlockSpec(memory_space=pltpu.HBM)] * 4,
        out_specs=(pl.BlockSpec(memory_space=vmem), pl.BlockSpec(memory_space=vmem)),
        scratch_shapes=scratch,
        compiler_params=pltpu.CompilerParams(
            collective_id=0, has_side_effects=True, vmem_limit_bytes=40 << 20
        ),
        name="vcycle",
    )(*placed)


def solution(mesh):
    placed = (P("gx", "yz", None),) * 4
    return jax.shard_map(
        on_device,
        mesh=mesh,
        in_specs=placed,
        out_specs=(P("gx", "yz", None), P(None, "yz", None)),
        check_vma=False,
    )
```

```python
import functools

import jax
import jax.numpy as jnp
from jax import lax
from jax.experimental import pallas as pl
from jax.experimental.pallas import tpu as pltpu
from jax.sharding import PartitionSpec as P

DEGREE = 4
THETA = 1.125
DELTA = 0.875
MESH = pl.DeviceIdType.MESH
F32 = jnp.float32

NX, NY, NZ = 8, 16, 512
CX, CY, CZ = 4, 8, 256
DEPTH = DEGREE + 1
PX, PY = DEPTH, 8
EX, EY = NX + 2 * DEPTH, NY + 2 * PY


def cheb_terms():
    sigma = THETA / DELTA
    rho_prev = 1.0 / sigma
    terms = []
    for _ in range(DEGREE - 1):
        rho_next = 1.0 / (2.0 * sigma - rho_prev)
        terms.append((rho_next * rho_prev, 2.0 * rho_next / DELTA))
        rho_prev = rho_next
    return terms


def lanes(shape):
    return lax.broadcasted_iota(jnp.int32, shape, 1)


def rows(shape):
    return lax.broadcasted_iota(jnp.int32, shape, 0)


def halve_z(field):
    count, width = field.shape
    lane = lanes((count, 128))
    even = jnp.where(lane < 64, 2 * lane, 2 * lane - 128)
    low = lane < 64
    tiles = []
    for t in range(width // 256):
        halves = []
        for h in range(2):
            part = field[:, (2 * t + h) * 128 : (2 * t + h + 1) * 128]
            part = part + pltpu.roll(part, 127, 1)
            halves.append(jnp.take_along_axis(part, even, axis=1))
        tiles.append(jnp.where(low, halves[0], halves[1]))
    return tiles[0] if len(tiles) == 1 else jnp.concatenate(tiles, axis=1)


def double_z(field):
    count, width = field.shape
    half = lanes((count, 128)) // 2
    tiles = []
    for t in range(width // 128):
        part = field[:, t * 128 : (t + 1) * 128]
        tiles.append(jnp.take_along_axis(part, half, axis=1))
        tiles.append(jnp.take_along_axis(part, half + 64, axis=1))
    return jnp.concatenate(tiles, axis=1)


def z_beside(field):
    width = field.shape[1]
    return pltpu.roll(field, width - 1, 1), pltpu.roll(field, 1, 1)


def y_beside(field, below, above):
    count = field.shape[0]
    row = rows(field.shape)
    up = jnp.where(row == count - 1, jnp.broadcast_to(above, field.shape), pltpu.roll(field, count - 1, 0))
    down = jnp.where(row == 0, jnp.broadcast_to(below, field.shape), pltpu.roll(field, 1, 0))
    return up, down


def tile_a(p):
    return 2 * p + (1 if p >= 4 else 0)


def tile_b(p):
    return 2 * p + (0 if p >= 4 else 1)


def kernel(
    guess_h, rhs_h, alpha_h, beta_h, out_ref, last_ref,
    xa, xb, be, al, rh, ds, gs, diag, ws, pk, rk, rc,
    pair, wide, cab, cg, cw, cxs, cds, cdiag, coarsest,
    load_sem, sx_sem, rx_sem, sy_sem, ry_sem, sc_sem, rc_sem, sab_sem, rab_sem, sg_sem, rg_sem, sl_sem, rl_sem,
):
    gx = lax.axis_index("gx")
    yz = lax.axis_index("yz")
    ngx = lax.axis_size("gx")
    nyz = lax.axis_size("yz")

    def at(dx, dy):
        return (lax.rem(gx + ngx + dx, ngx), lax.rem(yz + nyz + dy, nyz))

    beside = {-1: yz > 0, 0: None, 1: yz < nyz - 1}

    def when(condition, act):
        if condition is None:
            act()
        else:
            pl.when(condition)(act)

    def greet(dx, dy):
        pl.semaphore_signal(barrier, inc=1, device_id=at(dx, dy), device_id_type=MESH)

    around = [(dx, dy) for dx in (-1, 0, 1) for dy in (-1, 0, 1) if (dx, dy) != (0, 0)]
    barrier = pltpu.get_barrier_semaphore()
    for dx in range(1, 8):
        greet(dx, 0)
    for dx, dy in around:
        if dy != 0:
            when(beside[dy], functools.partial(greet, dx, dy))
    greeted = 7 + 3 * (yz > 0).astype(jnp.int32) + 3 * (yz < nyz - 1).astype(jnp.int32)

    own_x, own_y = pl.ds(PX, NX), pl.ds(PY, NY)
    loads = []
    for k, (src, dst) in enumerate(((guess_h, xa), (beta_h, be), (alpha_h, al), (rhs_h, rh))):
        copy = pltpu.make_async_copy(src, dst.at[own_x, own_y], load_sem.at[k])
        copy.start()
        loads.append(copy)
    for copy in loads:
        copy.wait()

    half = rows((8, NZ)) < 4

    def packed(first, second, side):
        moved = pltpu.roll(second, 4, 0)
        return jnp.where(half, moved, first) if side == 0 else jnp.where(half, first, moved)

    for side, start, fifth in ((0, PY + 8, PY + 11), (1, PY, PY + 4)):
        tile = pl.ds(start, 8)
        for p in range(NX):
            pk[side, tile_a(p)] = packed(xa[PX + p, tile, :], be[PX + p, tile, :], side)
            pk[side, tile_b(p)] = packed(al[PX + p, tile, :], rh[PX + p, tile, :], side)
            pk[side, 16, p : p + 1, :] = xa[PX + p, fifth : fifth + 1, :]
            pk[side, 17, p : p + 1, :] = be[PX + p, fifth : fifth + 1, :]
    for side, missing in ((0, yz == 0), (1, yz == nyz - 1)):

        @pl.when(missing)
        def _(side=side):
            rk[side] = jnp.ones(rk.shape[1:], F32)
            for k in range(3):
                if k < 2:
                    rc[k, side] = jnp.ones(rc.shape[2:], F32)
                cab[k, 2 * side] = jnp.ones(cab.shape[2:], F32)
                cg[k, 2 * side] = jnp.ones(cg.shape[2:], F32)

    pl.semaphore_wait(barrier, greeted)

    sent, corners_sent = [], []

    def copy_of(src, dst, s_sem, r_sem, device):
        return pltpu.make_async_remote_copy(
            src_ref=src, dst_ref=dst, send_sem=s_sem, recv_sem=r_sem, device_id=device, device_id_type=MESH
        )

    def send(src, dst, s_sem, r_sem, dx, dy):
        copy = copy_of(src, dst, s_sem, r_sem, at(dx, dy))
        when(beside[dy], copy.start)
        sent.append((copy, dy))
        return copy, dy

    def wait_for(copies):
        for copy, dy in copies:
            when(beside[-dy], copy.wait_recv)

    y_waits = [
        send(pk.at[side], rk.at[side], sy_sem.at[side], ry_sem.at[side], 0, 1 - 2 * side) for side in (0, 1)
    ]
    first_core = lax.rem(gx, 2) == 0
    c_waits, relays = [], ([], [])
    for sx in (0, 1):
        part = pl.ds(9, 7) if sx == 0 else pl.ds(0, 7)
        same_chip = first_core if sx == 0 else jnp.logical_not(first_core)
        for sy in (0, 1):
            dy = 1 - 2 * sy
            sems = (sc_sem.at[sx, sy], rc_sem.at[sx, sy])
            straight = copy_of(pk.at[sy, part], rc.at[sx, sy], *sems, at(1 - 2 * sx, dy))
            relay = copy_of(rk.at[sy, part], rc.at[sx, sy], *sems, at(1 - 2 * sx, 0))
            pl.when(jnp.logical_and(jnp.logical_not(same_chip), beside[dy]))(straight.start)
            relays[sy].append((relay, jnp.logical_and(same_chip, beside[-dy])))
            c_waits.append((straight, dy))
            gone = jnp.logical_or(
                jnp.logical_and(same_chip, beside[-dy]), jnp.logical_and(jnp.logical_not(same_chip), beside[dy])
            )
            corners_sent.append((straight, gone))
    x_waits = []
    for k, (src, dst, deep) in enumerate(
        ((guess_h, xa, DEPTH), (beta_h, be, DEPTH), (alpha_h, al, DEPTH - 1), (rhs_h, rh, DEPTH - 1))
    ):
        x_waits.append(
            send(
                src.at[pl.ds(NX - deep, deep)], dst.at[pl.ds(PX - deep, deep), own_y],
                sx_sem.at[k, 0], rx_sem.at[k, 0], 1, 0,
            )
        )
        x_waits.append(
            send(
                src.at[pl.ds(0, deep)], dst.at[pl.ds(PX + NX, deep), own_y],
                sx_sem.at[k, 1], rx_sem.at[k, 1], -1, 0,
            )
        )

    def restrict_pair(first, second):
        both = first + second
        for t in range(4):
            pair[t] = both[:, t * 128 : (t + 1) * 128]
        summed = jnp.concatenate(
            [pair[t, pl.ds(0, CY, 2), :] + pair[t, pl.ds(1, CY, 2), :] for t in range(4)], axis=1
        )
        return halve_z(summed)

    for q in range(CX):
        one, two = PX + 2 * q, PX + 2 * q + 1
        cab[1, 1, 0, q] = 0.125 * restrict_pair(al[one, own_y, :], al[two, own_y, :])
        cab[1, 1, 1, q] = 0.125 * restrict_pair(be[one, own_y, :], be[two, own_y, :])
    ab_waits = [
        send(cab.at[1, 1], cab.at[1 - dx, 1 - dy], sab_sem.at[k], rab_sem.at[k], dx, dy)
        for k, (dx, dy) in enumerate(around)
    ]

    in_lo_x = (gx > 0).astype(F32)
    in_hi_x = (gx < ngx - 1).astype(F32)
    in_lo_y = (yz > 0).astype(F32)
    in_hi_y = (yz < nyz - 1).astype(F32)
    terms = cheb_terms()

    sub = rows((8, NZ))
    sides = ((0, 0, 3, in_lo_y), (1, PY + NY, 4, in_hi_y))

    def place_rows():
        for side, start, fifth, inside in sides:
            tile = pl.ds(start, 8)
            for p in range(NX):
                a = rk[side, tile_a(p)] * inside
                deep = rk[side, 16, p : p + 1, :] * inside
                xa[PX + p, tile, :] = jnp.where(sub == fifth, jnp.broadcast_to(deep, a.shape), a)
                deep = rk[side, 17, p : p + 1, :] * inside
                be[PX + p, tile, :] = jnp.where(sub == fifth, jnp.broadcast_to(deep, a.shape), pltpu.roll(a, 4, 0))
                b = rk[side, tile_b(p)]
                al[PX + p, tile, :] = b
                rh[PX + p, tile, :] = pltpu.roll(b, 4, 0)

    def place_corners():
        for side, start, _, inside in sides:
            tile = pl.ds(start, 8)
            for sx in (0, 1):
                shift = 9 if sx == 0 else 0
                for p in range(4, 8) if sx == 0 else range(4):
                    plane = PX + p - NX if sx == 0 else PX + p + NX
                    a = rc[sx, side, tile_a(p) - shift] * inside
                    xa[plane, tile, :] = a
                    be[plane, tile, :] = pltpu.roll(a, 4, 0)
                    if p not in (3, 4):
                        b = rc[sx, side, tile_b(p) - shift]
                        al[plane, tile, :] = b
                        rh[plane, tile, :] = pltpu.roll(b, 4, 0)
        for edge, start in ((gx == 0, 0), (gx == ngx - 1, PX + NX)):

            @pl.when(edge)
            def _(start=start):
                for plane in range(start, start + DEPTH):
                    xa[plane] = jnp.zeros((EY, NZ), F32)
                    be[plane] = jnp.zeros((EY, NZ), F32)

    def fine_blocks(deep):
        found = []
        for p in range(-deep, NX + deep):
            beyond = max(-p, p - NX + 1, 0)
            found.append((p, (0, EY) if beyond < deep else (PY, PY + NY)))
        return found

    def spread(x, x_at, span, w):
        if span == (0, EY):
            up, down = pltpu.roll(x, EY - 1, 0), pltpu.roll(x, 1, 0)
        else:
            up, down = y_beside(x, x_at(0, (PY - 1, PY)), x_at(0, (PY + NY, PY + NY + 1)))
        right, left = z_beside(x)
        return (
            w(0) * x_at(1, span) + w(1) * x_at(-1, span) + w(2) * up + w(3) * down + w(4) * right + w(5) * left
        )

    def first_step(p, span):
        lo, hi = span
        here = pl.ds(lo, hi - lo)
        shape = (hi - lo, NZ)
        lane = lanes(shape)
        b = be[PX + p, here, :]
        if span == (0, EY):
            b_up, b_down = pltpu.roll(b, EY - 1, 0), pltpu.roll(b, 1, 0)
        else:
            b_up, b_down = y_beside(b, be[PX + p, PY - 1 : PY, :], be[PX + p, PY + NY : PY + NY + 1, :])
        b_right, b_left = z_beside(b)
        b_right = jnp.where(lane == NZ - 1, 0.0, b_right)
        b_left = jnp.where(lane == 0, 0.0, b_left)
        faces = [
            0.5 * (b + other)
            for other in (be[PX + p + 1, here, :], be[PX + p - 1, here, :], b_up, b_down, b_right, b_left)
        ]
        total = faces[0] + faces[1] + faces[2] + faces[3] + faces[4] + faces[5]
        whole = al[PX + p, here, :] + total
        if 0 <= p < NX:
            diag[p] = whole[PY - lo : PY - lo + NY]
        inverse = 1.0 / whole
        if p < 0:
            inverse = inverse * in_lo_x
        if p >= NX:
            inverse = inverse * in_hi_x
        if span == (0, EY):
            row = rows(shape)
            inside = jnp.where(row < PY, in_lo_y, jnp.where(row >= PY + NY, in_hi_y, 1.0))
            inverse = inverse * inside
        w = [inverse * face for face in faces]
        w[4] = jnp.where(lane == NZ - 1, 0.0, w[4])
        w[5] = jnp.where(lane == 0, 0.0, w[5])
        for e in range(6):
            ws[e, PX + p, here, :] = w[e]
        g = inverse * rh[PX + p, here, :]
        gs[PX + p, here, :] = g
        x = xa[PX + p, here, :]
        resid = g - x + spread(x, lambda step, part: xa[PX + p + step, part[0] : part[1], :], span, lambda e: w[e])
        update = resid * (1.0 / THETA)
        ds[PX + p, here, :] = update
        xb[PX + p, here, :] = x + update

    def residual(cur, p, span):
        here = pl.ds(span[0], span[1] - span[0])
        x = cur[PX + p, here, :]
        return (
            gs[PX + p, here, :]
            - x
            + spread(
                x, lambda step, part: cur[PX + p + step, part[0] : part[1], :], span,
                lambda e: ws[e, PX + p, here, :],
            )
        )

    slot_in_x = (in_lo_x, None, in_hi_x)
    slot_in_y = (in_lo_y, None, in_hi_y)

    def slot_mask(i, j):
        masks = [m for m in (slot_in_x[i], slot_in_y[j]) if m is not None]
        if not masks:
            return None
        return masks[0] if len(masks) == 1 else masks[0] * masks[1]

    def masked(value, i, j):
        mask = slot_mask(i, j)
        return value if mask is None else value * mask

    def coarse_y(get, i, q, j):
        here = get(i, j, q)
        below = get(i, j - 1, q)[CY - 1 : CY, :] if j > 0 else here[0:1, :]
        above = get(i, j + 1, q)[0:1, :] if j < 2 else here[CY - 1 : CY, :]
        return y_beside(here, below, above)

    def coarse_slots(depth):
        found = []
        for plane in range(-depth, CX + depth):
            beyond = max(-plane, plane - CX + 1, 0)
            i, q = (plane + CX) // CX, (plane + CX) % CX
            for j in (0, 1, 2) if beyond < depth else (1,):
                found.append((plane, i, q, j))
        return found

    def coarse_setup(own_only):
        clane = lanes((CY, CZ))

        def beta(i, j, q):
            return masked(cab[i, j, 1, q], i, j)

        for plane, i, q, j in coarse_slots(0 if own_only else 3):
            b = beta(i, j, q)
            hi, lo = plane + 1 + CX, plane - 1 + CX
            b_hi = beta(hi // CX, j, hi % CX)
            b_lo = beta(lo // CX, j, lo % CX)
            b_up, b_down = coarse_y(beta, i, q, j)
            b_right, b_left = z_beside(b)
            b_right = jnp.where(clane == CZ - 1, 0.0, b_right)
            b_left = jnp.where(clane == 0, 0.0, b_left)
            faces = [0.5 * (b + other) for other in (b_hi, b_lo, b_up, b_down, b_right, b_left)]
            total = faces[0] + faces[1] + faces[2] + faces[3] + faces[4] + faces[5]
            whole = cab[i, j, 0, q] + 0.25 * total
            if own_only:
                cdiag[q] = whole
                continue
            scale = masked(0.25 / whole, i, j)
            w = [scale * face for face in faces]
            w[4] = jnp.where(clane == CZ - 1, 0.0, w[4])
            w[5] = jnp.where(clane == 0, 0.0, w[5])
            for e in range(6):
                cw[e, i, j, q] = w[e]

    def later_step(step, p, span):
        cur, other = (xb, xa) if step % 2 == 1 else (xa, xb)
        first, second = terms[step - 1]
        here = pl.ds(span[0], span[1] - span[0])
        update = first * ds[PX + p, here, :] + second * residual(cur, p, span)
        ds[PX + p, here, :] = update
        other[PX + p, here, :] = cur[PX + p, here, :] + update

    def fine_step(step, chosen):
        for p, span in fine_blocks(DEPTH - 1 - step):
            if (1 + step <= p < NX - 1 - step) == chosen:
                if step == 0:
                    first_step(p, span)
                else:
                    later_step(step, p, span)

    for side in (0, 1):
        wait_for(y_waits[side : side + 1])
        for relay, passes in relays[side]:
            pl.when(passes)(relay.start)
    place_rows()
    for step in range(DEGREE):
        fine_step(step, True)
    wait_for(x_waits)
    wait_for(c_waits)
    place_corners()
    for step in range(DEGREE):
        fine_step(step, False)
    cur = xa if DEGREE % 2 == 0 else xb
    own = (PY, PY + NY)
    wait_for(ab_waits)
    coarse_setup(True)
    for q in range(CX):
        a = diag[2 * q] * residual(cur, 2 * q, own)
        b = diag[2 * q + 1] * residual(cur, 2 * q + 1, own)
        cg[1, 1, q] = 0.125 * restrict_pair(a, b) / cdiag[q]

    g_waits = [
        send(cg.at[1, 1], cg.at[1 - dx, 1 - dy], sg_sem.at[k], rg_sem.at[k], dx, dy)
        for k, (dx, dy) in enumerate(around)
    ]
    coarse_setup(False)
    wait_for(g_waits)

    def coarse_g(i, j, q):
        return masked(cg[i, j, q], i, j)

    for plane, i, q, j in coarse_slots(4):
        update = coarse_g(i, j, q) * (1.0 / THETA)
        cxs[0, i, j, q] = update
        cds[i, j, q] = update

    def coarse_residual(now, plane, i, q, j):
        def get(i, j, q):
            return cxs[now, i, j, q]

        x = get(i, j, q)
        hi, lo = plane + 1 + CX, plane - 1 + CX
        up, down = coarse_y(get, i, q, j)
        right, left = z_beside(x)
        return (
            coarse_g(i, j, q) - x
            + cw[0, i, j, q] * get(hi // CX, j, hi % CX)
            + cw[1, i, j, q] * get(lo // CX, j, lo % CX)
            + cw[2, i, j, q] * up
            + cw[3, i, j, q] * down
            + cw[4, i, j, q] * right
            + cw[5, i, j, q] * left
        )

    now = 0
    for step, (first, second) in enumerate(cheb_terms()):
        for plane, i, q, j in coarse_slots(3 - step):
            update = first * cds[i, j, q] + second * coarse_residual(now, plane, i, q, j)
            cds[i, j, q] = update
            cxs[1 - now, i, j, q] = cxs[now, i, j, q] + update
        now = 1 - now

    quarter = []
    for q in range(CX):
        quarter.append(cdiag[q] * coarse_residual(now, q, 1, q, 1))
    for h in range(CX // 2):
        both = quarter[2 * h] + quarter[2 * h + 1]
        for t in range(2):
            pair[t, 0:CY, :] = both[:, t * 128 : (t + 1) * 128]
        summed = jnp.concatenate(
            [pair[t, pl.ds(0, CY // 2, 2), :] + pair[t, pl.ds(1, CY // 2, 2), :] for t in range(2)], axis=1
        )
        coarsest[0, h] = 0.125 * halve_z(summed)
    l_waits = [
        send(coarsest.at[0], coarsest.at[dx], sl_sem.at[dx], rl_sem.at[dx], dx, 0) for dx in range(1, 8)
    ]

    for q in range(CX):
        fine = double_z(cxs[now, 1, 1, q])
        for t in range(4):
            part = fine[:, t * 128 : (t + 1) * 128]
            wide[t, pl.ds(0, CY, 2), :] = part
            wide[t, pl.ds(1, CY, 2), :] = part
        full = jnp.concatenate([wide[t] for t in range(4)], axis=1)
        for p in (2 * q, 2 * q + 1):
            out_ref[p] = cur[PX + p, own_y, :] + full

    wait_for(l_waits)
    for dx in range(8):
        owner = lax.rem(gx + ngx - dx, ngx)
        last_ref[pl.ds(2 * owner, 2)] = coarsest[dx]
    for copy, dy in sent:
        when(beside[dy], copy.wait_send)
    for copy, gone in corners_sent:
        pl.when(gone)(copy.wait_send)


def on_device(guess, rhs, alpha, beta):
    vmem = pltpu.VMEM
    dma = pltpu.SemaphoreType.DMA
    fine = (NX, NY, NZ)
    wide = (EX, EY, NZ)
    scratch = [
        vmem(wide, F32), vmem(wide, F32), vmem(wide, F32), vmem(wide, F32), vmem(wide, F32), vmem(wide, F32),
        vmem(wide, F32), vmem(fine, F32), vmem((6, *wide), F32),
        vmem((2, 18, 8, NZ), F32), vmem((2, 18, 8, NZ), F32), vmem((2, 2, 7, 8, NZ), F32),
        vmem((4, NY, 128), F32), vmem((4, NY, 128), F32),
        vmem((3, 3, 2, CX, CY, CZ), F32), vmem((3, 3, CX, CY, CZ), F32), vmem((6, 3, 3, CX, CY, CZ), F32),
        vmem((2, 3, 3, CX, CY, CZ), F32), vmem((3, 3, CX, CY, CZ), F32), vmem((CX, CY, CZ), F32),
        vmem((8, 2, CY // 2, CZ // 2), F32),
        dma((4,)), dma((4, 2)), dma((4, 2)), dma((2,)), dma((2,)), dma((2, 2)), dma((2, 2)),
        dma((8,)), dma((8,)), dma((8,)), dma((8,)), dma((8,)), dma((8,)),
    ]
    placed = [pltpu.with_memory_space_constraint(x, pltpu.HBM) for x in (guess, rhs, alpha, beta)]
    return pl.pallas_call(
        kernel,
        out_shape=(
            jax.ShapeDtypeStruct(fine, F32),
            jax.ShapeDtypeStruct((16, CY // 2, CZ // 2), F32),
        ),
        in_specs=[pl.BlockSpec(memory_space=pltpu.HBM)] * 4,
        out_specs=(pl.BlockSpec(memory_space=vmem), pl.BlockSpec(memory_space=vmem)),
        scratch_shapes=scratch,
        compiler_params=pltpu.CompilerParams(
            collective_id=0, has_side_effects=True, vmem_limit_bytes=40 << 20
        ),
        name="vcycle",
    )(*placed)


def solution(mesh):
    placed = (P("gx", "yz", None),) * 4
    return jax.shard_map(
        on_device,
        mesh=mesh,
        in_specs=placed,
        out_specs=(P("gx", "yz", None), P(None, "yz", None)),
        check_vma=False,
    )
```

```python
import functools

import jax
import jax.numpy as jnp
from jax import lax
from jax.experimental import pallas as pl
from jax.experimental.pallas import tpu as pltpu
from jax.sharding import PartitionSpec as P

DEGREE = 4
THETA = 1.125
DELTA = 0.875
MESH = pl.DeviceIdType.MESH
F32 = jnp.float32

NX, NY, NZ = 8, 16, 512
CX, CY, CZ = 4, 8, 256
DEPTH = DEGREE + 1
PX = DEPTH
EX, EY = NX + 2 * DEPTH, NY + 8
EXC, EYC = CX + 2 * DEGREE, CY + 8


def cheb_terms():
    sigma = THETA / DELTA
    rho_prev = 1.0 / sigma
    terms = []
    for _ in range(DEGREE - 1):
        rho_next = 1.0 / (2.0 * sigma - rho_prev)
        terms.append((rho_next * rho_prev, 2.0 * rho_next / DELTA))
        rho_prev = rho_next
    return terms


def lanes(shape):
    return lax.broadcasted_iota(jnp.int32, shape, 1)


def rows(shape):
    return lax.broadcasted_iota(jnp.int32, shape, 0)


def halve_z(field):
    count, width = field.shape
    lane = lanes((count, 128))
    even = jnp.where(lane < 64, 2 * lane, 2 * lane - 128)
    low = lane < 64
    tiles = []
    for t in range(width // 256):
        halves = []
        for h in range(2):
            part = field[:, (2 * t + h) * 128 : (2 * t + h + 1) * 128]
            part = part + pltpu.roll(part, 127, 1)
            halves.append(jnp.take_along_axis(part, even, axis=1))
        tiles.append(jnp.where(low, halves[0], halves[1]))
    return tiles[0] if len(tiles) == 1 else jnp.concatenate(tiles, axis=1)


def double_z(field):
    count, width = field.shape
    half = lanes((count, 128)) // 2
    tiles = []
    for t in range(width // 128):
        part = field[:, t * 128 : (t + 1) * 128]
        tiles.append(jnp.take_along_axis(part, half, axis=1))
        tiles.append(jnp.take_along_axis(part, half + 64, axis=1))
    return jnp.concatenate(tiles, axis=1)


def z_beside(field):
    width = field.shape[1]
    return pltpu.roll(field, width - 1, 1), pltpu.roll(field, 1, 1)


def y_beside(field, below, above):
    count = field.shape[0]
    row = rows(field.shape)
    up = jnp.where(row == count - 1, jnp.broadcast_to(above, field.shape), pltpu.roll(field, count - 1, 0))
    down = jnp.where(row == 0, jnp.broadcast_to(below, field.shape), pltpu.roll(field, 1, 0))
    return up, down


def tile_a(p):
    return 2 * p + (1 if p >= 4 else 0)


def tile_b(p):
    return 2 * p + (0 if p >= 4 else 1)


def kernel(
    guess_h, rhs_h, alpha_h, beta_h, out_ref, last_ref,
    xa, xb, be, al, rh, ds, gs, diag, ws, pk, rk, rc,
    pair, wide, cab, cg, pkc, rkc, cw, cxs, cds, cdiag, coarsest,
    load_sem, sx_sem, rx_sem, sy_sem, ry_sem, sc_sem, rc_sem, sab_sem, rab_sem, sg_sem, rg_sem, sl_sem, rl_sem,
):
    gx = lax.axis_index("gx")
    yz = lax.axis_index("yz")
    ngx = lax.axis_size("gx")
    nyz = lax.axis_size("yz")

    def at(dx, dy):
        return (lax.rem(gx + ngx + dx, ngx), lax.rem(yz + nyz + dy, nyz))

    beside = {-1: yz > 0, 0: None, 1: yz < nyz - 1}

    def when(condition, act):
        if condition is None:
            act()
        else:
            pl.when(condition)(act)

    def greet(dx, dy):
        pl.semaphore_signal(barrier, inc=1, device_id=at(dx, dy), device_id_type=MESH)

    around = [(dx, dy) for dx in (-1, 0, 1) for dy in (-1, 0, 1) if (dx, dy) != (0, 0)]
    barrier = pltpu.get_barrier_semaphore()
    for dx in range(1, 8):
        greet(dx, 0)
    for dx, dy in around:
        if dy != 0:
            when(beside[dy], functools.partial(greet, dx, dy))
    greeted = 7 + 3 * (yz > 0).astype(jnp.int32) + 3 * (yz < nyz - 1).astype(jnp.int32)

    own_x, own_y, edge_y = pl.ds(PX, NX), pl.ds(0, NY), pl.ds(NY, 8)
    loads = []
    for k, (src, dst) in enumerate(((guess_h, xa), (beta_h, be), (alpha_h, al), (rhs_h, rh))):
        copy = pltpu.make_async_copy(src, dst.at[own_x, own_y], load_sem.at[k])
        copy.start()
        loads.append(copy)
    for copy in loads:
        copy.wait()

    half = rows((8, NZ)) < 4

    def packed(first, second, side):
        moved = pltpu.roll(second, 4, 0)
        return jnp.where(half, moved, first) if side == 0 else jnp.where(half, first, moved)

    for side, start, fifth in ((0, 8, 11), (1, 0, 4)):
        tile = pl.ds(start, 8)
        for p in range(NX):
            pk[side, tile_a(p)] = packed(xa[PX + p, tile, :], be[PX + p, tile, :], side)
            pk[side, tile_b(p)] = packed(al[PX + p, tile, :], rh[PX + p, tile, :], side)
            pk[side, 16, p : p + 1, :] = xa[PX + p, fifth : fifth + 1, :]
            pk[side, 17, p : p + 1, :] = be[PX + p, fifth : fifth + 1, :]
    for side, missing in ((0, yz == 0), (1, yz == nyz - 1)):

        @pl.when(missing)
        def _(side=side):
            rk[side] = jnp.ones(rk.shape[1:], F32)
            for k in range(3):
                if k < 2:
                    rc[k, side] = jnp.ones(rc.shape[2:], F32)
                for f in range(3):
                    rkc[f, k, side] = jnp.ones(rkc.shape[3:], F32)

    pl.semaphore_wait(barrier, greeted)

    sent, corners_sent = [], []

    def copy_of(src, dst, s_sem, r_sem, device):
        return pltpu.make_async_remote_copy(
            src_ref=src, dst_ref=dst, send_sem=s_sem, recv_sem=r_sem, device_id=device, device_id_type=MESH
        )

    def send(src, dst, s_sem, r_sem, dx, dy):
        copy = copy_of(src, dst, s_sem, r_sem, at(dx, dy))
        when(beside[dy], copy.start)
        sent.append((copy, dy))
        return copy, dy

    def wait_for(copies):
        for copy, dy in copies:
            when(beside[-dy], copy.wait_recv)

    y_waits = [
        send(pk.at[side], rk.at[side], sy_sem.at[side], ry_sem.at[side], 0, 1 - 2 * side) for side in (0, 1)
    ]
    first_core = lax.rem(gx, 2) == 0
    c_waits, relays = [], ([], [])
    for sx in (0, 1):
        part = pl.ds(9, 7) if sx == 0 else pl.ds(0, 7)
        same_chip = first_core if sx == 0 else jnp.logical_not(first_core)
        for sy in (0, 1):
            dy = 1 - 2 * sy
            sems = (sc_sem.at[sx, sy], rc_sem.at[sx, sy])
            straight = copy_of(pk.at[sy, part], rc.at[sx, sy], *sems, at(1 - 2 * sx, dy))
            relay = copy_of(rk.at[sy, part], rc.at[sx, sy], *sems, at(1 - 2 * sx, 0))
            pl.when(jnp.logical_and(jnp.logical_not(same_chip), beside[dy]))(straight.start)
            relays[sy].append((relay, jnp.logical_and(same_chip, beside[-dy])))
            c_waits.append((straight, dy))
            gone = jnp.logical_or(
                jnp.logical_and(same_chip, beside[-dy]), jnp.logical_and(jnp.logical_not(same_chip), beside[dy])
            )
            corners_sent.append((straight, gone))
    x_waits = []
    for k, (src, dst, deep) in enumerate(
        ((guess_h, xa, DEPTH), (beta_h, be, DEPTH), (alpha_h, al, DEPTH - 1), (rhs_h, rh, DEPTH - 1))
    ):
        x_waits.append(
            send(
                src.at[pl.ds(NX - deep, deep)], dst.at[pl.ds(PX - deep, deep), own_y],
                sx_sem.at[k, 0], rx_sem.at[k, 0], 1, 0,
            )
        )
        x_waits.append(
            send(
                src.at[pl.ds(0, deep)], dst.at[pl.ds(PX + NX, deep), own_y],
                sx_sem.at[k, 1], rx_sem.at[k, 1], -1, 0,
            )
        )

    def restrict_pair(first, second):
        both = first + second
        for t in range(4):
            pair[t] = both[:, t * 128 : (t + 1) * 128]
        summed = jnp.concatenate(
            [pair[t, pl.ds(0, CY, 2), :] + pair[t, pl.ds(1, CY, 2), :] for t in range(4)], axis=1
        )
        return halve_z(summed)

    chalf = rows((8, CZ)) < 4

    def pack_coarse(f, get):
        for q in range(0, CX, 2):
            this, then = get(q), pltpu.roll(get(q + 1), 4, 0)
            pkc[f, 0, q // 2] = jnp.where(chalf, then, this)
            pkc[f, 1, q // 2] = jnp.where(chalf, this, then)

    def exchange_coarse(fields, own, others, s_sem, r_sem):
        copies = []
        for k, (dx, dy) in enumerate(around):
            if dy == 0:
                src, dst = own, others[1 - dx]
            else:
                side = (1 - dy) // 2
                src, dst = pkc.at[fields, side], rkc.at[fields, 1 - dx, side]
            copies.append(send(src, dst, s_sem.at[k], r_sem.at[k], dx, dy))
        return copies

    for q in range(CX):
        one, two = PX + 2 * q, PX + 2 * q + 1
        cab[0, CX + q, 0:CY] = 0.125 * restrict_pair(al[one, own_y, :], al[two, own_y, :])
        cab[1, CX + q, 0:CY] = 0.125 * restrict_pair(be[one, own_y, :], be[two, own_y, :])
    for f in range(2):
        pack_coarse(f, lambda q, f=f: cab[f, CX + q, 0:CY])
    slots = [pl.ds(k * CX, CX) for k in range(3)]
    ab_waits = exchange_coarse(
        pl.ds(0, 2), cab.at[:, slots[1], pl.ds(0, CY)],
        [cab.at[:, slot, pl.ds(0, CY)] for slot in slots], sab_sem, rab_sem,
    )

    in_lo_x = (gx > 0).astype(F32)
    in_hi_x = (gx < ngx - 1).astype(F32)
    in_lo_y = (yz > 0).astype(F32)
    in_hi_y = (yz < nyz - 1).astype(F32)
    terms = cheb_terms()

    def join(below, above):
        return jnp.where(half, above, below)

    def place(plane, a_below, a_above, b_below=None, b_above=None):
        a_below, a_above = a_below * in_lo_y, a_above * in_hi_y
        xa[plane, edge_y, :] = join(a_below, a_above)
        be[plane, edge_y, :] = pltpu.roll(join(a_above, a_below), 4, 0)
        if b_below is not None:
            al[plane, edge_y, :] = join(b_below, b_above)
            rh[plane, edge_y, :] = pltpu.roll(join(b_above, b_below), 4, 0)

    def place_rows():
        for p in range(NX):
            place(PX + p, rk[0, tile_a(p)], rk[1, tile_a(p)], rk[0, tile_b(p)], rk[1, tile_b(p)])

    def place_corners():
        for sx in (0, 1):
            shift = 9 if sx == 0 else 0
            for p in range(4, 8) if sx == 0 else range(4):
                plane = PX + p - NX if sx == 0 else PX + p + NX
                tiles = [tile_a(p) - shift] if p in (3, 4) else [tile_a(p) - shift, tile_b(p) - shift]
                place(plane, *(rc[sx, side, tile] for tile in tiles for side in (0, 1)))
        for edge, start in ((gx == 0, 0), (gx == ngx - 1, PX + NX)):

            @pl.when(edge)
            def _(start=start):
                for plane in range(start, start + DEPTH):
                    xa[plane] = jnp.zeros((EY, NZ), F32)
                    be[plane] = jnp.zeros((EY, NZ), F32)

    def fine_blocks(deep):
        found = []
        for p in range(-deep, NX + deep):
            beyond = max(-p, p - NX + 1, 0)
            found.append((p, (0, EY) if beyond < deep else (0, NY)))
        return found

    def along_y(x, at_row, span, own, fifth=None):
        count = own + 8
        if span == (0, own):
            return y_beside(x, at_row(count - 1), at_row(own))
        up, down = pltpu.roll(x, count - 1, 0), pltpu.roll(x, 1, 0)
        if fifth is not None:
            row = rows(x.shape)
            up = jnp.where(row == own + 3, jnp.broadcast_to(fifth[1], x.shape), up)
            down = jnp.where(row == own + 4, jnp.broadcast_to(fifth[0], x.shape), down)
        return up, down

    def spread(x, x_at, span, own, w, fifth=None):
        up, down = along_y(x, lambda row: x_at(0, (row, row + 1)), span, own, fifth)
        right, left = z_beside(x)
        return (
            w(0) * x_at(1, span) + w(1) * x_at(-1, span) + w(2) * up + w(3) * down + w(4) * right + w(5) * left
        )

    def in_rows(shape, own):
        row = rows(shape)
        return jnp.where(row < own, 1.0, jnp.where(row < own + 4, in_hi_y, in_lo_y))

    def first_step(p, span):
        lo, hi = span
        here = pl.ds(lo, hi - lo)
        shape = (hi - lo, NZ)
        lane = lanes(shape)
        b = be[PX + p, here, :]
        fifth = fifth_b = None
        if 0 <= p < NX:
            part = slice(p, p + 1)
            fifth = (rk[0, 16, part, :] * in_lo_y, rk[1, 16, part, :] * in_hi_y)
            fifth_b = (rk[0, 17, part, :] * in_lo_y, rk[1, 17, part, :] * in_hi_y)
        b_up, b_down = along_y(b, lambda row: be[PX + p, row : row + 1, :], span, NY, fifth_b)
        b_right, b_left = z_beside(b)
        b_right = jnp.where(lane == NZ - 1, 0.0, b_right)
        b_left = jnp.where(lane == 0, 0.0, b_left)
        faces = [
            0.5 * (b + other)
            for other in (be[PX + p + 1, here, :], be[PX + p - 1, here, :], b_up, b_down, b_right, b_left)
        ]
        total = faces[0] + faces[1] + faces[2] + faces[3] + faces[4] + faces[5]
        whole = al[PX + p, here, :] + total
        if 0 <= p < NX:
            diag[p] = whole[0:NY]
        inverse = 1.0 / whole
        if p < 0:
            inverse = inverse * in_lo_x
        if p >= NX:
            inverse = inverse * in_hi_x
        if span == (0, EY):
            inverse = inverse * in_rows(shape, NY)
        w = [inverse * face for face in faces]
        w[4] = jnp.where(lane == NZ - 1, 0.0, w[4])
        w[5] = jnp.where(lane == 0, 0.0, w[5])
        for e in range(6):
            ws[e, PX + p, here, :] = w[e]
        g = inverse * rh[PX + p, here, :]
        gs[PX + p, here, :] = g
        x = xa[PX + p, here, :]
        resid = g - x + spread(x, lambda step, part: xa[PX + p + step, part[0] : part[1], :], span, NY, lambda e: w[e], fifth)
        update = resid * (1.0 / THETA)
        ds[PX + p, here, :] = update
        xb[PX + p, here, :] = x + update

    def residual(cur, p, span):
        here = pl.ds(span[0], span[1] - span[0])
        x = cur[PX + p, here, :]
        return (
            gs[PX + p, here, :]
            - x
            + spread(
                x, lambda step, part: cur[PX + p + step, part[0] : part[1], :], span, NY,
                lambda e: ws[e, PX + p, here, :],
            )
        )

    def coarse_blocks(deep):
        found = []
        for p in range(-deep, CX + deep):
            beyond = max(-p, p - CX + 1, 0)
            found.append((p, CX + p, (0, EYC) if beyond < deep else (0, CY)))
        return found

    def in_planes(p):
        return in_lo_x if p < 0 else in_hi_x if p >= CX else None

    def masked(value, mask):
        return value if mask is None else value * mask

    def place_coarse(f, field, inside):
        for k in range(3):
            for q in range(0, CX, 2):
                below, above = rkc[f, k, 0, q // 2], rkc[f, k, 1, q // 2]
                if inside:
                    below, above = below * in_lo_y, above * in_hi_y
                field[k * CX + q, pl.ds(CY, 8), :] = jnp.where(chalf, above, below)
                field[k * CX + q + 1, pl.ds(CY, 8), :] = pltpu.roll(jnp.where(chalf, below, above), 4, 0)

    def coarse_setup(own_only):
        for p, at_p, span in coarse_blocks(0 if own_only else 3):
            here = pl.ds(0, span[1])
            shape = (span[1], CZ)
            clane = lanes(shape)
            b = cab[1, at_p, here, :]
            b_up, b_down = along_y(b, lambda row: cab[1, at_p, row : row + 1, :], span, CY)
            b_right, b_left = z_beside(b)
            b_right = jnp.where(clane == CZ - 1, 0.0, b_right)
            b_left = jnp.where(clane == 0, 0.0, b_left)
            faces = [
                0.5 * (b + other)
                for other in (cab[1, at_p + 1, here, :], cab[1, at_p - 1, here, :], b_up, b_down, b_right, b_left)
            ]
            total = faces[0] + faces[1] + faces[2] + faces[3] + faces[4] + faces[5]
            whole = cab[0, at_p, here, :] + 0.25 * total
            if own_only:
                cdiag[p] = whole
                continue
            scale = masked(0.25 / whole, in_planes(p))
            if span == (0, EYC):
                scale = scale * in_rows(shape, CY)
            w = [scale * face for face in faces]
            w[4] = jnp.where(clane == CZ - 1, 0.0, w[4])
            w[5] = jnp.where(clane == 0, 0.0, w[5])
            for e in range(6):
                cw[e, at_p, here, :] = w[e]

    def later_step(step, p, span):
        cur, other = (xb, xa) if step % 2 == 1 else (xa, xb)
        first, second = terms[step - 1]
        here = pl.ds(span[0], span[1] - span[0])
        update = first * ds[PX + p, here, :] + second * residual(cur, p, span)
        ds[PX + p, here, :] = update
        other[PX + p, here, :] = cur[PX + p, here, :] + update

    def fine_step(step, chosen):
        for p, span in fine_blocks(DEPTH - 1 - step):
            if (1 + step <= p < NX - 1 - step) == chosen:
                if step == 0:
                    first_step(p, span)
                else:
                    later_step(step, p, span)

    for side in (0, 1):
        wait_for(y_waits[side : side + 1])
        for relay, passes in relays[side]:
            pl.when(passes)(relay.start)
    place_rows()
    for step in range(DEGREE):
        fine_step(step, True)
    wait_for(x_waits)
    wait_for(c_waits)
    place_corners()
    for step in range(DEGREE):
        fine_step(step, False)
    cur = xa if DEGREE % 2 == 0 else xb
    own = (0, NY)
    wait_for(ab_waits)
    place_coarse(0, cab.at[0], False)
    place_coarse(1, cab.at[1], True)
    for p in (*range(-CX, 0), *range(CX, 2 * CX)):
        cab[1, CX + p] = cab[1, CX + p] * in_planes(p)
    coarse_setup(True)
    for q in range(CX):
        a = diag[2 * q] * residual(cur, 2 * q, own)
        b = diag[2 * q + 1] * residual(cur, 2 * q + 1, own)
        cg[CX + q, 0:CY] = 0.125 * restrict_pair(a, b) / cdiag[q]

    pack_coarse(2, lambda q: cg[CX + q, 0:CY])
    g_waits = exchange_coarse(
        2, cg.at[slots[1], pl.ds(0, CY)], [cg.at[slot, pl.ds(0, CY)] for slot in slots], sg_sem, rg_sem
    )
    coarse_setup(False)
    wait_for(g_waits)
    place_coarse(2, cg, True)

    for p, at_p, span in coarse_blocks(4):
        here = pl.ds(0, span[1])
        g = masked(cg[at_p, here, :], in_planes(p))
        if in_planes(p) is not None:
            cg[at_p, here, :] = g
        update = g * (1.0 / THETA)
        cxs[0, at_p, here, :] = update
        cds[at_p, here, :] = update

    def coarse_residual(now, at_p, span):
        here = pl.ds(0, span[1])
        x = cxs[now, at_p, here, :]
        return (
            cg[at_p, here, :]
            - x
            + spread(
                x, lambda step, part: cxs[now, at_p + step, part[0] : part[1], :], span, CY,
                lambda e: cw[e, at_p, here, :],
            )
        )

    now = 0
    for step, (first, second) in enumerate(terms):
        for p, at_p, span in coarse_blocks(3 - step):
            here = pl.ds(0, span[1])
            update = first * cds[at_p, here, :] + second * coarse_residual(now, at_p, span)
            cds[at_p, here, :] = update
            cxs[1 - now, at_p, here, :] = cxs[now, at_p, here, :] + update
        now = 1 - now

    quarter = []
    for q in range(CX):
        quarter.append(cdiag[q] * coarse_residual(now, CX + q, (0, CY)))
    for h in range(CX // 2):
        both = quarter[2 * h] + quarter[2 * h + 1]
        for t in range(2):
            pair[t, 0:CY, :] = both[:, t * 128 : (t + 1) * 128]
        summed = jnp.concatenate(
            [pair[t, pl.ds(0, CY // 2, 2), :] + pair[t, pl.ds(1, CY // 2, 2), :] for t in range(2)], axis=1
        )
        coarsest[0, h] = 0.125 * halve_z(summed)
    l_waits = [
        send(coarsest.at[0], coarsest.at[dx], sl_sem.at[dx], rl_sem.at[dx], dx, 0) for dx in range(1, 8)
    ]

    for q in range(CX):
        fine = double_z(cxs[now, CX + q, 0:CY])
        for t in range(4):
            part = fine[:, t * 128 : (t + 1) * 128]
            wide[t, pl.ds(0, CY, 2), :] = part
            wide[t, pl.ds(1, CY, 2), :] = part
        full = jnp.concatenate([wide[t] for t in range(4)], axis=1)
        for p in (2 * q, 2 * q + 1):
            out_ref[p] = cur[PX + p, own_y, :] + full

    wait_for(l_waits)
    for dx in range(8):
        owner = lax.rem(gx + ngx - dx, ngx)
        last_ref[pl.ds(2 * owner, 2)] = coarsest[dx]
    for copy, dy in sent:
        when(beside[dy], copy.wait_send)
    for copy, gone in corners_sent:
        pl.when(gone)(copy.wait_send)


def on_device(guess, rhs, alpha, beta):
    vmem = pltpu.VMEM
    dma = pltpu.SemaphoreType.DMA
    fine = (NX, NY, NZ)
    wide = (EX, EY, NZ)
    coarse = (EXC, EYC, CZ)
    scratch = [
        vmem(wide, F32), vmem(wide, F32), vmem(wide, F32), vmem(wide, F32), vmem(wide, F32), vmem(wide, F32),
        vmem(wide, F32), vmem(fine, F32), vmem((6, *wide), F32),
        vmem((2, 18, 8, NZ), F32), vmem((2, 18, 8, NZ), F32), vmem((2, 2, 7, 8, NZ), F32),
        vmem((4, NY, 128), F32), vmem((4, NY, 128), F32),
        vmem((2, *coarse), F32), vmem(coarse, F32), vmem((3, 2, CX // 2, 8, CZ), F32),
        vmem((3, 3, 2, CX // 2, 8, CZ), F32), vmem((6, *coarse), F32),
        vmem((2, *coarse), F32), vmem(coarse, F32), vmem((CX, CY, CZ), F32),
        vmem((8, 2, CY // 2, CZ // 2), F32),
        dma((4,)), dma((4, 2)), dma((4, 2)), dma((2,)), dma((2,)), dma((2, 2)), dma((2, 2)),
        dma((8,)), dma((8,)), dma((8,)), dma((8,)), dma((8,)), dma((8,)),
    ]
    placed = [pltpu.with_memory_space_constraint(x, pltpu.HBM) for x in (guess, rhs, alpha, beta)]
    return pl.pallas_call(
        kernel,
        out_shape=(
            jax.ShapeDtypeStruct(fine, F32),
            jax.ShapeDtypeStruct((16, CY // 2, CZ // 2), F32),
        ),
        in_specs=[pl.BlockSpec(memory_space=pltpu.HBM)] * 4,
        out_specs=(pl.BlockSpec(memory_space=vmem), pl.BlockSpec(memory_space=vmem)),
        scratch_shapes=scratch,
        compiler_params=pltpu.CompilerParams(
            collective_id=0, has_side_effects=True, vmem_limit_bytes=40 << 20
        ),
        name="vcycle",
    )(*placed)


def solution(mesh):
    placed = (P("gx", "yz", None),) * 4
    return jax.shard_map(
        on_device,
        mesh=mesh,
        in_specs=placed,
        out_specs=(P("gx", "yz", None), P(None, "yz", None)),
        check_vma=False,
    )
```

```python
import functools

import jax
import jax.numpy as jnp
from jax import lax
from jax.experimental import pallas as pl
from jax.experimental.pallas import tpu as pltpu
from jax.sharding import PartitionSpec as P

DEGREE = 4
THETA = 1.125
DELTA = 0.875
MESH = pl.DeviceIdType.MESH
F32 = jnp.float32

NX, NY, NZ = 8, 16, 512
CX, CY, CZ = 4, 8, 256
DEPTH = DEGREE + 1
PX = DEPTH
EX, EY = NX + 2 * DEPTH, NY + 8
EXC, EYC = CX + 2 * DEGREE, CY + 8


def cheb_terms():
    sigma = THETA / DELTA
    rho_prev = 1.0 / sigma
    terms = []
    for _ in range(DEGREE - 1):
        rho_next = 1.0 / (2.0 * sigma - rho_prev)
        terms.append((rho_next * rho_prev, 2.0 * rho_next / DELTA))
        rho_prev = rho_next
    return terms


def lanes(shape):
    return lax.broadcasted_iota(jnp.int32, shape, 1)


def rows(shape):
    return lax.broadcasted_iota(jnp.int32, shape, 0)


def halve_z(field):
    count, width = field.shape
    lane = lanes((count, 128))
    even = jnp.where(lane < 64, 2 * lane, 2 * lane - 128)
    low = lane < 64
    tiles = []
    for t in range(width // 256):
        halves = []
        for h in range(2):
            part = field[:, (2 * t + h) * 128 : (2 * t + h + 1) * 128]
            part = part + pltpu.roll(part, 127, 1)
            halves.append(jnp.take_along_axis(part, even, axis=1))
        tiles.append(jnp.where(low, halves[0], halves[1]))
    return tiles[0] if len(tiles) == 1 else jnp.concatenate(tiles, axis=1)


def double_z(field):
    count, width = field.shape
    half = lanes((count, 128)) // 2
    tiles = []
    for t in range(width // 128):
        part = field[:, t * 128 : (t + 1) * 128]
        tiles.append(jnp.take_along_axis(part, half, axis=1))
        tiles.append(jnp.take_along_axis(part, half + 64, axis=1))
    return jnp.concatenate(tiles, axis=1)


def z_beside(field):
    width = field.shape[1]
    return pltpu.roll(field, width - 1, 1), pltpu.roll(field, 1, 1)


def y_beside(field, below, above):
    count = field.shape[0]
    row = rows(field.shape)
    up = jnp.where(row == count - 1, jnp.broadcast_to(above, field.shape), pltpu.roll(field, count - 1, 0))
    down = jnp.where(row == 0, jnp.broadcast_to(below, field.shape), pltpu.roll(field, 1, 0))
    return up, down


def tile_a(p):
    return 2 * p + (1 if p >= 4 else 0)


def tile_b(p):
    return 2 * p + (0 if p >= 4 else 1)


def kernel(
    guess_h, rhs_h, alpha_h, beta_h, out_ref, last_ref,
    xa, xb, be, al, rh, ds, gs, diag, ws, pk, rk, qk, rc,
    pair, wide, cab, cg, pkc, rkc, cw, cxs, cds, cdiag, coarsest,
    load_sem, sx_sem, rx_sem, sy_sem, ry_sem, sc_sem, rc_sem, sab_sem, rab_sem, sg_sem, rg_sem, sl_sem, rl_sem,
):
    gx = lax.axis_index("gx")
    yz = lax.axis_index("yz")
    ngx = lax.axis_size("gx")
    nyz = lax.axis_size("yz")

    def at(dx, dy):
        return (lax.rem(gx + ngx + dx, ngx), lax.rem(yz + nyz + dy, nyz))

    beside = {-1: yz > 0, 0: None, 1: yz < nyz - 1}

    def when(condition, act):
        if condition is None:
            act()
        else:
            pl.when(condition)(act)

    def greet(dx, dy):
        pl.semaphore_signal(barrier, inc=1, device_id=at(dx, dy), device_id_type=MESH)

    own_x, own_y, edge_y = pl.ds(PX, NX), pl.ds(0, NY), pl.ds(NY, 8)
    around = [(dx, dy) for dx in (-1, 0, 1) for dy in (-1, 0, 1) if (dx, dy) != (0, 0)]
    barrier = pltpu.get_barrier_semaphore()
    for dx, dy in around:
        if dy != 0:
            when(beside[dy], functools.partial(greet, dx, dy))
    loads = []
    for k, (src, dst) in enumerate(((guess_h, xa), (beta_h, be), (alpha_h, al), (rhs_h, rh))):
        copy = pltpu.make_async_copy(src, dst.at[own_x, own_y], load_sem.at[k])
        copy.start()
        loads.append(copy)
    for dx in range(1, 8):
        greet(dx, 0)
    greeted = 7 + 3 * (yz > 0).astype(jnp.int32) + 3 * (yz < nyz - 1).astype(jnp.int32)

    half = rows((8, NZ)) < 4

    def packed(first, second, side):
        moved = pltpu.roll(second, 4, 0)
        return jnp.where(half, moved, first) if side == 0 else jnp.where(half, first, moved)

    odd = lax.rem(gx, 2)

    def pack_rows(half_at):
        for side, start in ((0, 8), (1, 0)):
            tile = pl.ds(start, 8)
            for k in range(4):
                p = 4 * half_at + k
                one = PX + p
                pk[side, 2 * p + half_at] = packed(xa[one, tile, :], be[one, tile, :], side)
                pk[side, 2 * p + 1 - half_at] = packed(al[one, tile, :], rh[one, tile, :], side)

    for copy in loads:
        copy.wait()
    pack_rows(odd)
    for side, missing in ((0, yz == 0), (1, yz == nyz - 1)):

        @pl.when(missing)
        def _(side=side):
            rk[side] = jnp.ones(rk.shape[1:], F32)
            for k in range(3):
                if k < 2:
                    rc[k, side] = jnp.ones(rc.shape[2:], F32)
                for f in range(3):
                    rkc[f, k, side] = jnp.ones(rkc.shape[3:], F32)

    pl.semaphore_wait(barrier, greeted)

    sent = []

    def copy_of(src, dst, s_sem, r_sem, device):
        return pltpu.make_async_remote_copy(
            src_ref=src, dst_ref=dst, send_sem=s_sem, recv_sem=r_sem, device_id=device, device_id_type=MESH
        )

    def send(src, dst, s_sem, r_sem, dx, dy):
        copy = copy_of(src, dst, s_sem, r_sem, at(dx, dy))
        when(beside[dy], copy.start)
        sent.append((copy, dy))
        return copy, dy

    def wait_for(copies):
        for copy, dy in copies:
            when(beside[-dy], copy.wait_recv)

    first_core = lax.rem(gx, 2) == 0
    ahead = 8 * odd
    parts = (pl.ds(ahead, 8), pl.ds(8 - ahead, 8), pl.ds(16, 2))

    def send_rows(k):
        part = parts[k]
        return [
            send(pk.at[side, part], rk.at[side, part], sy_sem.at[side, k], ry_sem.at[side, k], 0, 1 - 2 * side)
            for side in (0, 1)
        ]

    y_waits = [send_rows(0)]
    x_waits = []
    for k, (src, dst, deep) in enumerate(
        ((guess_h, xa, DEPTH), (beta_h, be, DEPTH), (alpha_h, al, DEPTH - 1), (rhs_h, rh, DEPTH - 1))
    ):
        x_waits.append(
            send(
                src.at[pl.ds(NX - deep, deep)], dst.at[pl.ds(PX - deep, deep), own_y],
                sx_sem.at[k, 0], rx_sem.at[k, 0], 1, 0,
            )
        )
        x_waits.append(
            send(
                src.at[pl.ds(0, deep)], dst.at[pl.ds(PX + NX, deep), own_y],
                sx_sem.at[k, 1], rx_sem.at[k, 1], -1, 0,
            )
        )

    pack_rows(1 - odd)
    y_waits.append(send_rows(1))
    for side, fifth in ((0, 11), (1, 4)):
        for p in range(NX):
            pk[side, 16, p : p + 1, :] = xa[PX + p, fifth : fifth + 1, :]
            pk[side, 17, p : p + 1, :] = be[PX + p, fifth : fifth + 1, :]
    y_waits.append(send_rows(2))
    sub = rows((8, NZ))
    nearest = [(sub % 4) == 0, (sub % 4) == 3]
    near_two = [(sub % 4) < 2, (sub % 4) >= 2]

    def pack_corner(sx, sy):
        planes = range(7, 3, -1) if sx == 0 else range(4)
        a = [rk[sy, tile_a(p)] for p in planes]
        b = [rk[sy, tile_b(p)] for p in planes]
        one = 1 if sy == 0 else 7
        qk[sx, sy, 0] = a[0]
        qk[sx, sy, 1] = jnp.where(nearest[sy], pltpu.roll(a[3], one, 0), b[0])
        qk[sx, sy, 2] = jnp.where(nearest[sy], pltpu.roll(b[2], one, 0), a[1])
        qk[sx, sy, 3] = jnp.where(near_two[sy], pltpu.roll(a[2], 2, 0), b[1])

    corners = []
    for sx in (0, 1):
        same_chip = first_core if sx == 0 else jnp.logical_not(first_core)
        for sy in (0, 1):
            relay = copy_of(qk.at[sx, sy], rc.at[sx, sy], sc_sem.at[sx, sy], rc_sem.at[sx, sy], at(1 - 2 * sx, 0))
            corners.append((relay, beside[2 * sy - 1], sx, sy, same_chip))

    def pass_on(side, on_chip):
        for relay, arrives, sx, sy, same_chip in corners:
            if sy == side:
                chosen = same_chip if on_chip else jnp.logical_not(same_chip)

                @pl.when(jnp.logical_and(arrives, chosen))
                def _(relay=relay, sx=sx, sy=sy):
                    pack_corner(sx, sy)
                    relay.start()

    def restrict_pair(first, second):
        both = first + second
        for t in range(4):
            pair[t] = both[:, t * 128 : (t + 1) * 128]
        summed = jnp.concatenate(
            [pair[t, pl.ds(0, CY, 2), :] + pair[t, pl.ds(1, CY, 2), :] for t in range(4)], axis=1
        )
        return halve_z(summed)

    chalf = rows((8, CZ)) < 4

    def pack_coarse(f, get):
        for q in range(0, CX, 2):
            this, then = get(q), pltpu.roll(get(q + 1), 4, 0)
            pkc[f, 0, q // 2] = jnp.where(chalf, then, this)
            pkc[f, 1, q // 2] = jnp.where(chalf, this, then)

    def exchange_coarse(fields, own, others, s_sem, r_sem):
        copies = []
        for k, (dx, dy) in enumerate(around):
            if dy == 0:
                src, dst = own, others[1 - dx]
            else:
                side = (1 - dy) // 2
                src, dst = pkc.at[fields, side], rkc.at[fields, 1 - dx, side]
            copies.append(send(src, dst, s_sem.at[k], r_sem.at[k], dx, dy))
        return copies

    for q in range(CX):
        one, two = PX + 2 * q, PX + 2 * q + 1
        cab[0, CX + q, 0:CY] = 0.125 * restrict_pair(al[one, own_y, :], al[two, own_y, :])
        cab[1, CX + q, 0:CY] = 0.125 * restrict_pair(be[one, own_y, :], be[two, own_y, :])
    for f in range(2):
        pack_coarse(f, lambda q, f=f: cab[f, CX + q, 0:CY])
    in_lo_x = (gx > 0).astype(F32)
    in_hi_x = (gx < ngx - 1).astype(F32)
    in_lo_y = (yz > 0).astype(F32)
    in_hi_y = (yz < nyz - 1).astype(F32)
    terms = cheb_terms()

    def join(below, above):
        return jnp.where(half, above, below)

    def place(plane, a_below, a_above, b_below=None, b_above=None):
        a_below, a_above = a_below * in_lo_y, a_above * in_hi_y
        xa[plane, edge_y, :] = join(a_below, a_above)
        be[plane, edge_y, :] = pltpu.roll(join(a_above, a_below), 4, 0)
        if b_below is not None:
            al[plane, edge_y, :] = join(b_below, b_above)
            rh[plane, edge_y, :] = pltpu.roll(join(b_above, b_below), 4, 0)

    def place_rows():
        for p in range(NX):
            place(PX + p, rk[0, tile_a(p)], rk[1, tile_a(p)], rk[0, tile_b(p)], rk[1, tile_b(p)])

    def place_corners():
        for sx in (0, 1):
            tiles = [[rc[sx, sy, k] for sy in (0, 1)] for k in range(4)]

            def back(k):
                return [pltpu.roll(tiles[k][0], 7, 0), pltpu.roll(tiles[k][1], 1, 0)]

            blocks = (
                [*tiles[0], *tiles[1]],
                [*tiles[2], *tiles[3]],
                [*(pltpu.roll(tile, 6, 0) for tile in tiles[3]), *back(2)],
                back(1),
            )
            for k, block in enumerate(blocks):
                place(PX - 1 - k if sx == 0 else PX + NX + k, *block)
        for edge, start in ((gx == 0, 0), (gx == ngx - 1, PX + NX)):

            @pl.when(edge)
            def _(start=start):
                for plane in range(start, start + DEPTH):
                    xa[plane] = jnp.zeros((EY, NZ), F32)
                    be[plane] = jnp.zeros((EY, NZ), F32)

    def fine_blocks(deep):
        found = []
        for p in range(-deep, NX + deep):
            beyond = max(-p, p - NX + 1, 0)
            found.append((p, (0, EY) if beyond < deep else (0, NY)))
        return found

    def along_y(x, at_row, span, own, fifth=None):
        count = own + 8
        if span == (0, own):
            return y_beside(x, at_row(count - 1), at_row(own))
        up, down = pltpu.roll(x, count - 1, 0), pltpu.roll(x, 1, 0)
        if fifth is not None:
            row = rows(x.shape)
            up = jnp.where(row == own + 3, jnp.broadcast_to(fifth[1], x.shape), up)
            down = jnp.where(row == own + 4, jnp.broadcast_to(fifth[0], x.shape), down)
        return up, down

    def spread(x, x_at, span, own, w, fifth=None):
        up, down = along_y(x, lambda row: x_at(0, (row, row + 1)), span, own, fifth)
        right, left = z_beside(x)
        return (
            w(0) * x_at(1, span) + w(1) * x_at(-1, span) + w(2) * up + w(3) * down + w(4) * right + w(5) * left
        )

    def in_rows(shape, own):
        row = rows(shape)
        return jnp.where(row < own, 1.0, jnp.where(row < own + 4, in_hi_y, in_lo_y))

    def first_step(p, span):
        lo, hi = span
        here = pl.ds(lo, hi - lo)
        shape = (hi - lo, NZ)
        lane = lanes(shape)
        b = be[PX + p, here, :]
        fifth = fifth_b = None
        if 0 <= p < NX:
            part = slice(p, p + 1)
            fifth = (rk[0, 16, part, :] * in_lo_y, rk[1, 16, part, :] * in_hi_y)
            fifth_b = (rk[0, 17, part, :] * in_lo_y, rk[1, 17, part, :] * in_hi_y)
        b_up, b_down = along_y(b, lambda row: be[PX + p, row : row + 1, :], span, NY, fifth_b)
        b_right, b_left = z_beside(b)
        b_right = jnp.where(lane == NZ - 1, 0.0, b_right)
        b_left = jnp.where(lane == 0, 0.0, b_left)
        faces = [
            0.5 * (b + other)
            for other in (be[PX + p + 1, here, :], be[PX + p - 1, here, :], b_up, b_down, b_right, b_left)
        ]
        total = faces[0] + faces[1] + faces[2] + faces[3] + faces[4] + faces[5]
        whole = al[PX + p, here, :] + total
        if 0 <= p < NX:
            diag[p] = whole[0:NY]
        inverse = 1.0 / whole
        if p < 0:
            inverse = inverse * in_lo_x
        if p >= NX:
            inverse = inverse * in_hi_x
        if span == (0, EY):
            inverse = inverse * in_rows(shape, NY)
        w = [inverse * face for face in faces]
        w[4] = jnp.where(lane == NZ - 1, 0.0, w[4])
        w[5] = jnp.where(lane == 0, 0.0, w[5])
        for e in range(6):
            ws[e, PX + p, here, :] = w[e]
        g = inverse * rh[PX + p, here, :]
        gs[PX + p, here, :] = g
        x = xa[PX + p, here, :]
        resid = g - x + spread(x, lambda step, part: xa[PX + p + step, part[0] : part[1], :], span, NY, lambda e: w[e], fifth)
        update = resid * (1.0 / THETA)
        ds[PX + p, here, :] = update
        xb[PX + p, here, :] = x + update

    def residual(cur, p, span):
        here = pl.ds(span[0], span[1] - span[0])
        x = cur[PX + p, here, :]
        return (
            gs[PX + p, here, :]
            - x
            + spread(
                x, lambda step, part: cur[PX + p + step, part[0] : part[1], :], span, NY,
                lambda e: ws[e, PX + p, here, :],
            )
        )

    def coarse_blocks(deep):
        found = []
        for p in range(-deep, CX + deep):
            beyond = max(-p, p - CX + 1, 0)
            found.append((p, CX + p, (0, EYC) if beyond < deep else (0, CY)))
        return found

    def in_planes(p):
        return in_lo_x if p < 0 else in_hi_x if p >= CX else None

    def masked(value, mask):
        return value if mask is None else value * mask

    def place_coarse(f, field, inside):
        for k in range(3):
            for q in range(0, CX, 2):
                below, above = rkc[f, k, 0, q // 2], rkc[f, k, 1, q // 2]
                if inside:
                    below, above = below * in_lo_y, above * in_hi_y
                field[k * CX + q, pl.ds(CY, 8), :] = jnp.where(chalf, above, below)
                field[k * CX + q + 1, pl.ds(CY, 8), :] = pltpu.roll(jnp.where(chalf, below, above), 4, 0)

    def coarse_setup(own_only):
        for p, at_p, span in coarse_blocks(0 if own_only else 3):
            here = pl.ds(0, span[1])
            shape = (span[1], CZ)
            clane = lanes(shape)
            b = cab[1, at_p, here, :]
            b_up, b_down = along_y(b, lambda row: cab[1, at_p, row : row + 1, :], span, CY)
            b_right, b_left = z_beside(b)
            b_right = jnp.where(clane == CZ - 1, 0.0, b_right)
            b_left = jnp.where(clane == 0, 0.0, b_left)
            faces = [
                0.5 * (b + other)
                for other in (cab[1, at_p + 1, here, :], cab[1, at_p - 1, here, :], b_up, b_down, b_right, b_left)
            ]
            total = faces[0] + faces[1] + faces[2] + faces[3] + faces[4] + faces[5]
            whole = cab[0, at_p, here, :] + 0.25 * total
            if own_only:
                cdiag[p] = whole
                continue
            scale = masked(0.25 / whole, in_planes(p))
            if span == (0, EYC):
                scale = scale * in_rows(shape, CY)
            w = [scale * face for face in faces]
            w[4] = jnp.where(clane == CZ - 1, 0.0, w[4])
            w[5] = jnp.where(clane == 0, 0.0, w[5])
            for e in range(6):
                cw[e, at_p, here, :] = w[e]

    def later_step(step, p, span):
        cur, other = (xb, xa) if step % 2 == 1 else (xa, xb)
        first, second = terms[step - 1]
        here = pl.ds(span[0], span[1] - span[0])
        update = first * ds[PX + p, here, :] + second * residual(cur, p, span)
        ds[PX + p, here, :] = update
        other[PX + p, here, :] = cur[PX + p, here, :] + update

    def fine_step(step, chosen):
        for p, span in fine_blocks(DEPTH - 1 - step):
            if (1 + step <= p < NX - 1 - step) == chosen:
                if step == 0:
                    first_step(p, span)
                else:
                    later_step(step, p, span)

    for side in (0, 1):
        wait_for(y_waits[0][side : side + 1])
        pass_on(side, False)
    slots = [pl.ds(k * CX, CX) for k in range(3)]
    ab_waits = exchange_coarse(
        pl.ds(0, 2), cab.at[:, slots[1], pl.ds(0, CY)],
        [cab.at[:, slot, pl.ds(0, CY)] for slot in slots], sab_sem, rab_sem,
    )
    for side in (0, 1):
        wait_for(y_waits[1][side : side + 1])
        pass_on(side, True)
    wait_for(y_waits[2])
    place_rows()
    for step in range(DEGREE):
        fine_step(step, True)
    wait_for(x_waits)
    for relay, arrives, *_ in corners:
        pl.when(arrives)(relay.wait_recv)
    place_corners()
    for step in range(DEGREE):
        fine_step(step, False)
    cur = xa if DEGREE % 2 == 0 else xb
    own = (0, NY)
    wait_for(ab_waits)
    place_coarse(0, cab.at[0], False)
    place_coarse(1, cab.at[1], True)
    for p in (*range(-CX, 0), *range(CX, 2 * CX)):
        cab[1, CX + p] = cab[1, CX + p] * in_planes(p)
    coarse_setup(True)
    for q in range(CX):
        a = diag[2 * q] * residual(cur, 2 * q, own)
        b = diag[2 * q + 1] * residual(cur, 2 * q + 1, own)
        cg[CX + q, 0:CY] = 0.125 * restrict_pair(a, b) / cdiag[q]

    pack_coarse(2, lambda q: cg[CX + q, 0:CY])
    g_waits = exchange_coarse(
        2, cg.at[slots[1], pl.ds(0, CY)], [cg.at[slot, pl.ds(0, CY)] for slot in slots], sg_sem, rg_sem
    )
    coarse_setup(False)
    wait_for(g_waits)
    place_coarse(2, cg, True)

    for p, at_p, span in coarse_blocks(4):
        here = pl.ds(0, span[1])
        g = masked(cg[at_p, here, :], in_planes(p))
        if in_planes(p) is not None:
            cg[at_p, here, :] = g
        update = g * (1.0 / THETA)
        cxs[0, at_p, here, :] = update
        cds[at_p, here, :] = update

    def coarse_residual(now, at_p, span):
        here = pl.ds(0, span[1])
        x = cxs[now, at_p, here, :]
        return (
            cg[at_p, here, :]
            - x
            + spread(
                x, lambda step, part: cxs[now, at_p + step, part[0] : part[1], :], span, CY,
                lambda e: cw[e, at_p, here, :],
            )
        )

    now = 0
    for step, (first, second) in enumerate(terms):
        for p, at_p, span in coarse_blocks(3 - step):
            here = pl.ds(0, span[1])
            update = first * cds[at_p, here, :] + second * coarse_residual(now, at_p, span)
            cds[at_p, here, :] = update
            cxs[1 - now, at_p, here, :] = cxs[now, at_p, here, :] + update
        now = 1 - now

    quarter = []
    for q in range(CX):
        quarter.append(cdiag[q] * coarse_residual(now, CX + q, (0, CY)))
    for h in range(CX // 2):
        both = quarter[2 * h] + quarter[2 * h + 1]
        for t in range(2):
            pair[t, 0:CY, :] = both[:, t * 128 : (t + 1) * 128]
        summed = jnp.concatenate(
            [pair[t, pl.ds(0, CY // 2, 2), :] + pair[t, pl.ds(1, CY // 2, 2), :] for t in range(2)], axis=1
        )
        coarsest[0, h] = 0.125 * halve_z(summed)
    l_waits = [
        send(coarsest.at[0], coarsest.at[dx], sl_sem.at[dx], rl_sem.at[dx], dx, 0) for dx in range(1, 8)
    ]

    for q in range(CX):
        fine = double_z(cxs[now, CX + q, 0:CY])
        for t in range(4):
            part = fine[:, t * 128 : (t + 1) * 128]
            wide[t, pl.ds(0, CY, 2), :] = part
            wide[t, pl.ds(1, CY, 2), :] = part
        full = jnp.concatenate([wide[t] for t in range(4)], axis=1)
        for p in (2 * q, 2 * q + 1):
            out_ref[p] = cur[PX + p, own_y, :] + full

    wait_for(l_waits)
    for dx in range(8):
        owner = lax.rem(gx + ngx - dx, ngx)
        last_ref[pl.ds(2 * owner, 2)] = coarsest[dx]
    for copy, dy in sent:
        when(beside[dy], copy.wait_send)
    for relay, arrives, *_ in corners:
        pl.when(arrives)(relay.wait_send)


def on_device(guess, rhs, alpha, beta):
    vmem = pltpu.VMEM
    dma = pltpu.SemaphoreType.DMA
    fine = (NX, NY, NZ)
    wide = (EX, EY, NZ)
    coarse = (EXC, EYC, CZ)
    scratch = [
        vmem(wide, F32), vmem(wide, F32), vmem(wide, F32), vmem(wide, F32), vmem(wide, F32), vmem(wide, F32),
        vmem(wide, F32), vmem(fine, F32), vmem((6, *wide), F32),
        vmem((2, 18, 8, NZ), F32), vmem((2, 18, 8, NZ), F32), vmem((2, 2, 4, 8, NZ), F32), vmem((2, 2, 4, 8, NZ), F32),
        vmem((4, NY, 128), F32), vmem((4, NY, 128), F32),
        vmem((2, *coarse), F32), vmem(coarse, F32), vmem((3, 2, CX // 2, 8, CZ), F32),
        vmem((3, 3, 2, CX // 2, 8, CZ), F32), vmem((6, *coarse), F32),
        vmem((2, *coarse), F32), vmem(coarse, F32), vmem((CX, CY, CZ), F32),
        vmem((8, 2, CY // 2, CZ // 2), F32),
        dma((4,)), dma((4, 2)), dma((4, 2)), dma((2, 3)), dma((2, 3)), dma((2, 2)), dma((2, 2)),
        dma((8,)), dma((8,)), dma((8,)), dma((8,)), dma((8,)), dma((8,)),
    ]
    placed = [pltpu.with_memory_space_constraint(x, pltpu.HBM) for x in (guess, rhs, alpha, beta)]
    return pl.pallas_call(
        kernel,
        out_shape=(
            jax.ShapeDtypeStruct(fine, F32),
            jax.ShapeDtypeStruct((16, CY // 2, CZ // 2), F32),
        ),
        in_specs=[pl.BlockSpec(memory_space=pltpu.HBM)] * 4,
        out_specs=(pl.BlockSpec(memory_space=vmem), pl.BlockSpec(memory_space=vmem)),
        scratch_shapes=scratch,
        compiler_params=pltpu.CompilerParams(
            collective_id=0, has_side_effects=True, vmem_limit_bytes=40 << 20
        ),
        name="vcycle",
    )(*placed)


def solution(mesh):
    placed = (P("gx", "yz", None),) * 4
    return jax.shard_map(
        on_device,
        mesh=mesh,
        in_specs=placed,
        out_specs=(P("gx", "yz", None), P(None, "yz", None)),
        check_vma=False,
    )
```

```python
import functools

import jax
import jax.numpy as jnp
from jax import lax
from jax.experimental import pallas as pl
from jax.experimental.pallas import tpu as pltpu
from jax.sharding import PartitionSpec as P

DEGREE = 4
THETA = 1.125
DELTA = 0.875
MESH = pl.DeviceIdType.MESH
F32 = jnp.float32

NX, NY, NZ = 8, 16, 512
CX, CY, CZ = 4, 8, 256
DEPTH = DEGREE + 1
PX = DEPTH
EX, EY = NX + 2 * DEPTH, NY + 8
EXC, EYC = CX + 2 * DEGREE, CY + 8


def cheb_terms():
    sigma = THETA / DELTA
    rho_prev = 1.0 / sigma
    terms = []
    for _ in range(DEGREE - 1):
        rho_next = 1.0 / (2.0 * sigma - rho_prev)
        terms.append((rho_next * rho_prev, 2.0 * rho_next / DELTA))
        rho_prev = rho_next
    return terms


def lanes(shape):
    return lax.broadcasted_iota(jnp.int32, shape, 1)


def rows(shape):
    return lax.broadcasted_iota(jnp.int32, shape, 0)


def halve_z(field):
    count, width = field.shape
    lane = lanes((count, 128))
    even = jnp.where(lane < 64, 2 * lane, 2 * lane - 128)
    low = lane < 64
    tiles = []
    for t in range(width // 256):
        halves = []
        for h in range(2):
            part = field[:, (2 * t + h) * 128 : (2 * t + h + 1) * 128]
            part = part + pltpu.roll(part, 127, 1)
            halves.append(jnp.take_along_axis(part, even, axis=1))
        tiles.append(jnp.where(low, halves[0], halves[1]))
    return tiles[0] if len(tiles) == 1 else jnp.concatenate(tiles, axis=1)


def double_z(field):
    count, width = field.shape
    half = lanes((count, 128)) // 2
    tiles = []
    for t in range(width // 128):
        part = field[:, t * 128 : (t + 1) * 128]
        tiles.append(jnp.take_along_axis(part, half, axis=1))
        tiles.append(jnp.take_along_axis(part, half + 64, axis=1))
    return jnp.concatenate(tiles, axis=1)


def without_last(field):
    width = field.shape[1]
    tail = field[:, width - 128 :]
    return jnp.concatenate([field[:, : width - 128], jnp.where(lanes(tail.shape) == 127, 0.0, tail)], axis=1)


def without_first(field):
    head = field[:, :128]
    return jnp.concatenate([jnp.where(lanes(head.shape) == 0, 0.0, head), field[:, 128:]], axis=1)


def z_beside(field):
    width = field.shape[1]
    return pltpu.roll(field, width - 1, 1), pltpu.roll(field, 1, 1)


def y_beside(field, below, above):
    count = field.shape[0]
    row = rows(field.shape)
    up = jnp.where(row == count - 1, jnp.broadcast_to(above, field.shape), pltpu.roll(field, count - 1, 0))
    down = jnp.where(row == 0, jnp.broadcast_to(below, field.shape), pltpu.roll(field, 1, 0))
    return up, down


def tile_a(p):
    return 2 * p + (1 if p >= 4 else 0)


def tile_b(p):
    return 2 * p + (0 if p >= 4 else 1)


def kernel(
    guess_h, rhs_h, alpha_h, beta_h, out_ref, last_ref,
    xa, xb, be, al, rh, ds, gs, diag, ws, pk, rk, qk, rc,
    pair, wide, cab, cg, pkc, rkc, cw, cxs, cds, cdiag, coarsest,
    load_sem, sx_sem, rx_sem, sy_sem, ry_sem, sc_sem, rc_sem, sab_sem, rab_sem, sg_sem, rg_sem, sl_sem, rl_sem,
):
    gx = lax.axis_index("gx")
    yz = lax.axis_index("yz")
    ngx = lax.axis_size("gx")
    nyz = lax.axis_size("yz")

    def at(dx, dy):
        return (lax.rem(gx + ngx + dx, ngx), lax.rem(yz + nyz + dy, nyz))

    beside = {-1: yz > 0, 0: None, 1: yz < nyz - 1}

    def when(condition, act):
        if condition is None:
            act()
        else:
            pl.when(condition)(act)

    def greet(dx, dy):
        pl.semaphore_signal(barrier, inc=1, device_id=at(dx, dy), device_id_type=MESH)

    own_x, own_y, edge_y = pl.ds(PX, NX), pl.ds(0, NY), pl.ds(NY, 8)
    around = [(-1, -1), (-1, 1), (1, -1), (1, 1), (0, -1), (0, 1), (-1, 0), (1, 0)]
    barrier = pltpu.get_barrier_semaphore()
    for dx, dy in around:
        if dy != 0:
            when(beside[dy], functools.partial(greet, dx, dy))
    loads = []
    for k, (src, dst) in enumerate(((guess_h, xa), (beta_h, be), (alpha_h, al), (rhs_h, rh))):
        copy = pltpu.make_async_copy(src, dst.at[own_x, own_y], load_sem.at[k])
        copy.start()
        loads.append(copy)
    for dx in range(1, 8):
        greet(dx, 0)
    greeted = 7 + 3 * (yz > 0).astype(jnp.int32) + 3 * (yz < nyz - 1).astype(jnp.int32)

    half = rows((8, NZ)) < 4

    def packed(first, second, side):
        moved = pltpu.roll(second, 4, 0)
        return jnp.where(half, moved, first) if side == 0 else jnp.where(half, first, moved)

    odd = lax.rem(gx, 2)

    def pack_rows(half_at):
        for side, start in ((0, 8), (1, 0)):
            tile = pl.ds(start, 8)
            for k in range(4):
                p = 4 * half_at + k
                one = PX + p
                pk[side, 2 * p + half_at] = packed(xa[one, tile, :], be[one, tile, :], side)
                pk[side, 2 * p + 1 - half_at] = packed(al[one, tile, :], rh[one, tile, :], side)

    for copy in loads:
        copy.wait()
    pack_rows(odd)
    for side, missing in ((0, yz == 0), (1, yz == nyz - 1)):

        @pl.when(missing)
        def _(side=side):
            rk[side] = jnp.ones(rk.shape[1:], F32)
            for k in range(3):
                if k < 2:
                    rc[k, side] = jnp.ones(rc.shape[2:], F32)
                for f in range(3):
                    rkc[f, k, side] = jnp.ones(rkc.shape[3:], F32)

    pl.semaphore_wait(barrier, greeted)

    sent = []

    def copy_of(src, dst, s_sem, r_sem, device):
        return pltpu.make_async_remote_copy(
            src_ref=src, dst_ref=dst, send_sem=s_sem, recv_sem=r_sem, device_id=device, device_id_type=MESH
        )

    def send(src, dst, s_sem, r_sem, dx, dy):
        copy = copy_of(src, dst, s_sem, r_sem, at(dx, dy))
        when(beside[dy], copy.start)
        sent.append((copy, dy))
        return copy, dy

    def wait_for(copies):
        for copy, dy in copies:
            when(beside[-dy], copy.wait_recv)

    first_core = lax.rem(gx, 2) == 0
    ahead = 8 * odd
    parts = (pl.ds(ahead, 8), pl.ds(8 - ahead, 8), pl.ds(16, 2))

    def send_rows(k):
        part = parts[k]
        return [
            send(pk.at[side, part], rk.at[side, part], sy_sem.at[side, k], ry_sem.at[side, k], 0, 1 - 2 * side)
            for side in (0, 1)
        ]

    y_waits = [send_rows(0)]
    x_waits = []
    for k, (src, dst, deep) in enumerate(
        ((guess_h, xa, DEPTH), (beta_h, be, DEPTH), (alpha_h, al, DEPTH - 1), (rhs_h, rh, DEPTH - 1))
    ):
        x_waits.append(
            send(
                src.at[pl.ds(NX - deep, deep)], dst.at[pl.ds(PX - deep, deep), own_y],
                sx_sem.at[k, 0], rx_sem.at[k, 0], 1, 0,
            )
        )
        x_waits.append(
            send(
                src.at[pl.ds(0, deep)], dst.at[pl.ds(PX + NX, deep), own_y],
                sx_sem.at[k, 1], rx_sem.at[k, 1], -1, 0,
            )
        )

    pack_rows(1 - odd)
    y_waits.append(send_rows(1))
    for side, fifth in ((0, 11), (1, 4)):
        for p in range(NX):
            pk[side, 16, p : p + 1, :] = xa[PX + p, fifth : fifth + 1, :]
            pk[side, 17, p : p + 1, :] = be[PX + p, fifth : fifth + 1, :]
    y_waits.append(send_rows(2))
    sub = rows((8, NZ))
    nearest = [(sub % 4) == 0, (sub % 4) == 3]
    near_two = [(sub % 4) < 2, (sub % 4) >= 2]

    def pack_corner(sx, sy):
        planes = range(7, 3, -1) if sx == 0 else range(4)
        a = [rk[sy, tile_a(p)] for p in planes]
        b = [rk[sy, tile_b(p)] for p in planes]
        one = 1 if sy == 0 else 7
        qk[sx, sy, 0] = a[0]
        qk[sx, sy, 1] = jnp.where(nearest[sy], pltpu.roll(a[3], one, 0), b[0])
        qk[sx, sy, 2] = jnp.where(nearest[sy], pltpu.roll(b[2], one, 0), a[1])
        qk[sx, sy, 3] = jnp.where(near_two[sy], pltpu.roll(a[2], 2, 0), b[1])

    corners = []
    for sx in (0, 1):
        same_chip = first_core if sx == 0 else jnp.logical_not(first_core)
        for sy in (0, 1):
            relay = copy_of(qk.at[sx, sy], rc.at[sx, sy], sc_sem.at[sx, sy], rc_sem.at[sx, sy], at(1 - 2 * sx, 0))
            corners.append((relay, beside[2 * sy - 1], sx, sy, same_chip))

    def pass_on(side, on_chip):
        for relay, arrives, sx, sy, same_chip in corners:
            if sy == side:
                chosen = same_chip if on_chip else jnp.logical_not(same_chip)

                @pl.when(jnp.logical_and(arrives, chosen))
                def _(relay=relay, sx=sx, sy=sy):
                    pack_corner(sx, sy)
                    relay.start()

    def restrict_pair(first, second):
        both = first + second
        for t in range(4):
            pair[t] = both[:, t * 128 : (t + 1) * 128]
        summed = jnp.concatenate(
            [pair[t, pl.ds(0, CY, 2), :] + pair[t, pl.ds(1, CY, 2), :] for t in range(4)], axis=1
        )
        return halve_z(summed)

    chalf = rows((8, CZ)) < 4

    def pack_coarse(f, get):
        for q in range(0, CX, 2):
            this, then = get(q), pltpu.roll(get(q + 1), 4, 0)
            pkc[f, 0, q // 2] = jnp.where(chalf, then, this)
            pkc[f, 1, q // 2] = jnp.where(chalf, this, then)

    def exchange_coarse(fields, own, others, s_sem, r_sem):
        copies = []
        for k, (dx, dy) in enumerate(around):
            if dy == 0:
                src, dst = own, others[1 - dx]
            else:
                side = (1 - dy) // 2
                src, dst = pkc.at[fields, side], rkc.at[fields, 1 - dx, side]
            copies.append(send(src, dst, s_sem.at[k], r_sem.at[k], dx, dy))
        return copies

    for q in range(CX):
        one, two = PX + 2 * q, PX + 2 * q + 1
        cab[0, CX + q, 0:CY] = 0.125 * restrict_pair(al[one, own_y, :], al[two, own_y, :])
        cab[1, CX + q, 0:CY] = 0.125 * restrict_pair(be[one, own_y, :], be[two, own_y, :])
    for f in range(2):
        pack_coarse(f, lambda q, f=f: cab[f, CX + q, 0:CY])
    in_lo_x = (gx > 0).astype(F32)
    in_hi_x = (gx < ngx - 1).astype(F32)
    in_lo_y = (yz > 0).astype(F32)
    in_hi_y = (yz < nyz - 1).astype(F32)
    terms = cheb_terms()

    def join(below, above):
        return jnp.where(half, above, below)

    def place(plane, a_below, a_above, b_below=None, b_above=None):
        a_below, a_above = a_below * in_lo_y, a_above * in_hi_y
        xa[plane, edge_y, :] = join(a_below, a_above)
        be[plane, edge_y, :] = pltpu.roll(join(a_above, a_below), 4, 0)
        if b_below is not None:
            al[plane, edge_y, :] = join(b_below, b_above)
            rh[plane, edge_y, :] = pltpu.roll(join(b_above, b_below), 4, 0)

    def place_rows():
        for p in range(NX):
            place(PX + p, rk[0, tile_a(p)], rk[1, tile_a(p)], rk[0, tile_b(p)], rk[1, tile_b(p)])

    def place_corners():
        for sx in (0, 1):
            tiles = [[rc[sx, sy, k] for sy in (0, 1)] for k in range(4)]

            def back(k):
                return [pltpu.roll(tiles[k][0], 7, 0), pltpu.roll(tiles[k][1], 1, 0)]

            blocks = (
                [*tiles[0], *tiles[1]],
                [*tiles[2], *tiles[3]],
                [*(pltpu.roll(tile, 6, 0) for tile in tiles[3]), *back(2)],
                back(1),
            )
            for k, block in enumerate(blocks):
                place(PX - 1 - k if sx == 0 else PX + NX + k, *block)
        for edge, start in ((gx == 0, 0), (gx == ngx - 1, PX + NX)):

            @pl.when(edge)
            def _(start=start):
                for plane in range(start, start + DEPTH):
                    xa[plane] = jnp.zeros((EY, NZ), F32)
                    be[plane] = jnp.zeros((EY, NZ), F32)

    def fine_blocks(deep):
        found = []
        for p in range(-deep, NX + deep):
            beyond = max(-p, p - NX + 1, 0)
            found.append((p, (0, EY) if beyond < deep else (0, NY)))
        return found

    def along_y(x, at_row, span, own, fifth=None):
        count = own + 8
        if span == (0, own):
            return y_beside(x, at_row(count - 1), at_row(own))
        up, down = pltpu.roll(x, count - 1, 0), pltpu.roll(x, 1, 0)
        if fifth is not None:
            row = rows(x.shape)
            up = jnp.where(row == own + 3, jnp.broadcast_to(fifth[1], x.shape), up)
            down = jnp.where(row == own + 4, jnp.broadcast_to(fifth[0], x.shape), down)
        return up, down

    def spread(x, x_at, span, own, w, fifth=None):
        up, down = along_y(x, lambda row: x_at(0, (row, row + 1)), span, own, fifth)
        right, left = z_beside(x)
        return (
            w(0) * x_at(1, span) + w(1) * x_at(-1, span) + w(2) * up + w(3) * down + w(4) * right + w(5) * left
        )

    def in_rows(value, own):
        tail = value[own:]
        inside = jnp.where(rows(tail.shape) < 4, in_hi_y, in_lo_y)
        return jnp.concatenate([value[:own], tail * inside], axis=0)

    def first_step(p, span):
        lo, hi = span
        here = pl.ds(lo, hi - lo)
        b = be[PX + p, here, :]
        fifth = fifth_b = None
        if 0 <= p < NX:
            part = slice(p, p + 1)
            fifth = (rk[0, 16, part, :] * in_lo_y, rk[1, 16, part, :] * in_hi_y)
            fifth_b = (rk[0, 17, part, :] * in_lo_y, rk[1, 17, part, :] * in_hi_y)
        b_up, b_down = along_y(b, lambda row: be[PX + p, row : row + 1, :], span, NY, fifth_b)
        b_right, b_left = z_beside(b)
        b_right = without_last(b_right)
        b_left = without_first(b_left)
        pairs = [
            b + other for other in (be[PX + p + 1, here, :], be[PX + p - 1, here, :], b_up, b_down, b_right, b_left)
        ]
        total = pairs[0] + pairs[1] + pairs[2] + pairs[3] + pairs[4] + pairs[5]
        whole = al[PX + p, here, :] + 0.5 * total
        if 0 <= p < NX:
            diag[p] = whole[0:NY]
        inverse = 1.0 / whole
        if p < 0:
            inverse = inverse * in_lo_x
        if p >= NX:
            inverse = inverse * in_hi_x
        if span == (0, EY):
            inverse = in_rows(inverse, NY)
        scale = 0.5 * inverse
        w = [scale * pair for pair in pairs]
        w[4] = without_last(w[4])
        w[5] = without_first(w[5])
        for e in range(6):
            ws[e, PX + p, here, :] = w[e]
        g = inverse * rh[PX + p, here, :]
        gs[PX + p, here, :] = g
        x = xa[PX + p, here, :]
        resid = g - x + spread(x, lambda step, part: xa[PX + p + step, part[0] : part[1], :], span, NY, lambda e: w[e], fifth)
        update = resid * (1.0 / THETA)
        ds[PX + p, here, :] = update
        xb[PX + p, here, :] = x + update

    def residual(cur, p, span):
        here = pl.ds(span[0], span[1] - span[0])
        x = cur[PX + p, here, :]
        return (
            gs[PX + p, here, :]
            - x
            + spread(
                x, lambda step, part: cur[PX + p + step, part[0] : part[1], :], span, NY,
                lambda e: ws[e, PX + p, here, :],
            )
        )

    def coarse_blocks(deep):
        found = []
        for p in range(-deep, CX + deep):
            beyond = max(-p, p - CX + 1, 0)
            found.append((p, CX + p, (0, EYC) if beyond < deep else (0, CY)))
        return found

    def in_planes(p):
        return in_lo_x if p < 0 else in_hi_x if p >= CX else None

    def masked(value, mask):
        return value if mask is None else value * mask

    def place_coarse(f, field, inside, slots=(0, 1, 2)):
        for k in slots:
            for q in range(0, CX, 2):
                below, above = rkc[f, k, 0, q // 2], rkc[f, k, 1, q // 2]
                if inside:
                    below, above = below * in_lo_y, above * in_hi_y
                field[k * CX + q, pl.ds(CY, 8), :] = jnp.where(chalf, above, below)
                field[k * CX + q + 1, pl.ds(CY, 8), :] = pltpu.roll(jnp.where(chalf, below, above), 4, 0)

    def coarse_setup(own_only):
        for p, at_p, span in coarse_blocks(0 if own_only else 3):
            here = pl.ds(0, span[1])
            b = cab[1, at_p, here, :]
            b_up, b_down = along_y(b, lambda row: cab[1, at_p, row : row + 1, :], span, CY)
            b_right, b_left = z_beside(b)
            b_right = without_last(b_right)
            b_left = without_first(b_left)
            faces = [
                0.5 * (b + other)
                for other in (cab[1, at_p + 1, here, :], cab[1, at_p - 1, here, :], b_up, b_down, b_right, b_left)
            ]
            total = faces[0] + faces[1] + faces[2] + faces[3] + faces[4] + faces[5]
            whole = cab[0, at_p, here, :] + 0.25 * total
            if own_only:
                cdiag[p] = whole
                continue
            scale = masked(0.25 / whole, in_planes(p))
            if span == (0, EYC):
                scale = in_rows(scale, CY)
            w = [scale * face for face in faces]
            w[4] = without_last(w[4])
            w[5] = without_first(w[5])
            for e in range(6):
                cw[e, at_p, here, :] = w[e]

    def later_step(step, p, span):
        cur, other = (xb, xa) if step % 2 == 1 else (xa, xb)
        first, second = terms[step - 1]
        here = pl.ds(span[0], span[1] - span[0])
        update = first * ds[PX + p, here, :] + second * residual(cur, p, span)
        ds[PX + p, here, :] = update
        other[PX + p, here, :] = cur[PX + p, here, :] + update

    def fine_step(step, chosen):
        for p, span in fine_blocks(DEPTH - 1 - step):
            if (1 + step <= p < NX - 1 - step) == chosen:
                if step == 0:
                    first_step(p, span)
                else:
                    later_step(step, p, span)

    for side in (0, 1):
        wait_for(y_waits[0][side : side + 1])
        pass_on(side, False)
    slots = [pl.ds(k * CX, CX) for k in range(3)]
    ab_waits = exchange_coarse(
        pl.ds(0, 2), cab.at[:, slots[1], pl.ds(0, CY)],
        [cab.at[:, slot, pl.ds(0, CY)] for slot in slots], sab_sem, rab_sem,
    )
    for side in (0, 1):
        wait_for(y_waits[1][side : side + 1])
        pass_on(side, True)
    wait_for(y_waits[2])
    place_rows()
    for step in range(DEGREE):
        fine_step(step, True)
    wait_for(x_waits)
    for relay, arrives, *_ in corners:
        pl.when(arrives)(relay.wait_recv)
    place_corners()
    for step in range(DEGREE):
        fine_step(step, False)
    cur = xa if DEGREE % 2 == 0 else xb
    own = (0, NY)
    wait_for(ab_waits)
    place_coarse(1, cab.at[1], True, (1,))
    for p in (-1, CX):
        cab[1, CX + p, 0:CY] = cab[1, CX + p, 0:CY] * in_planes(p)
    coarse_setup(True)
    for q in range(CX):
        a = diag[2 * q] * residual(cur, 2 * q, own)
        b = diag[2 * q + 1] * residual(cur, 2 * q + 1, own)
        cg[CX + q, 0:CY] = 0.125 * restrict_pair(a, b) / cdiag[q]

    pack_coarse(2, lambda q: cg[CX + q, 0:CY])
    g_waits = exchange_coarse(
        2, cg.at[slots[1], pl.ds(0, CY)], [cg.at[slot, pl.ds(0, CY)] for slot in slots], sg_sem, rg_sem
    )
    place_coarse(0, cab.at[0], False)
    place_coarse(1, cab.at[1], True, (0, 2))
    for p in (*range(-CX, 0), *range(CX, 2 * CX)):
        cab[1, CX + p] = cab[1, CX + p] * in_planes(p)
    coarse_setup(False)
    wait_for(g_waits)
    place_coarse(2, cg, True)

    for p, at_p, span in coarse_blocks(4):
        here = pl.ds(0, span[1])
        g = masked(cg[at_p, here, :], in_planes(p))
        if in_planes(p) is not None:
            cg[at_p, here, :] = g
        update = g * (1.0 / THETA)
        cxs[0, at_p, here, :] = update
        cds[at_p, here, :] = update

    def coarse_residual(now, at_p, span):
        here = pl.ds(0, span[1])
        x = cxs[now, at_p, here, :]
        return (
            cg[at_p, here, :]
            - x
            + spread(
                x, lambda step, part: cxs[now, at_p + step, part[0] : part[1], :], span, CY,
                lambda e: cw[e, at_p, here, :],
            )
        )

    now = 0
    for step, (first, second) in enumerate(terms):
        for p, at_p, span in coarse_blocks(3 - step):
            here = pl.ds(0, span[1])
            update = first * cds[at_p, here, :] + second * coarse_residual(now, at_p, span)
            cds[at_p, here, :] = update
            cxs[1 - now, at_p, here, :] = cxs[now, at_p, here, :] + update
        now = 1 - now

    quarter = []
    for q in range(CX):
        quarter.append(cdiag[q] * coarse_residual(now, CX + q, (0, CY)))
    for h in range(CX // 2):
        both = quarter[2 * h] + quarter[2 * h + 1]
        for t in range(2):
            pair[t, 0:CY, :] = both[:, t * 128 : (t + 1) * 128]
        summed = jnp.concatenate(
            [pair[t, pl.ds(0, CY // 2, 2), :] + pair[t, pl.ds(1, CY // 2, 2), :] for t in range(2)], axis=1
        )
        coarsest[0, h] = 0.125 * halve_z(summed)
    l_waits = [
        send(coarsest.at[0], coarsest.at[dx], sl_sem.at[dx], rl_sem.at[dx], dx, 0) for dx in (4, 5, 3, 6, 2, 7, 1)
    ]

    for q in range(CX):
        fine = double_z(cxs[now, CX + q, 0:CY])
        for t in range(4):
            part = fine[:, t * 128 : (t + 1) * 128]
            wide[t, pl.ds(0, CY, 2), :] = part
            wide[t, pl.ds(1, CY, 2), :] = part
        full = jnp.concatenate([wide[t] for t in range(4)], axis=1)
        for p in (2 * q, 2 * q + 1):
            out_ref[p] = cur[PX + p, own_y, :] + full

    wait_for(l_waits)
    for dx in range(8):
        owner = lax.rem(gx + ngx - dx, ngx)
        last_ref[pl.ds(2 * owner, 2)] = coarsest[dx]
    for copy, dy in sent:
        when(beside[dy], copy.wait_send)
    for relay, arrives, *_ in corners:
        pl.when(arrives)(relay.wait_send)


def store(field, last, field_out, last_out, sem):
    copies = [pltpu.make_async_copy(field, field_out, sem.at[0]), pltpu.make_async_copy(last, last_out, sem.at[1])]
    for copy in copies:
        copy.start()
    for copy in copies:
        copy.wait()


def on_device(guess, rhs, alpha, beta):
    vmem = pltpu.VMEM
    dma = pltpu.SemaphoreType.DMA
    fine = (NX, NY, NZ)
    wide = (EX, EY, NZ)
    coarse = (EXC, EYC, CZ)
    scratch = [
        vmem(wide, F32), vmem(wide, F32), vmem(wide, F32), vmem(wide, F32), vmem(wide, F32), vmem(wide, F32),
        vmem(wide, F32), vmem(fine, F32), vmem((6, *wide), F32),
        vmem((2, 18, 8, NZ), F32), vmem((2, 18, 8, NZ), F32), vmem((2, 2, 4, 8, NZ), F32), vmem((2, 2, 4, 8, NZ), F32),
        vmem((4, NY, 128), F32), vmem((4, NY, 128), F32),
        vmem((2, *coarse), F32), vmem(coarse, F32), vmem((3, 2, CX // 2, 8, CZ), F32),
        vmem((3, 3, 2, CX // 2, 8, CZ), F32), vmem((6, *coarse), F32),
        vmem((2, *coarse), F32), vmem(coarse, F32), vmem((CX, CY, CZ), F32),
        vmem((8, 2, CY // 2, CZ // 2), F32),
        dma((4,)), dma((4, 2)), dma((4, 2)), dma((2, 3)), dma((2, 3)), dma((2, 2)), dma((2, 2)),
        dma((8,)), dma((8,)), dma((8,)), dma((8,)), dma((8,)), dma((8,)),
    ]
    placed = [pltpu.with_memory_space_constraint(x, pltpu.HBM) for x in (guess, rhs, alpha, beta)]
    results = pl.pallas_call(
        kernel,
        out_shape=(
            jax.ShapeDtypeStruct(fine, F32),
            jax.ShapeDtypeStruct((16, CY // 2, CZ // 2), F32),
        ),
        in_specs=[pl.BlockSpec(memory_space=pltpu.HBM)] * 4,
        out_specs=(pl.BlockSpec(memory_space=vmem), pl.BlockSpec(memory_space=vmem)),
        scratch_shapes=scratch,
        compiler_params=pltpu.CompilerParams(
            collective_id=0, has_side_effects=True, vmem_limit_bytes=40 << 20
        ),
        name="vcycle",
    )(*placed)
    return pl.pallas_call(
        store,
        out_shape=(
            jax.ShapeDtypeStruct(fine, F32),
            jax.ShapeDtypeStruct((16, CY // 2, CZ // 2), F32),
        ),
        in_specs=[pl.BlockSpec(memory_space=vmem)] * 2,
        out_specs=(pl.BlockSpec(memory_space=pltpu.HBM), pl.BlockSpec(memory_space=pltpu.HBM)),
        scratch_shapes=[dma((2,))],
        compiler_params=pltpu.CompilerParams(vmem_limit_bytes=4 << 20),
        name="store",
    )(*results)


def solution(mesh):
    placed = (P("gx", "yz", None),) * 4
    return jax.shard_map(
        on_device,
        mesh=mesh,
        in_specs=placed,
        out_specs=(P("gx", "yz", None), P(None, "yz", None)),
        check_vma=False,
    )
```

```python
import functools

import jax
import jax.numpy as jnp
from jax import lax
from jax.experimental import pallas as pl
from jax.experimental.pallas import tpu as pltpu
from jax.sharding import PartitionSpec as P

DEGREE = 4
THETA = 1.125
DELTA = 0.875
MESH = pl.DeviceIdType.MESH
F32 = jnp.float32

NX, NY, NZ = 8, 16, 512
CX, CY, CZ = 4, 8, 256
DEPTH = DEGREE + 1
PX = DEPTH
EX, EY = NX + 2 * DEPTH, NY + 8
EXC, EYC = CX + 2 * DEGREE, CY + 8


def cheb_terms():
    sigma = THETA / DELTA
    rho_prev = 1.0 / sigma
    terms = []
    for _ in range(DEGREE - 1):
        rho_next = 1.0 / (2.0 * sigma - rho_prev)
        terms.append((rho_next * rho_prev, 2.0 * rho_next / DELTA))
        rho_prev = rho_next
    return terms


def lanes(shape):
    return lax.broadcasted_iota(jnp.int32, shape, 1)


def rows(shape):
    return lax.broadcasted_iota(jnp.int32, shape, 0)


def halve_z(field):
    count, width = field.shape
    lane = lanes((count, 128))
    even = jnp.where(lane < 64, 2 * lane, 2 * lane - 128)
    low = lane < 64
    tiles = []
    for t in range(width // 256):
        halves = []
        for h in range(2):
            part = field[:, (2 * t + h) * 128 : (2 * t + h + 1) * 128]
            part = part + pltpu.roll(part, 127, 1)
            halves.append(jnp.take_along_axis(part, even, axis=1))
        tiles.append(jnp.where(low, halves[0], halves[1]))
    return tiles[0] if len(tiles) == 1 else jnp.concatenate(tiles, axis=1)


def double_z(field):
    count, width = field.shape
    half = lanes((count, 128)) // 2
    tiles = []
    for t in range(width // 128):
        part = field[:, t * 128 : (t + 1) * 128]
        tiles.append(jnp.take_along_axis(part, half, axis=1))
        tiles.append(jnp.take_along_axis(part, half + 64, axis=1))
    return jnp.concatenate(tiles, axis=1)


def without_last(field):
    width = field.shape[1]
    tail = field[:, width - 128 :]
    return jnp.concatenate([field[:, : width - 128], jnp.where(lanes(tail.shape) == 127, 0.0, tail)], axis=1)


def without_first(field):
    head = field[:, :128]
    return jnp.concatenate([jnp.where(lanes(head.shape) == 0, 0.0, head), field[:, 128:]], axis=1)


def z_beside(field):
    width = field.shape[1]
    return pltpu.roll(field, width - 1, 1), pltpu.roll(field, 1, 1)


def y_beside(field, below, above):
    count = field.shape[0]
    row = rows(field.shape)
    up = jnp.where(row == count - 1, jnp.broadcast_to(above, field.shape), pltpu.roll(field, count - 1, 0))
    down = jnp.where(row == 0, jnp.broadcast_to(below, field.shape), pltpu.roll(field, 1, 0))
    return up, down


def tile_a(p):
    return 2 * p + (1 if p >= 4 else 0)


def tile_b(p):
    return 2 * p + (0 if p >= 4 else 1)


def kernel(
    guess_h, rhs_h, alpha_h, beta_h, out_ref, last_ref,
    xa, xb, be, al, rh, ds, gs, diag, ws, pk, rk, qk, rc,
    pair, wide, cab, cg, pkc, rkc, pcc, rcc, cw, cxs, cds, cdiag, coarsest,
    load_sem, sx_sem, rx_sem, sy_sem, ry_sem, sc_sem, rc_sem, sab_sem, rab_sem, sg_sem, rg_sem, sl_sem, rl_sem,
):
    gx = lax.axis_index("gx")
    yz = lax.axis_index("yz")
    ngx = lax.axis_size("gx")
    nyz = lax.axis_size("yz")

    def at(dx, dy):
        return (lax.rem(gx + ngx + dx, ngx), lax.rem(yz + nyz + dy, nyz))

    beside = {-1: yz > 0, 0: None, 1: yz < nyz - 1}

    def when(condition, act):
        if condition is None:
            act()
        else:
            pl.when(condition)(act)

    def greet(dx, dy):
        pl.semaphore_signal(barrier, inc=1, device_id=at(dx, dy), device_id_type=MESH)

    own_x, own_y, edge_y = pl.ds(PX, NX), pl.ds(0, NY), pl.ds(NY, 8)
    around = [(-1, -1), (-1, 1), (1, -1), (1, 1), (0, -1), (0, 1), (-1, 0), (1, 0)]
    barrier = pltpu.get_barrier_semaphore()
    for dx, dy in around:
        if dy != 0:
            when(beside[dy], functools.partial(greet, dx, dy))
    loads = []
    for k, (src, dst) in enumerate(((guess_h, xa), (beta_h, be), (alpha_h, al), (rhs_h, rh))):
        copy = pltpu.make_async_copy(src, dst.at[own_x, own_y], load_sem.at[k])
        copy.start()
        loads.append(copy)
    for dx in range(1, 8):
        greet(dx, 0)
    greeted = 7 + 3 * (yz > 0).astype(jnp.int32) + 3 * (yz < nyz - 1).astype(jnp.int32)

    half = rows((8, NZ)) < 4

    def packed(first, second, side):
        moved = pltpu.roll(second, 4, 0)
        return jnp.where(half, moved, first) if side == 0 else jnp.where(half, first, moved)

    odd = lax.rem(gx, 2)

    def pack_rows(half_at):
        for side, start in ((0, 8), (1, 0)):
            tile = pl.ds(start, 8)
            for k in range(4):
                p = 4 * half_at + k
                one = PX + p
                pk[side, 2 * p + half_at] = packed(xa[one, tile, :], be[one, tile, :], side)
                pk[side, 2 * p + 1 - half_at] = packed(al[one, tile, :], rh[one, tile, :], side)

    for copy in loads:
        copy.wait()
    pack_rows(odd)
    for side, missing in ((0, yz == 0), (1, yz == nyz - 1)):

        @pl.when(missing)
        def _(side=side):
            rk[side] = jnp.ones(rk.shape[1:], F32)
            for k in range(3):
                if k < 2:
                    rc[k, side] = jnp.ones(rc.shape[2:], F32)
                    for f in range(3):
                        rcc[f, k, side] = jnp.ones(rcc.shape[3:], F32)
                rkc[k, side] = jnp.ones(rkc.shape[2:], F32)

    pl.semaphore_wait(barrier, greeted)

    sent = []

    def copy_of(src, dst, s_sem, r_sem, device):
        return pltpu.make_async_remote_copy(
            src_ref=src, dst_ref=dst, send_sem=s_sem, recv_sem=r_sem, device_id=device, device_id_type=MESH
        )

    def send(src, dst, s_sem, r_sem, dx, dy):
        copy = copy_of(src, dst, s_sem, r_sem, at(dx, dy))
        when(beside[dy], copy.start)
        sent.append((copy, dy))
        return copy, dy

    def wait_for(copies):
        for copy, dy in copies:
            when(beside[-dy], copy.wait_recv)

    first_core = lax.rem(gx, 2) == 0
    ahead = 8 * odd
    parts = (pl.ds(ahead, 8), pl.ds(8 - ahead, 8), pl.ds(16, 2))

    def send_rows(k):
        part = parts[k]
        return [
            send(pk.at[side, part], rk.at[side, part], sy_sem.at[side, k], ry_sem.at[side, k], 0, 1 - 2 * side)
            for side in (0, 1)
        ]

    y_waits = [send_rows(0)]
    x_waits = []
    for k, (src, dst, deep) in enumerate(
        ((guess_h, xa, DEPTH), (beta_h, be, DEPTH), (alpha_h, al, DEPTH - 1), (rhs_h, rh, DEPTH - 1))
    ):
        x_waits.append(
            send(
                src.at[pl.ds(NX - deep, deep)], dst.at[pl.ds(PX - deep, deep), own_y],
                sx_sem.at[k, 0], rx_sem.at[k, 0], 1, 0,
            )
        )
        x_waits.append(
            send(
                src.at[pl.ds(0, deep)], dst.at[pl.ds(PX + NX, deep), own_y],
                sx_sem.at[k, 1], rx_sem.at[k, 1], -1, 0,
            )
        )

    pack_rows(1 - odd)
    y_waits.append(send_rows(1))
    for side, fifth in ((0, 11), (1, 4)):
        for p in range(NX):
            pk[side, 16, p : p + 1, :] = xa[PX + p, fifth : fifth + 1, :]
            pk[side, 17, p : p + 1, :] = be[PX + p, fifth : fifth + 1, :]
    y_waits.append(send_rows(2))
    sub = rows((8, NZ))
    nearest = [(sub % 4) == 0, (sub % 4) == 3]
    near_two = [(sub % 4) < 2, (sub % 4) >= 2]

    def pack_corner(sx, sy):
        planes = range(7, 3, -1) if sx == 0 else range(4)
        a = [rk[sy, tile_a(p)] for p in planes]
        b = [rk[sy, tile_b(p)] for p in planes]
        one = 1 if sy == 0 else 7
        qk[sx, sy, 0] = a[0]
        qk[sx, sy, 1] = jnp.where(nearest[sy], pltpu.roll(a[3], one, 0), b[0])
        qk[sx, sy, 2] = jnp.where(nearest[sy], pltpu.roll(b[2], one, 0), a[1])
        qk[sx, sy, 3] = jnp.where(near_two[sy], pltpu.roll(a[2], 2, 0), b[1])

    corners = []
    for sx in (0, 1):
        same_chip = first_core if sx == 0 else jnp.logical_not(first_core)
        for sy in (0, 1):
            relay = copy_of(qk.at[sx, sy], rc.at[sx, sy], sc_sem.at[sx, sy], rc_sem.at[sx, sy], at(1 - 2 * sx, 0))
            corners.append((relay, beside[2 * sy - 1], sx, sy, same_chip))

    def pass_on(side, on_chip):
        for relay, arrives, sx, sy, same_chip in corners:
            if sy == side:
                chosen = same_chip if on_chip else jnp.logical_not(same_chip)

                @pl.when(jnp.logical_and(arrives, chosen))
                def _(relay=relay, sx=sx, sy=sy):
                    pack_corner(sx, sy)
                    relay.start()

    def restrict_pair(first, second):
        both = first + second
        for t in range(4):
            pair[t] = both[:, t * 128 : (t + 1) * 128]
        summed = jnp.concatenate(
            [pair[t, pl.ds(0, CY, 2), :] + pair[t, pl.ds(1, CY, 2), :] for t in range(4)], axis=1
        )
        return halve_z(summed)

    csub = rows((8, CZ))
    chalf = csub < 4

    def pack_coarse(f, get):
        for q in range(0, CX, 2):
            this, then = get(q), pltpu.roll(get(q + 1), 4, 0)
            pkc[f, 0, q // 2] = jnp.where(chalf, then, this)
            pkc[f, 1, q // 2] = jnp.where(chalf, this, then)
        for ix, (tile, third, slots_at) in enumerate(((1, 1, (4, 3)), (0, 2, (0, 7)))):
            near = get(third)
            for side, row in ((0, near[CY - 1 : CY]), (1, near[0:1])):
                pcc[f, ix, side] = jnp.where(
                    csub == slots_at[side], jnp.broadcast_to(row, (8, CZ)), pkc[f, side, tile]
                )

    def exchange_coarse(fields, own, others, s_sem, r_sem):
        copies = []
        for k, (dx, dy) in enumerate(around):
            if dy == 0:
                src, dst = own, others[1 - dx]
            else:
                side = (1 - dy) // 2
                if dx == 0:
                    src, dst = pkc.at[fields, side], rkc.at[fields, side]
                else:
                    ix = (1 - dx) // 2
                    src, dst = pcc.at[fields, ix, side], rcc.at[fields, ix, side]
            copies.append(send(src, dst, s_sem.at[k], r_sem.at[k], dx, dy))
        return copies

    for q in range(CX):
        one, two = PX + 2 * q, PX + 2 * q + 1
        cab[0, CX + q, 0:CY] = 0.125 * restrict_pair(al[one, own_y, :], al[two, own_y, :])
        cab[1, CX + q, 0:CY] = 0.125 * restrict_pair(be[one, own_y, :], be[two, own_y, :])
    for f in range(2):
        pack_coarse(f, lambda q, f=f: cab[f, CX + q, 0:CY])
    in_lo_x = (gx > 0).astype(F32)
    in_hi_x = (gx < ngx - 1).astype(F32)
    in_lo_y = (yz > 0).astype(F32)
    in_hi_y = (yz < nyz - 1).astype(F32)
    terms = cheb_terms()

    def join(below, above):
        return jnp.where(half, above, below)

    def place(plane, a_below, a_above, b_below=None, b_above=None):
        a_below, a_above = a_below * in_lo_y, a_above * in_hi_y
        xa[plane, edge_y, :] = join(a_below, a_above)
        be[plane, edge_y, :] = pltpu.roll(join(a_above, a_below), 4, 0)
        if b_below is not None:
            al[plane, edge_y, :] = join(b_below, b_above)
            rh[plane, edge_y, :] = pltpu.roll(join(b_above, b_below), 4, 0)

    def place_rows():
        for p in range(NX):
            place(PX + p, rk[0, tile_a(p)], rk[1, tile_a(p)], rk[0, tile_b(p)], rk[1, tile_b(p)])

    def place_corners():
        for sx in (0, 1):
            tiles = [[rc[sx, sy, k] for sy in (0, 1)] for k in range(4)]

            def back(k):
                return [pltpu.roll(tiles[k][0], 7, 0), pltpu.roll(tiles[k][1], 1, 0)]

            blocks = (
                [*tiles[0], *tiles[1]],
                [*tiles[2], *tiles[3]],
                [*(pltpu.roll(tile, 6, 0) for tile in tiles[3]), *back(2)],
                back(1),
            )
            for k, block in enumerate(blocks):
                place(PX - 1 - k if sx == 0 else PX + NX + k, *block)
        for edge, start in ((gx == 0, 0), (gx == ngx - 1, PX + NX)):

            @pl.when(edge)
            def _(start=start):
                for plane in range(start, start + DEPTH):
                    xa[plane] = jnp.zeros((EY, NZ), F32)
                    be[plane] = jnp.zeros((EY, NZ), F32)

    def fine_blocks(deep):
        found = []
        for p in range(-deep, NX + deep):
            beyond = max(-p, p - NX + 1, 0)
            found.append((p, (0, EY) if beyond < deep else (0, NY)))
        return found

    def along_y(x, at_row, span, own, fifth=None):
        count = own + 8
        if span == (0, own):
            return y_beside(x, at_row(count - 1), at_row(own))
        up, down = pltpu.roll(x, count - 1, 0), pltpu.roll(x, 1, 0)
        if fifth is not None:
            row = rows(x.shape)
            up = jnp.where(row == own + 3, jnp.broadcast_to(fifth[1], x.shape), up)
            down = jnp.where(row == own + 4, jnp.broadcast_to(fifth[0], x.shape), down)
        return up, down

    def spread(x, x_at, span, own, w, fifth=None):
        up, down = along_y(x, lambda row: x_at(0, (row, row + 1)), span, own, fifth)
        right, left = z_beside(x)
        return (
            w(0) * x_at(1, span) + w(1) * x_at(-1, span) + w(2) * up + w(3) * down + w(4) * right + w(5) * left
        )

    def in_rows(value, own):
        tail = value[own:]
        inside = jnp.where(rows(tail.shape) < 4, in_hi_y, in_lo_y)
        return jnp.concatenate([value[:own], tail * inside], axis=0)

    def first_step(p, span):
        lo, hi = span
        here = pl.ds(lo, hi - lo)
        b = be[PX + p, here, :]
        fifth = fifth_b = None
        if 0 <= p < NX:
            part = slice(p, p + 1)
            fifth = (rk[0, 16, part, :] * in_lo_y, rk[1, 16, part, :] * in_hi_y)
            fifth_b = (rk[0, 17, part, :] * in_lo_y, rk[1, 17, part, :] * in_hi_y)
        b_up, b_down = along_y(b, lambda row: be[PX + p, row : row + 1, :], span, NY, fifth_b)
        b_right, b_left = z_beside(b)
        b_right = without_last(b_right)
        b_left = without_first(b_left)
        pairs = [
            b + other for other in (be[PX + p + 1, here, :], be[PX + p - 1, here, :], b_up, b_down, b_right, b_left)
        ]
        total = pairs[0] + pairs[1] + pairs[2] + pairs[3] + pairs[4] + pairs[5]
        whole = al[PX + p, here, :] + 0.5 * total
        if 0 <= p < NX:
            diag[p] = whole[0:NY]
        inverse = 1.0 / whole
        if p < 0:
            inverse = inverse * in_lo_x
        if p >= NX:
            inverse = inverse * in_hi_x
        if span == (0, EY):
            inverse = in_rows(inverse, NY)
        scale = 0.5 * inverse
        w = [scale * pair for pair in pairs]
        w[4] = without_last(w[4])
        w[5] = without_first(w[5])
        for e in range(6):
            ws[e, PX + p, here, :] = w[e]
        g = inverse * rh[PX + p, here, :]
        gs[PX + p, here, :] = g
        x = xa[PX + p, here, :]
        resid = g - x + spread(x, lambda step, part: xa[PX + p + step, part[0] : part[1], :], span, NY, lambda e: w[e], fifth)
        update = resid * (1.0 / THETA)
        ds[PX + p, here, :] = update
        xb[PX + p, here, :] = x + update

    def residual(cur, p, span):
        here = pl.ds(span[0], span[1] - span[0])
        x = cur[PX + p, here, :]
        return (
            gs[PX + p, here, :]
            - x
            + spread(
                x, lambda step, part: cur[PX + p + step, part[0] : part[1], :], span, NY,
                lambda e: ws[e, PX + p, here, :],
            )
        )

    def coarse_blocks(deep):
        found = []
        for p in range(-deep, CX + deep):
            beyond = max(-p, p - CX + 1, 0)
            found.append((p, CX + p, (0, EYC) if beyond < deep else (0, CY)))
        return found

    def in_planes(p):
        return in_lo_x if p < 0 else in_hi_x if p >= CX else None

    def masked(value, mask):
        return value if mask is None else value * mask

    def place_coarse(f, field, inside, slots=(0, 1, 2)):
        def inner(below, above):
            return (below * in_lo_y, above * in_hi_y) if inside else (below, above)

        def join_rows(plane, below, above):
            field[plane, pl.ds(CY, 8), :] = jnp.where(chalf, above, below)
            field[plane + 1, pl.ds(CY, 8), :] = pltpu.roll(jnp.where(chalf, below, above), 4, 0)

        for k in slots:
            if k == 1:
                for q in range(0, CX, 2):
                    join_rows(CX + q, *inner(rkc[f, 0, q // 2], rkc[f, 1, q // 2]))
                continue
            ix = k // 2
            below, above = inner(rcc[f, ix, 0], rcc[f, ix, 1])
            join_rows(2 if ix == 0 else 2 * CX, below, above)
            low, high = (4, 3) if ix == 0 else (0, 7)
            field[1 if ix == 0 else 2 * CX + 2, pl.ds(CY, 8), :] = jnp.where(
                chalf,
                jnp.broadcast_to(above[high : high + 1], (8, CZ)),
                jnp.broadcast_to(below[low : low + 1], (8, CZ)),
            )

    def coarse_setup(own_only):
        for p, at_p, span in coarse_blocks(0 if own_only else 3):
            here = pl.ds(0, span[1])
            b = cab[1, at_p, here, :]
            b_up, b_down = along_y(b, lambda row: cab[1, at_p, row : row + 1, :], span, CY)
            b_right, b_left = z_beside(b)
            b_right = without_last(b_right)
            b_left = without_first(b_left)
            faces = [
                0.5 * (b + other)
                for other in (cab[1, at_p + 1, here, :], cab[1, at_p - 1, here, :], b_up, b_down, b_right, b_left)
            ]
            total = faces[0] + faces[1] + faces[2] + faces[3] + faces[4] + faces[5]
            whole = cab[0, at_p, here, :] + 0.25 * total
            if own_only:
                cdiag[p] = whole
                continue
            scale = masked(0.25 / whole, in_planes(p))
            if span == (0, EYC):
                scale = in_rows(scale, CY)
            w = [scale * face for face in faces]
            w[4] = without_last(w[4])
            w[5] = without_first(w[5])
            for e in range(6):
                cw[e, at_p, here, :] = w[e]

    def later_step(step, p, span):
        cur, other = (xb, xa) if step % 2 == 1 else (xa, xb)
        first, second = terms[step - 1]
        here = pl.ds(span[0], span[1] - span[0])
        update = first * ds[PX + p, here, :] + second * residual(cur, p, span)
        ds[PX + p, here, :] = update
        other[PX + p, here, :] = cur[PX + p, here, :] + update

    def fine_step(step, chosen):
        for p, span in fine_blocks(DEPTH - 1 - step):
            if (1 + step <= p < NX - 1 - step) == chosen:
                if step == 0:
                    first_step(p, span)
                else:
                    later_step(step, p, span)

    for side in (0, 1):
        wait_for(y_waits[0][side : side + 1])
        pass_on(side, False)
    slots = [pl.ds(k * CX, CX) for k in range(3)]
    ab_waits = exchange_coarse(
        pl.ds(0, 2), cab.at[:, slots[1], pl.ds(0, CY)],
        [cab.at[:, slot, pl.ds(0, CY)] for slot in slots], sab_sem, rab_sem,
    )
    for side in (0, 1):
        wait_for(y_waits[1][side : side + 1])
        pass_on(side, True)
    wait_for(y_waits[2])
    place_rows()
    for step in range(DEGREE):
        fine_step(step, True)
    wait_for(x_waits)
    for relay, arrives, *_ in corners:
        pl.when(arrives)(relay.wait_recv)
    place_corners()
    for step in range(DEGREE):
        fine_step(step, False)
    cur = xa if DEGREE % 2 == 0 else xb
    own = (0, NY)
    wait_for(ab_waits)
    place_coarse(1, cab.at[1], True, (1,))
    for p in (-1, CX):
        cab[1, CX + p, 0:CY] = cab[1, CX + p, 0:CY] * in_planes(p)
    coarse_setup(True)
    for q in range(CX):
        a = diag[2 * q] * residual(cur, 2 * q, own)
        b = diag[2 * q + 1] * residual(cur, 2 * q + 1, own)
        cg[CX + q, 0:CY] = 0.125 * restrict_pair(a, b) / cdiag[q]

    pack_coarse(2, lambda q: cg[CX + q, 0:CY])
    g_waits = exchange_coarse(
        2, cg.at[slots[1], pl.ds(0, CY)], [cg.at[slot, pl.ds(0, CY)] for slot in slots], sg_sem, rg_sem
    )
    place_coarse(0, cab.at[0], False)
    place_coarse(1, cab.at[1], True, (0, 2))
    for p in (*range(-CX, 0), *range(CX, 2 * CX)):
        cab[1, CX + p] = cab[1, CX + p] * in_planes(p)
    coarse_setup(False)
    wait_for(g_waits)
    place_coarse(2, cg, True)

    for p, at_p, span in coarse_blocks(4):
        here = pl.ds(0, span[1])
        g = masked(cg[at_p, here, :], in_planes(p))
        if in_planes(p) is not None:
            cg[at_p, here, :] = g
        update = g * (1.0 / THETA)
        cxs[0, at_p, here, :] = update
        cds[at_p, here, :] = update

    def coarse_residual(now, at_p, span):
        here = pl.ds(0, span[1])
        x = cxs[now, at_p, here, :]
        return (
            cg[at_p, here, :]
            - x
            + spread(
                x, lambda step, part: cxs[now, at_p + step, part[0] : part[1], :], span, CY,
                lambda e: cw[e, at_p, here, :],
            )
        )

    now = 0
    for step, (first, second) in enumerate(terms):
        for p, at_p, span in coarse_blocks(3 - step):
            here = pl.ds(0, span[1])
            update = first * cds[at_p, here, :] + second * coarse_residual(now, at_p, span)
            cds[at_p, here, :] = update
            cxs[1 - now, at_p, here, :] = cxs[now, at_p, here, :] + update
        now = 1 - now

    quarter = []
    for q in range(CX):
        quarter.append(cdiag[q] * coarse_residual(now, CX + q, (0, CY)))
    for h in range(CX // 2):
        both = quarter[2 * h] + quarter[2 * h + 1]
        for t in range(2):
            pair[t, 0:CY, :] = both[:, t * 128 : (t + 1) * 128]
        summed = jnp.concatenate(
            [pair[t, pl.ds(0, CY // 2, 2), :] + pair[t, pl.ds(1, CY // 2, 2), :] for t in range(2)], axis=1
        )
        coarsest[0, h] = 0.125 * halve_z(summed)
    earlier = len(sent)
    l_waits = [
        send(coarsest.at[0], coarsest.at[dx], sl_sem.at[dx], rl_sem.at[dx], dx, 0) for dx in (4, 5, 3, 6, 2, 7, 1)
    ]

    for q in range(CX):
        fine = double_z(cxs[now, CX + q, 0:CY])
        for t in range(4):
            part = fine[:, t * 128 : (t + 1) * 128]
            wide[t, pl.ds(0, CY, 2), :] = part
            wide[t, pl.ds(1, CY, 2), :] = part
        full = jnp.concatenate([wide[t] for t in range(4)], axis=1)
        for p in (2 * q, 2 * q + 1):
            out_ref[p] = cur[PX + p, own_y, :] + full

    for copy, dy in sent[:earlier]:
        when(beside[dy], copy.wait_send)
    for relay, arrives, *_ in corners:
        pl.when(arrives)(relay.wait_send)
    wait_for(l_waits)
    for dx in range(8):
        owner = lax.rem(gx + ngx - dx, ngx)
        last_ref[pl.ds(2 * owner, 2)] = coarsest[dx]
    for copy, _ in l_waits:
        copy.wait_send()


def store(field, last, field_out, last_out, sem):
    copies = [pltpu.make_async_copy(field, field_out, sem.at[0]), pltpu.make_async_copy(last, last_out, sem.at[1])]
    for copy in copies:
        copy.start()
    for copy in copies:
        copy.wait()


def on_device(guess, rhs, alpha, beta):
    vmem = pltpu.VMEM
    dma = pltpu.SemaphoreType.DMA
    fine = (NX, NY, NZ)
    wide = (EX, EY, NZ)
    coarse = (EXC, EYC, CZ)
    scratch = [
        vmem(wide, F32), vmem(wide, F32), vmem(wide, F32), vmem(wide, F32), vmem(wide, F32), vmem(wide, F32),
        vmem(wide, F32), vmem(fine, F32), vmem((6, *wide), F32),
        vmem((2, 18, 8, NZ), F32), vmem((2, 18, 8, NZ), F32), vmem((2, 2, 4, 8, NZ), F32), vmem((2, 2, 4, 8, NZ), F32),
        vmem((4, NY, 128), F32), vmem((4, NY, 128), F32),
        vmem((2, *coarse), F32), vmem(coarse, F32), vmem((3, 2, CX // 2, 8, CZ), F32),
        vmem((3, 2, CX // 2, 8, CZ), F32), vmem((3, 2, 2, 8, CZ), F32), vmem((3, 2, 2, 8, CZ), F32),
        vmem((6, *coarse), F32),
        vmem((2, *coarse), F32), vmem(coarse, F32), vmem((CX, CY, CZ), F32),
        vmem((8, 2, CY // 2, CZ // 2), F32),
        dma((4,)), dma((4, 2)), dma((4, 2)), dma((2, 3)), dma((2, 3)), dma((2, 2)), dma((2, 2)),
        dma((8,)), dma((8,)), dma((8,)), dma((8,)), dma((8,)), dma((8,)),
    ]
    placed = [pltpu.with_memory_space_constraint(x, pltpu.HBM) for x in (guess, rhs, alpha, beta)]
    results = pl.pallas_call(
        kernel,
        out_shape=(
            jax.ShapeDtypeStruct(fine, F32),
            jax.ShapeDtypeStruct((16, CY // 2, CZ // 2), F32),
        ),
        in_specs=[pl.BlockSpec(memory_space=pltpu.HBM)] * 4,
        out_specs=(pl.BlockSpec(memory_space=vmem), pl.BlockSpec(memory_space=vmem)),
        scratch_shapes=scratch,
        compiler_params=pltpu.CompilerParams(
            collective_id=0, has_side_effects=True, vmem_limit_bytes=40 << 20
        ),
        name="vcycle",
    )(*placed)
    return pl.pallas_call(
        store,
        out_shape=(
            jax.ShapeDtypeStruct(fine, F32),
            jax.ShapeDtypeStruct((16, CY // 2, CZ // 2), F32),
        ),
        in_specs=[pl.BlockSpec(memory_space=vmem)] * 2,
        out_specs=(pl.BlockSpec(memory_space=pltpu.HBM), pl.BlockSpec(memory_space=pltpu.HBM)),
        scratch_shapes=[dma((2,))],
        compiler_params=pltpu.CompilerParams(vmem_limit_bytes=4 << 20),
        name="store",
    )(*results)


def solution(mesh):
    placed = (P("gx", "yz", None),) * 4
    return jax.shard_map(
        on_device,
        mesh=mesh,
        in_specs=placed,
        out_specs=(P("gx", "yz", None), P(None, "yz", None)),
        check_vma=False,
    )
```

```python
import functools

import jax
import jax.numpy as jnp
from jax import lax
from jax.experimental import pallas as pl
from jax.experimental.pallas import tpu as pltpu
from jax.sharding import PartitionSpec as P

DEGREE = 4
THETA = 1.125
DELTA = 0.875
MESH = pl.DeviceIdType.MESH
F32 = jnp.float32

NX, NY, NZ = 8, 16, 512
CX, CY, CZ = 4, 8, 256
DEPTH = DEGREE + 1
PX = DEPTH
EX, EY = NX + 2 * DEPTH, NY + 8
EXC, EYC = CX + 2 * DEGREE, CY + 8


def cheb_terms():
    sigma = THETA / DELTA
    rho_prev = 1.0 / sigma
    terms = []
    for _ in range(DEGREE - 1):
        rho_next = 1.0 / (2.0 * sigma - rho_prev)
        terms.append((rho_next * rho_prev, 2.0 * rho_next / DELTA))
        rho_prev = rho_next
    return terms


def lanes(shape):
    return lax.broadcasted_iota(jnp.int32, shape, 1)


def rows(shape):
    return lax.broadcasted_iota(jnp.int32, shape, 0)


def halve_z(field):
    count, width = field.shape
    lane = lanes((count, 128))
    even = jnp.where(lane < 64, 2 * lane, 2 * lane - 128)
    low = lane < 64
    tiles = []
    for t in range(width // 256):
        halves = []
        for h in range(2):
            part = field[:, (2 * t + h) * 128 : (2 * t + h + 1) * 128]
            part = part + pltpu.roll(part, 127, 1)
            halves.append(jnp.take_along_axis(part, even, axis=1))
        tiles.append(jnp.where(low, halves[0], halves[1]))
    return tiles[0] if len(tiles) == 1 else jnp.concatenate(tiles, axis=1)


def double_z(field):
    count, width = field.shape
    half = lanes((count, 128)) // 2
    tiles = []
    for t in range(width // 128):
        part = field[:, t * 128 : (t + 1) * 128]
        tiles.append(jnp.take_along_axis(part, half, axis=1))
        tiles.append(jnp.take_along_axis(part, half + 64, axis=1))
    return jnp.concatenate(tiles, axis=1)


def without_last(field):
    width = field.shape[1]
    tail = field[:, width - 128 :]
    return jnp.concatenate([field[:, : width - 128], jnp.where(lanes(tail.shape) == 127, 0.0, tail)], axis=1)


def without_first(field):
    head = field[:, :128]
    return jnp.concatenate([jnp.where(lanes(head.shape) == 0, 0.0, head), field[:, 128:]], axis=1)


def z_beside(field):
    width = field.shape[1]
    return pltpu.roll(field, width - 1, 1), pltpu.roll(field, 1, 1)


def y_beside(field, below, above):
    count = field.shape[0]
    row = rows(field.shape)
    up = jnp.where(row == count - 1, jnp.broadcast_to(above, field.shape), pltpu.roll(field, count - 1, 0))
    down = jnp.where(row == 0, jnp.broadcast_to(below, field.shape), pltpu.roll(field, 1, 0))
    return up, down


def tile_a(p):
    return 2 * p + (1 if p >= 4 else 0)


def tile_b(p):
    return 2 * p + (0 if p >= 4 else 1)


def kernel(
    guess_h, rhs_h, alpha_h, beta_h, out_ref, last_ref,
    xa, xb, be, al, rh, ds, gs, diag, ws, pk, rk, qk, rc,
    pair, wide, cab, cg, pkc, rkc, pcc, rcc, cw, cxs, cds, cdiag, coarsest,
    load_sem, sx_sem, rx_sem, sy_sem, ry_sem, sc_sem, rc_sem, sab_sem, rab_sem, sg_sem, rg_sem, sl_sem, rl_sem,
):
    gx = lax.axis_index("gx")
    yz = lax.axis_index("yz")
    ngx = lax.axis_size("gx")
    nyz = lax.axis_size("yz")

    def at(dx, dy):
        return (lax.rem(gx + ngx + dx, ngx), lax.rem(yz + nyz + dy, nyz))

    beside = {-1: yz > 0, 0: None, 1: yz < nyz - 1}

    def when(condition, act):
        if condition is None:
            act()
        else:
            pl.when(condition)(act)

    def greet(dx, dy):
        pl.semaphore_signal(barrier, inc=1, device_id=at(dx, dy), device_id_type=MESH)

    own_x, own_y, edge_y = pl.ds(PX, NX), pl.ds(0, NY), pl.ds(NY, 8)
    around = [(-1, -1), (-1, 1), (1, -1), (1, 1), (0, -1), (0, 1), (-1, 0), (1, 0)]
    barrier = pltpu.get_barrier_semaphore()
    for dx, dy in around:
        if dy != 0:
            when(beside[dy], functools.partial(greet, dx, dy))
    loads = []
    for k, (src, dst) in enumerate(((guess_h, xa), (beta_h, be), (alpha_h, al), (rhs_h, rh))):
        copy = pltpu.make_async_copy(src, dst.at[own_x, own_y], load_sem.at[k])
        copy.start()
        loads.append(copy)
    for dx in range(1, 8):
        greet(dx, 0)
    greeted = 7 + 3 * (yz > 0).astype(jnp.int32) + 3 * (yz < nyz - 1).astype(jnp.int32)

    half = rows((8, NZ)) < 4

    def packed(first, second, side):
        moved = pltpu.roll(second, 4, 0)
        return jnp.where(half, moved, first) if side == 0 else jnp.where(half, first, moved)

    odd = lax.rem(gx, 2)

    def pack_rows(half_at):
        for side, start in ((0, 8), (1, 0)):
            tile = pl.ds(start, 8)
            for k in range(4):
                p = 4 * half_at + k
                one = PX + p
                pk[side, 2 * p + half_at] = packed(xa[one, tile, :], be[one, tile, :], side)
                pk[side, 2 * p + 1 - half_at] = packed(al[one, tile, :], rh[one, tile, :], side)

    for copy in loads:
        copy.wait()
    pack_rows(odd)
    for side, missing in ((0, yz == 0), (1, yz == nyz - 1)):

        @pl.when(missing)
        def _(side=side):
            rk[side] = jnp.ones(rk.shape[1:], F32)
            for k in range(3):
                if k < 2:
                    rc[k, side] = jnp.ones(rc.shape[2:], F32)
                    for f in range(3):
                        rcc[f, k, side] = jnp.ones(rcc.shape[3:], F32)
                rkc[k, side] = jnp.ones(rkc.shape[2:], F32)

    pl.semaphore_wait(barrier, greeted)

    sent = []

    def copy_of(src, dst, s_sem, r_sem, device):
        return pltpu.make_async_remote_copy(
            src_ref=src, dst_ref=dst, send_sem=s_sem, recv_sem=r_sem, device_id=device, device_id_type=MESH
        )

    def send(src, dst, s_sem, r_sem, dx, dy):
        copy = copy_of(src, dst, s_sem, r_sem, at(dx, dy))
        when(beside[dy], copy.start)
        sent.append((copy, dy))
        return copy, dy

    def wait_for(copies):
        for copy, dy in copies:
            when(beside[-dy], copy.wait_recv)

    first_core = lax.rem(gx, 2) == 0
    ahead = 8 * odd
    parts = (pl.ds(ahead, 8), pl.ds(8 - ahead, 8), pl.ds(16, 2))

    def send_rows(k):
        part = parts[k]
        return [
            send(pk.at[side, part], rk.at[side, part], sy_sem.at[side, k], ry_sem.at[side, k], 0, 1 - 2 * side)
            for side in (0, 1)
        ]

    y_waits = [send_rows(0)]
    x_waits = []
    for k, (src, dst, deep) in enumerate(
        ((guess_h, xa, DEPTH), (beta_h, be, DEPTH), (alpha_h, al, DEPTH - 1), (rhs_h, rh, DEPTH - 1))
    ):
        x_waits.append(
            send(
                src.at[pl.ds(NX - deep, deep)], dst.at[pl.ds(PX - deep, deep), own_y],
                sx_sem.at[k, 0], rx_sem.at[k, 0], 1, 0,
            )
        )
        x_waits.append(
            send(
                src.at[pl.ds(0, deep)], dst.at[pl.ds(PX + NX, deep), own_y],
                sx_sem.at[k, 1], rx_sem.at[k, 1], -1, 0,
            )
        )

    pack_rows(1 - odd)
    y_waits.append(send_rows(1))
    for side, fifth in ((0, 11), (1, 4)):
        for p in range(NX):
            pk[side, 16, p : p + 1, :] = xa[PX + p, fifth : fifth + 1, :]
            pk[side, 17, p : p + 1, :] = be[PX + p, fifth : fifth + 1, :]
    y_waits.append(send_rows(2))
    sub = rows((8, NZ))
    nearest = [(sub % 4) == 0, (sub % 4) == 3]
    near_two = [(sub % 4) < 2, (sub % 4) >= 2]

    def pack_corner(sx, sy):
        planes = range(7, 3, -1) if sx == 0 else range(4)
        a = [rk[sy, tile_a(p)] for p in planes]
        b = [rk[sy, tile_b(p)] for p in planes]
        one = 1 if sy == 0 else 7
        qk[sx, sy, 0] = a[0]
        qk[sx, sy, 1] = jnp.where(nearest[sy], pltpu.roll(a[3], one, 0), b[0])
        qk[sx, sy, 2] = jnp.where(nearest[sy], pltpu.roll(b[2], one, 0), a[1])
        qk[sx, sy, 3] = jnp.where(near_two[sy], pltpu.roll(a[2], 2, 0), b[1])

    corners = []
    for sx in (0, 1):
        same_chip = first_core if sx == 0 else jnp.logical_not(first_core)
        for sy in (0, 1):
            relay = copy_of(qk.at[sx, sy], rc.at[sx, sy], sc_sem.at[sx, sy], rc_sem.at[sx, sy], at(1 - 2 * sx, 0))
            corners.append((relay, beside[2 * sy - 1], sx, sy, same_chip))

    def pass_on(side, on_chip):
        for relay, arrives, sx, sy, same_chip in corners:
            if sy == side:
                chosen = same_chip if on_chip else jnp.logical_not(same_chip)

                @pl.when(jnp.logical_and(arrives, chosen))
                def _(relay=relay, sx=sx, sy=sy):
                    pack_corner(sx, sy)
                    relay.start()

    def restrict_pair(first, second):
        both = first + second
        for t in range(4):
            pair[t] = both[:, t * 128 : (t + 1) * 128]
        summed = jnp.concatenate(
            [pair[t, pl.ds(0, CY, 2), :] + pair[t, pl.ds(1, CY, 2), :] for t in range(4)], axis=1
        )
        return halve_z(summed)

    csub = rows((8, CZ))
    chalf = csub < 4

    def pack_coarse(f, get):
        for q in range(0, CX, 2):
            this, then = get(q), pltpu.roll(get(q + 1), 4, 0)
            pkc[f, 0, q // 2] = jnp.where(chalf, then, this)
            pkc[f, 1, q // 2] = jnp.where(chalf, this, then)
        for ix, (tile, third, slots_at) in enumerate(((1, 1, (4, 3)), (0, 2, (0, 7)))):
            near = get(third)
            for side, row in ((0, near[CY - 1 : CY]), (1, near[0:1])):
                pcc[f, ix, side] = jnp.where(
                    csub == slots_at[side], jnp.broadcast_to(row, (8, CZ)), pkc[f, side, tile]
                )

    def exchange_coarse(fields, own, others, s_sem, r_sem):
        copies = []
        for k, (dx, dy) in enumerate(around):
            if dy == 0:
                src, dst = own, others[1 - dx]
            else:
                side = (1 - dy) // 2
                if dx == 0:
                    src, dst = pkc.at[fields, side], rkc.at[fields, side]
                else:
                    ix = (1 - dx) // 2
                    src, dst = pcc.at[fields, ix, side], rcc.at[fields, ix, side]
            copies.append(send(src, dst, s_sem.at[k], r_sem.at[k], dx, dy))
        return copies

    for q in range(CX):
        one, two = PX + 2 * q, PX + 2 * q + 1
        cab[0, CX + q, 0:CY] = 0.125 * restrict_pair(al[one, own_y, :], al[two, own_y, :])
        cab[1, CX + q, 0:CY] = 0.125 * restrict_pair(be[one, own_y, :], be[two, own_y, :])
    for f in range(2):
        pack_coarse(f, lambda q, f=f: cab[f, CX + q, 0:CY])
    in_lo_x = (gx > 0).astype(F32)
    in_hi_x = (gx < ngx - 1).astype(F32)
    in_lo_y = (yz > 0).astype(F32)
    in_hi_y = (yz < nyz - 1).astype(F32)
    terms = cheb_terms()

    def join(below, above):
        return jnp.where(half, above, below)

    def place(plane, a_below, a_above, b_below=None, b_above=None):
        a_below, a_above = a_below * in_lo_y, a_above * in_hi_y
        xa[plane, edge_y, :] = join(a_below, a_above)
        be[plane, edge_y, :] = pltpu.roll(join(a_above, a_below), 4, 0)
        if b_below is not None:
            al[plane, edge_y, :] = join(b_below, b_above)
            rh[plane, edge_y, :] = pltpu.roll(join(b_above, b_below), 4, 0)

    def place_rows():
        for p in range(NX):
            place(PX + p, rk[0, tile_a(p)], rk[1, tile_a(p)], rk[0, tile_b(p)], rk[1, tile_b(p)])

    def fill_edges():
        for edge, start in ((gx == 0, 0), (gx == ngx - 1, PX + NX)):

            @pl.when(edge)
            def _(start=start):
                for plane in range(start, start + DEPTH):
                    xa[plane] = jnp.zeros((EY, NZ), F32)
                    be[plane] = jnp.zeros((EY, NZ), F32)

    def place_corners():
        for sx in (0, 1):
            tiles = [[rc[sx, sy, k] for sy in (0, 1)] for k in range(4)]

            def back(k):
                return [pltpu.roll(tiles[k][0], 7, 0), pltpu.roll(tiles[k][1], 1, 0)]

            blocks = (
                [*tiles[0], *tiles[1]],
                [*tiles[2], *tiles[3]],
                [*(pltpu.roll(tile, 6, 0) for tile in tiles[3]), *back(2)],
                back(1),
            )
            for k, block in enumerate(blocks):
                place(PX - 1 - k if sx == 0 else PX + NX + k, *block)
        fill_edges()

    def fine_blocks(deep):
        found = []
        for p in range(-deep, NX + deep):
            beyond = max(-p, p - NX + 1, 0)
            found.append((p, (0, EY) if beyond < deep else (0, NY)))
        return found

    def along_y(x, at_row, span, own, fifth=None):
        count = own + 8
        if span == (0, own):
            return y_beside(x, at_row(count - 1), at_row(own))
        if span == (own, count):
            up, down = y_beside(x, at_row(own - 1), at_row(0))
            if fifth is not None:
                row = rows(x.shape)
                up = jnp.where(row == 3, jnp.broadcast_to(fifth[1], x.shape), up)
                down = jnp.where(row == 4, jnp.broadcast_to(fifth[0], x.shape), down)
            return up, down
        up, down = pltpu.roll(x, count - 1, 0), pltpu.roll(x, 1, 0)
        if fifth is not None:
            row = rows(x.shape)
            up = jnp.where(row == own + 3, jnp.broadcast_to(fifth[1], x.shape), up)
            down = jnp.where(row == own + 4, jnp.broadcast_to(fifth[0], x.shape), down)
        return up, down

    def spread(x, x_at, span, own, w, fifth=None):
        up, down = along_y(x, lambda row: x_at(0, (row, row + 1)), span, own, fifth)
        right, left = z_beside(x)
        return (
            w(0) * x_at(1, span) + w(1) * x_at(-1, span) + w(2) * up + w(3) * down + w(4) * right + w(5) * left
        )

    def in_rows(value, own):
        tail = value[own:]
        inside = jnp.where(rows(tail.shape) < 4, in_hi_y, in_lo_y)
        return jnp.concatenate([value[:own], tail * inside], axis=0)

    def first_step(p, span):
        lo, hi = span
        here = pl.ds(lo, hi - lo)
        b = be[PX + p, here, :]
        fifth = fifth_b = None
        if 0 <= p < NX:
            part = slice(p, p + 1)
            fifth = (rk[0, 16, part, :] * in_lo_y, rk[1, 16, part, :] * in_hi_y)
            fifth_b = (rk[0, 17, part, :] * in_lo_y, rk[1, 17, part, :] * in_hi_y)
        b_up, b_down = along_y(b, lambda row: be[PX + p, row : row + 1, :], span, NY, fifth_b)
        b_right, b_left = z_beside(b)
        b_right = without_last(b_right)
        b_left = without_first(b_left)
        pairs = [
            b + other for other in (be[PX + p + 1, here, :], be[PX + p - 1, here, :], b_up, b_down, b_right, b_left)
        ]
        total = pairs[0] + pairs[1] + pairs[2] + pairs[3] + pairs[4] + pairs[5]
        whole = al[PX + p, here, :] + 0.5 * total
        if 0 <= p < NX and lo == 0:
            diag[p] = whole[0:NY]
        inverse = 1.0 / whole
        if p < 0:
            inverse = inverse * in_lo_x
        if p >= NX:
            inverse = inverse * in_hi_x
        if span == (0, EY):
            inverse = in_rows(inverse, NY)
        if span == (NY, EY):
            inverse = inverse * jnp.where(rows(inverse.shape) < 4, in_hi_y, in_lo_y)
        scale = 0.5 * inverse
        w = [scale * pair for pair in pairs]
        w[4] = without_last(w[4])
        w[5] = without_first(w[5])
        for e in range(6):
            ws[e, PX + p, here, :] = w[e]
        g = inverse * rh[PX + p, here, :]
        gs[PX + p, here, :] = g
        x = xa[PX + p, here, :]
        resid = g - x + spread(x, lambda step, part: xa[PX + p + step, part[0] : part[1], :], span, NY, lambda e: w[e], fifth)
        update = resid * (1.0 / THETA)
        ds[PX + p, here, :] = update
        xb[PX + p, here, :] = x + update

    def residual(cur, p, span):
        here = pl.ds(span[0], span[1] - span[0])
        x = cur[PX + p, here, :]
        return (
            gs[PX + p, here, :]
            - x
            + spread(
                x, lambda step, part: cur[PX + p + step, part[0] : part[1], :], span, NY,
                lambda e: ws[e, PX + p, here, :],
            )
        )

    def coarse_blocks(deep):
        found = []
        for p in range(-deep, CX + deep):
            beyond = max(-p, p - CX + 1, 0)
            found.append((p, CX + p, (0, EYC) if beyond < deep else (0, CY)))
        return found

    def in_planes(p):
        return in_lo_x if p < 0 else in_hi_x if p >= CX else None

    def masked(value, mask):
        return value if mask is None else value * mask

    def place_coarse(f, field, inside, slots=(0, 1, 2)):
        def inner(below, above):
            return (below * in_lo_y, above * in_hi_y) if inside else (below, above)

        def join_rows(plane, below, above):
            field[plane, pl.ds(CY, 8), :] = jnp.where(chalf, above, below)
            field[plane + 1, pl.ds(CY, 8), :] = pltpu.roll(jnp.where(chalf, below, above), 4, 0)

        for k in slots:
            if k == 1:
                for q in range(0, CX, 2):
                    join_rows(CX + q, *inner(rkc[f, 0, q // 2], rkc[f, 1, q // 2]))
                continue
            ix = k // 2
            below, above = inner(rcc[f, ix, 0], rcc[f, ix, 1])
            join_rows(2 if ix == 0 else 2 * CX, below, above)
            low, high = (4, 3) if ix == 0 else (0, 7)
            field[1 if ix == 0 else 2 * CX + 2, pl.ds(CY, 8), :] = jnp.where(
                chalf,
                jnp.broadcast_to(above[high : high + 1], (8, CZ)),
                jnp.broadcast_to(below[low : low + 1], (8, CZ)),
            )

    def coarse_setup(own_only):
        for p, at_p, span in coarse_blocks(0 if own_only else 3):
            here = pl.ds(0, span[1])
            b = cab[1, at_p, here, :]
            b_up, b_down = along_y(b, lambda row: cab[1, at_p, row : row + 1, :], span, CY)
            b_right, b_left = z_beside(b)
            b_right = without_last(b_right)
            b_left = without_first(b_left)
            faces = [
                0.5 * (b + other)
                for other in (cab[1, at_p + 1, here, :], cab[1, at_p - 1, here, :], b_up, b_down, b_right, b_left)
            ]
            total = faces[0] + faces[1] + faces[2] + faces[3] + faces[4] + faces[5]
            whole = cab[0, at_p, here, :] + 0.25 * total
            if own_only:
                cdiag[p] = whole
                continue
            scale = masked(0.25 / whole, in_planes(p))
            if span == (0, EYC):
                scale = in_rows(scale, CY)
            w = [scale * face for face in faces]
            w[4] = without_last(w[4])
            w[5] = without_first(w[5])
            for e in range(6):
                cw[e, at_p, here, :] = w[e]

    def later_step(step, p, span):
        cur, other = (xb, xa) if step % 2 == 1 else (xa, xb)
        first, second = terms[step - 1]
        here = pl.ds(span[0], span[1] - span[0])
        update = first * ds[PX + p, here, :] + second * residual(cur, p, span)
        ds[PX + p, here, :] = update
        other[PX + p, here, :] = cur[PX + p, here, :] + update

    def fine_step(step, chosen):
        for p, span in fine_blocks(DEPTH - 1 - step):
            if (1 + step <= p < NX - 1 - step) == chosen:
                later_step(step, p, span)

    for side in (0, 1):
        wait_for(y_waits[0][side : side + 1])
        pass_on(side, False)
    slots = [pl.ds(k * CX, CX) for k in range(3)]
    ab_waits = exchange_coarse(
        pl.ds(0, 2), cab.at[:, slots[1], pl.ds(0, CY)],
        [cab.at[:, slot, pl.ds(0, CY)] for slot in slots], sab_sem, rab_sem,
    )
    for side in (0, 1):
        wait_for(y_waits[1][side : side + 1])
        pass_on(side, True)
    place_rows()
    wait_for(x_waits)
    fill_edges()
    for p in range(NX):
        first_step(p, (0, NY))
    wait_for(y_waits[2])
    for p in range(1, NX - 1):
        first_step(p, (NY, EY))
    for step in range(1, DEGREE):
        fine_step(step, True)
    for relay, arrives, *_ in corners:
        pl.when(arrives)(relay.wait_recv)
    place_corners()
    for p, span in fine_blocks(DEPTH - 1):
        if not 0 <= p < NX:
            first_step(p, span)
        elif p in (0, NX - 1):
            first_step(p, (NY, EY))
    for step in range(1, DEGREE):
        fine_step(step, False)
    cur = xa if DEGREE % 2 == 0 else xb
    own = (0, NY)
    wait_for(ab_waits)
    place_coarse(1, cab.at[1], True, (1,))
    for p in (-1, CX):
        cab[1, CX + p, 0:CY] = cab[1, CX + p, 0:CY] * in_planes(p)
    coarse_setup(True)
    for q in range(CX):
        a = diag[2 * q] * residual(cur, 2 * q, own)
        b = diag[2 * q + 1] * residual(cur, 2 * q + 1, own)
        cg[CX + q, 0:CY] = 0.125 * restrict_pair(a, b) / cdiag[q]

    pack_coarse(2, lambda q: cg[CX + q, 0:CY])
    g_waits = exchange_coarse(
        2, cg.at[slots[1], pl.ds(0, CY)], [cg.at[slot, pl.ds(0, CY)] for slot in slots], sg_sem, rg_sem
    )
    place_coarse(0, cab.at[0], False)
    place_coarse(1, cab.at[1], True, (0, 2))
    for p in (*range(-CX, 0), *range(CX, 2 * CX)):
        cab[1, CX + p] = cab[1, CX + p] * in_planes(p)
    coarse_setup(False)
    wait_for(g_waits)
    place_coarse(2, cg, True)

    for p, at_p, span in coarse_blocks(4):
        here = pl.ds(0, span[1])
        g = masked(cg[at_p, here, :], in_planes(p))
        if in_planes(p) is not None:
            cg[at_p, here, :] = g
        update = g * (1.0 / THETA)
        cxs[0, at_p, here, :] = update
        cds[at_p, here, :] = update

    def coarse_residual(now, at_p, span):
        here = pl.ds(0, span[1])
        x = cxs[now, at_p, here, :]
        return (
            cg[at_p, here, :]
            - x
            + spread(
                x, lambda step, part: cxs[now, at_p + step, part[0] : part[1], :], span, CY,
                lambda e: cw[e, at_p, here, :],
            )
        )

    now = 0
    for step, (first, second) in enumerate(terms):
        for p, at_p, span in coarse_blocks(3 - step):
            here = pl.ds(0, span[1])
            update = first * cds[at_p, here, :] + second * coarse_residual(now, at_p, span)
            cds[at_p, here, :] = update
            cxs[1 - now, at_p, here, :] = cxs[now, at_p, here, :] + update
        now = 1 - now

    quarter = []
    for q in range(CX):
        quarter.append(cdiag[q] * coarse_residual(now, CX + q, (0, CY)))
    for h in range(CX // 2):
        both = quarter[2 * h] + quarter[2 * h + 1]
        for t in range(2):
            pair[t, 0:CY, :] = both[:, t * 128 : (t + 1) * 128]
        summed = jnp.concatenate(
            [pair[t, pl.ds(0, CY // 2, 2), :] + pair[t, pl.ds(1, CY // 2, 2), :] for t in range(2)], axis=1
        )
        coarsest[0, h] = 0.125 * halve_z(summed)
    earlier = len(sent)
    l_waits = [
        send(coarsest.at[0], coarsest.at[dx], sl_sem.at[dx], rl_sem.at[dx], dx, 0) for dx in (4, 5, 3, 6, 2, 7, 1)
    ]

    for q in range(CX):
        fine = double_z(cxs[now, CX + q, 0:CY])
        for t in range(4):
            part = fine[:, t * 128 : (t + 1) * 128]
            wide[t, pl.ds(0, CY, 2), :] = part
            wide[t, pl.ds(1, CY, 2), :] = part
        full = jnp.concatenate([wide[t] for t in range(4)], axis=1)
        for p in (2 * q, 2 * q + 1):
            out_ref[p] = cur[PX + p, own_y, :] + full

    for copy, dy in sent[:earlier]:
        when(beside[dy], copy.wait_send)
    for relay, arrives, *_ in corners:
        pl.when(arrives)(relay.wait_send)
    wait_for(l_waits)
    for dx in range(8):
        owner = lax.rem(gx + ngx - dx, ngx)
        last_ref[pl.ds(2 * owner, 2)] = coarsest[dx]
    for copy, _ in l_waits:
        copy.wait_send()


def store(field, last, field_out, last_out, sem):
    copies = [pltpu.make_async_copy(field, field_out, sem.at[0]), pltpu.make_async_copy(last, last_out, sem.at[1])]
    for copy in copies:
        copy.start()
    for copy in copies:
        copy.wait()


def on_device(guess, rhs, alpha, beta):
    vmem = pltpu.VMEM
    dma = pltpu.SemaphoreType.DMA
    fine = (NX, NY, NZ)
    wide = (EX, EY, NZ)
    coarse = (EXC, EYC, CZ)
    scratch = [
        vmem(wide, F32), vmem(wide, F32), vmem(wide, F32), vmem(wide, F32), vmem(wide, F32), vmem(wide, F32),
        vmem(wide, F32), vmem(fine, F32), vmem((6, *wide), F32),
        vmem((2, 18, 8, NZ), F32), vmem((2, 18, 8, NZ), F32), vmem((2, 2, 4, 8, NZ), F32), vmem((2, 2, 4, 8, NZ), F32),
        vmem((4, NY, 128), F32), vmem((4, NY, 128), F32),
        vmem((2, *coarse), F32), vmem(coarse, F32), vmem((3, 2, CX // 2, 8, CZ), F32),
        vmem((3, 2, CX // 2, 8, CZ), F32), vmem((3, 2, 2, 8, CZ), F32), vmem((3, 2, 2, 8, CZ), F32),
        vmem((6, *coarse), F32),
        vmem((2, *coarse), F32), vmem(coarse, F32), vmem((CX, CY, CZ), F32),
        vmem((8, 2, CY // 2, CZ // 2), F32),
        dma((4,)), dma((4, 2)), dma((4, 2)), dma((2, 3)), dma((2, 3)), dma((2, 2)), dma((2, 2)),
        dma((8,)), dma((8,)), dma((8,)), dma((8,)), dma((8,)), dma((8,)),
    ]
    placed = [pltpu.with_memory_space_constraint(x, pltpu.HBM) for x in (guess, rhs, alpha, beta)]
    results = pl.pallas_call(
        kernel,
        out_shape=(
            jax.ShapeDtypeStruct(fine, F32),
            jax.ShapeDtypeStruct((16, CY // 2, CZ // 2), F32),
        ),
        in_specs=[pl.BlockSpec(memory_space=pltpu.HBM)] * 4,
        out_specs=(pl.BlockSpec(memory_space=vmem), pl.BlockSpec(memory_space=vmem)),
        scratch_shapes=scratch,
        compiler_params=pltpu.CompilerParams(
            collective_id=0, has_side_effects=True, vmem_limit_bytes=40 << 20
        ),
        name="vcycle",
    )(*placed)
    return pl.pallas_call(
        store,
        out_shape=(
            jax.ShapeDtypeStruct(fine, F32),
            jax.ShapeDtypeStruct((16, CY // 2, CZ // 2), F32),
        ),
        in_specs=[pl.BlockSpec(memory_space=vmem)] * 2,
        out_specs=(pl.BlockSpec(memory_space=pltpu.HBM), pl.BlockSpec(memory_space=pltpu.HBM)),
        scratch_shapes=[dma((2,))],
        compiler_params=pltpu.CompilerParams(vmem_limit_bytes=4 << 20),
        name="store",
    )(*results)


def solution(mesh):
    placed = (P("gx", "yz", None),) * 4
    return jax.shard_map(
        on_device,
        mesh=mesh,
        in_specs=placed,
        out_specs=(P("gx", "yz", None), P(None, "yz", None)),
        check_vma=False,
    )
```

```python
import functools

import jax
import jax.numpy as jnp
from jax import lax
from jax.experimental import pallas as pl
from jax.experimental.pallas import tpu as pltpu
from jax.sharding import PartitionSpec as P

DEGREE = 4
THETA = 1.125
DELTA = 0.875
MESH = pl.DeviceIdType.MESH
F32 = jnp.float32

NX, NY, NZ = 8, 16, 512
CX, CY, CZ = 4, 8, 256
DEPTH = DEGREE + 1
PX = DEPTH
EX, EY = NX + 2 * DEPTH, NY + 8
EXC, EYC = CX + 2 * DEGREE, CY + 8


def cheb_terms():
    sigma = THETA / DELTA
    rho_prev = 1.0 / sigma
    terms = []
    for _ in range(DEGREE - 1):
        rho_next = 1.0 / (2.0 * sigma - rho_prev)
        terms.append((rho_next * rho_prev, 2.0 * rho_next / DELTA))
        rho_prev = rho_next
    return terms


def lanes(shape):
    return lax.broadcasted_iota(jnp.int32, shape, 1)


def rows(shape):
    return lax.broadcasted_iota(jnp.int32, shape, 0)


def halve_z(field):
    count, width = field.shape
    lane = lanes((count, 128))
    even = jnp.where(lane < 64, 2 * lane, 2 * lane - 128)
    low = lane < 64
    tiles = []
    for t in range(width // 256):
        halves = []
        for h in range(2):
            part = field[:, (2 * t + h) * 128 : (2 * t + h + 1) * 128]
            part = part + pltpu.roll(part, 127, 1)
            halves.append(jnp.take_along_axis(part, even, axis=1))
        tiles.append(jnp.where(low, halves[0], halves[1]))
    return tiles[0] if len(tiles) == 1 else jnp.concatenate(tiles, axis=1)


def double_z(field):
    count, width = field.shape
    half = lanes((count, 128)) // 2
    tiles = []
    for t in range(width // 128):
        part = field[:, t * 128 : (t + 1) * 128]
        tiles.append(jnp.take_along_axis(part, half, axis=1))
        tiles.append(jnp.take_along_axis(part, half + 64, axis=1))
    return jnp.concatenate(tiles, axis=1)


def without_last(field):
    width = field.shape[1]
    tail = field[:, width - 128 :]
    return jnp.concatenate([field[:, : width - 128], jnp.where(lanes(tail.shape) == 127, 0.0, tail)], axis=1)


def without_first(field):
    head = field[:, :128]
    return jnp.concatenate([jnp.where(lanes(head.shape) == 0, 0.0, head), field[:, 128:]], axis=1)


def z_beside(field):
    width = field.shape[1]
    return pltpu.roll(field, width - 1, 1), pltpu.roll(field, 1, 1)


def y_beside(field, below, above):
    count = field.shape[0]
    row = rows(field.shape)
    up = jnp.where(row == count - 1, jnp.broadcast_to(above, field.shape), pltpu.roll(field, count - 1, 0))
    down = jnp.where(row == 0, jnp.broadcast_to(below, field.shape), pltpu.roll(field, 1, 0))
    return up, down


def tile_a(p):
    return 2 * p + (1 if p >= 4 else 0)


def tile_b(p):
    return 2 * p + (0 if p >= 4 else 1)


def kernel(
    guess_h, rhs_h, alpha_h, beta_h, out_ref, last_ref,
    xa, xb, be, al, rh, ds, gs, diag, ws, pk, rk, qk, rc,
    pair, wide, cab, cg, pkc, rkc, pcc, rcc, cw, cxs, cds, cdiag, coarsest,
    load_sem, sx_sem, rx_sem, sy_sem, ry_sem, sc_sem, rc_sem, sab_sem, rab_sem, sg_sem, rg_sem, sl_sem, rl_sem,
):
    gx = lax.axis_index("gx")
    yz = lax.axis_index("yz")
    ngx = lax.axis_size("gx")
    nyz = lax.axis_size("yz")

    def at(dx, dy):
        return (lax.rem(gx + ngx + dx, ngx), lax.rem(yz + nyz + dy, nyz))

    beside = {-1: yz > 0, 0: None, 1: yz < nyz - 1}

    def when(condition, act):
        if condition is None:
            act()
        else:
            pl.when(condition)(act)

    def greet(dx, dy):
        pl.semaphore_signal(barrier, inc=1, device_id=at(dx, dy), device_id_type=MESH)

    own_x, own_y, edge_y = pl.ds(PX, NX), pl.ds(0, NY), pl.ds(NY, 8)
    around = [(-1, -1), (-1, 1), (1, -1), (1, 1), (0, -1), (0, 1), (-1, 0), (1, 0)]
    barrier = pltpu.get_barrier_semaphore()
    for dx, dy in around:
        if dy != 0:
            when(beside[dy], functools.partial(greet, dx, dy))
    loads = []
    for k, (src, dst) in enumerate(((guess_h, xa), (beta_h, be), (alpha_h, al), (rhs_h, rh))):
        copy = pltpu.make_async_copy(src, dst.at[own_x, own_y], load_sem.at[k])
        copy.start()
        loads.append(copy)
    for dx in range(1, 8):
        greet(dx, 0)
    greeted = 7 + 3 * (yz > 0).astype(jnp.int32) + 3 * (yz < nyz - 1).astype(jnp.int32)

    half = rows((8, NZ)) < 4

    def packed(first, second, side):
        moved = pltpu.roll(second, 4, 0)
        return jnp.where(half, moved, first) if side == 0 else jnp.where(half, first, moved)

    odd = lax.rem(gx, 2)

    def pack_rows(half_at):
        for side, start in ((0, 8), (1, 0)):
            tile = pl.ds(start, 8)
            for k in range(4):
                p = 4 * half_at + k
                one = PX + p
                pk[side, 2 * p + half_at] = packed(xa[one, tile, :], be[one, tile, :], side)
                pk[side, 2 * p + 1 - half_at] = packed(al[one, tile, :], rh[one, tile, :], side)

    for copy in loads:
        copy.wait()
    pack_rows(odd)
    for side, missing in ((0, yz == 0), (1, yz == nyz - 1)):

        @pl.when(missing)
        def _(side=side):
            rk[side] = jnp.ones(rk.shape[1:], F32)
            for k in range(3):
                if k < 2:
                    rc[k, side] = jnp.ones(rc.shape[2:], F32)
                    for f in range(3):
                        rcc[f, k, side] = jnp.ones(rcc.shape[3:], F32)
                rkc[k, side] = jnp.ones(rkc.shape[2:], F32)

    pl.semaphore_wait(barrier, greeted)

    sent = []

    def copy_of(src, dst, s_sem, r_sem, device):
        return pltpu.make_async_remote_copy(
            src_ref=src, dst_ref=dst, send_sem=s_sem, recv_sem=r_sem, device_id=device, device_id_type=MESH
        )

    def send(src, dst, s_sem, r_sem, dx, dy):
        copy = copy_of(src, dst, s_sem, r_sem, at(dx, dy))
        when(beside[dy], copy.start)
        sent.append((copy, dy))
        return copy, dy

    def wait_for(copies):
        for copy, dy in copies:
            when(beside[-dy], copy.wait_recv)

    first_core = lax.rem(gx, 2) == 0
    ahead = 8 * odd
    parts = (pl.ds(ahead, 8), pl.ds(8 - ahead, 8), pl.ds(16, 2))

    def send_rows(k):
        part = parts[k]
        return [
            send(pk.at[side, part], rk.at[side, part], sy_sem.at[side, k], ry_sem.at[side, k], 0, 1 - 2 * side)
            for side in (0, 1)
        ]

    y_waits = [send_rows(0)]
    x_waits = []
    for k, (src, dst, deep) in enumerate(
        ((guess_h, xa, DEPTH), (beta_h, be, DEPTH), (alpha_h, al, DEPTH - 1), (rhs_h, rh, DEPTH - 1))
    ):
        x_waits.append(
            send(
                src.at[pl.ds(NX - deep, deep)], dst.at[pl.ds(PX - deep, deep), own_y],
                sx_sem.at[k, 0], rx_sem.at[k, 0], 1, 0,
            )
        )
        x_waits.append(
            send(
                src.at[pl.ds(0, deep)], dst.at[pl.ds(PX + NX, deep), own_y],
                sx_sem.at[k, 1], rx_sem.at[k, 1], -1, 0,
            )
        )

    pack_rows(1 - odd)
    y_waits.append(send_rows(1))
    for side, fifth in ((0, 11), (1, 4)):
        for p in range(NX):
            pk[side, 16, p : p + 1, :] = xa[PX + p, fifth : fifth + 1, :]
            pk[side, 17, p : p + 1, :] = be[PX + p, fifth : fifth + 1, :]
    y_waits.append(send_rows(2))
    sub = rows((8, NZ))
    nearest = [(sub % 4) == 0, (sub % 4) == 3]
    near_two = [(sub % 4) < 2, (sub % 4) >= 2]

    def pack_corner(sx, sy):
        planes = range(7, 3, -1) if sx == 0 else range(4)
        a = [rk[sy, tile_a(p)] for p in planes]
        b = [rk[sy, tile_b(p)] for p in planes]
        one = 1 if sy == 0 else 7
        qk[sx, sy, 0] = a[0]
        qk[sx, sy, 1] = jnp.where(nearest[sy], pltpu.roll(a[3], one, 0), b[0])
        qk[sx, sy, 2] = jnp.where(nearest[sy], pltpu.roll(b[2], one, 0), a[1])
        qk[sx, sy, 3] = jnp.where(near_two[sy], pltpu.roll(a[2], 2, 0), b[1])

    corners = []
    for sx in (0, 1):
        same_chip = first_core if sx == 0 else jnp.logical_not(first_core)
        for sy in (0, 1):
            relay = copy_of(qk.at[sx, sy], rc.at[sx, sy], sc_sem.at[sx, sy], rc_sem.at[sx, sy], at(1 - 2 * sx, 0))
            corners.append((relay, beside[2 * sy - 1], sx, sy, same_chip))

    def pass_on(side, on_chip):
        for relay, arrives, sx, sy, same_chip in corners:
            if sy == side:
                chosen = same_chip if on_chip else jnp.logical_not(same_chip)

                @pl.when(jnp.logical_and(arrives, chosen))
                def _(relay=relay, sx=sx, sy=sy):
                    pack_corner(sx, sy)
                    relay.start()

    def restrict_pair(first, second):
        both = first + second
        for t in range(4):
            pair[t] = both[:, t * 128 : (t + 1) * 128]
        summed = jnp.concatenate(
            [pair[t, pl.ds(0, CY, 2), :] + pair[t, pl.ds(1, CY, 2), :] for t in range(4)], axis=1
        )
        return halve_z(summed)

    csub = rows((8, CZ))
    chalf = csub < 4

    def pack_coarse(f, get):
        for q in range(0, CX, 2):
            this, then = get(q), pltpu.roll(get(q + 1), 4, 0)
            pkc[f, 0, q // 2] = jnp.where(chalf, then, this)
            pkc[f, 1, q // 2] = jnp.where(chalf, this, then)
        for ix, (tile, third, slots_at) in enumerate(((1, 1, (4, 3)), (0, 2, (0, 7)))):
            near = get(third)
            for side, row in ((0, near[CY - 1 : CY]), (1, near[0:1])):
                pcc[f, ix, side] = jnp.where(
                    csub == slots_at[side], jnp.broadcast_to(row, (8, CZ)), pkc[f, side, tile]
                )

    def exchange_coarse(fields, own, others, s_sem, r_sem):
        copies = []
        for k, (dx, dy) in enumerate(around):
            if dy == 0:
                src, dst = own, others[1 - dx]
            else:
                side = (1 - dy) // 2
                if dx == 0:
                    src, dst = pkc.at[fields, side], rkc.at[fields, side]
                else:
                    ix = (1 - dx) // 2
                    src, dst = pcc.at[fields, ix, side], rcc.at[fields, ix, side]
            copies.append(send(src, dst, s_sem.at[k], r_sem.at[k], dx, dy))
        return copies

    for q in range(CX):
        one, two = PX + 2 * q, PX + 2 * q + 1
        cab[0, CX + q, 0:CY] = 0.125 * restrict_pair(al[one, own_y, :], al[two, own_y, :])
        cab[1, CX + q, 0:CY] = 0.125 * restrict_pair(be[one, own_y, :], be[two, own_y, :])
    for f in range(2):
        pack_coarse(f, lambda q, f=f: cab[f, CX + q, 0:CY])
    in_lo_x = (gx > 0).astype(F32)
    in_hi_x = (gx < ngx - 1).astype(F32)
    in_lo_y = (yz > 0).astype(F32)
    in_hi_y = (yz < nyz - 1).astype(F32)
    terms = cheb_terms()

    def join(below, above):
        return jnp.where(half, above, below)

    def place(plane, a_below, a_above, b_below=None, b_above=None):
        a_below, a_above = a_below * in_lo_y, a_above * in_hi_y
        xa[plane, edge_y, :] = join(a_below, a_above)
        be[plane, edge_y, :] = pltpu.roll(join(a_above, a_below), 4, 0)
        if b_below is not None:
            al[plane, edge_y, :] = join(b_below, b_above)
            rh[plane, edge_y, :] = pltpu.roll(join(b_above, b_below), 4, 0)

    def place_rows():
        for p in range(NX):
            place(PX + p, rk[0, tile_a(p)], rk[1, tile_a(p)], rk[0, tile_b(p)], rk[1, tile_b(p)])

    def fill_edges():
        for edge, start in ((gx == 0, 0), (gx == ngx - 1, PX + NX)):

            @pl.when(edge)
            def _(start=start):
                for plane in range(start, start + DEPTH):
                    xa[plane] = jnp.zeros((EY, NZ), F32)
                    be[plane] = jnp.zeros((EY, NZ), F32)

    def place_corners():
        for sx in (0, 1):
            tiles = [[rc[sx, sy, k] for sy in (0, 1)] for k in range(4)]

            def back(k):
                return [pltpu.roll(tiles[k][0], 7, 0), pltpu.roll(tiles[k][1], 1, 0)]

            blocks = (
                [*tiles[0], *tiles[1]],
                [*tiles[2], *tiles[3]],
                [*(pltpu.roll(tile, 6, 0) for tile in tiles[3]), *back(2)],
                back(1),
            )
            for k, block in enumerate(blocks):
                place(PX - 1 - k if sx == 0 else PX + NX + k, *block)
        fill_edges()

    def fine_blocks(deep):
        found = []
        for p in range(-deep, NX + deep):
            beyond = max(-p, p - NX + 1, 0)
            found.append((p, (0, EY) if beyond < deep else (0, NY)))
        return found

    def along_y(x, at_row, span, own, fifth=None):
        count = own + 8
        if span == (0, own):
            return y_beside(x, at_row(count - 1), at_row(own))
        if span == (own, count):
            up, down = y_beside(x, at_row(own - 1), at_row(0))
            if fifth is not None:
                row = rows(x.shape)
                up = jnp.where(row == 3, jnp.broadcast_to(fifth[1], x.shape), up)
                down = jnp.where(row == 4, jnp.broadcast_to(fifth[0], x.shape), down)
            return up, down
        up, down = pltpu.roll(x, count - 1, 0), pltpu.roll(x, 1, 0)
        if fifth is not None:
            row = rows(x.shape)
            up = jnp.where(row == own + 3, jnp.broadcast_to(fifth[1], x.shape), up)
            down = jnp.where(row == own + 4, jnp.broadcast_to(fifth[0], x.shape), down)
        return up, down

    def spread(x, x_at, span, own, w, fifth=None):
        up, down = along_y(x, lambda row: x_at(0, (row, row + 1)), span, own, fifth)
        right, left = z_beside(x)
        return (
            w(0) * x_at(1, span) + w(1) * x_at(-1, span) + w(2) * up + w(3) * down + w(4) * right + w(5) * left
        )

    def in_rows(value, own):
        tail = value[own:]
        inside = jnp.where(rows(tail.shape) < 4, in_hi_y, in_lo_y)
        return jnp.concatenate([value[:own], tail * inside], axis=0)

    def first_step(p, span):
        lo, hi = span
        here = pl.ds(lo, hi - lo)
        b = be[PX + p, here, :]
        fifth = fifth_b = None
        if 0 <= p < NX:
            part = slice(p, p + 1)
            fifth = (rk[0, 16, part, :] * in_lo_y, rk[1, 16, part, :] * in_hi_y)
            fifth_b = (rk[0, 17, part, :] * in_lo_y, rk[1, 17, part, :] * in_hi_y)
        b_up, b_down = along_y(b, lambda row: be[PX + p, row : row + 1, :], span, NY, fifth_b)
        b_right, b_left = z_beside(b)
        b_right = without_last(b_right)
        b_left = without_first(b_left)
        pairs = [
            b + other for other in (be[PX + p + 1, here, :], be[PX + p - 1, here, :], b_up, b_down, b_right, b_left)
        ]
        total = pairs[0] + pairs[1] + pairs[2] + pairs[3] + pairs[4] + pairs[5]
        whole = al[PX + p, here, :] + 0.5 * total
        if 0 <= p < NX and lo == 0:
            diag[p] = whole[0:NY]
        inverse = 1.0 / whole
        if p < 0:
            inverse = inverse * in_lo_x
        if p >= NX:
            inverse = inverse * in_hi_x
        if span == (0, EY):
            inverse = in_rows(inverse, NY)
        if span == (NY, EY):
            inverse = inverse * jnp.where(rows(inverse.shape) < 4, in_hi_y, in_lo_y)
        scale = 0.5 * inverse
        w = [scale * pair for pair in pairs]
        w[4] = without_last(w[4])
        w[5] = without_first(w[5])
        for e in range(6):
            ws[e, PX + p, here, :] = w[e]
        g = inverse * rh[PX + p, here, :]
        gs[PX + p, here, :] = g
        x = xa[PX + p, here, :]
        resid = g - x + spread(x, lambda step, part: xa[PX + p + step, part[0] : part[1], :], span, NY, lambda e: w[e], fifth)
        update = resid * (1.0 / THETA)
        ds[PX + p, here, :] = update
        xb[PX + p, here, :] = x + update

    def residual(cur, p, span):
        here = pl.ds(span[0], span[1] - span[0])
        x = cur[PX + p, here, :]
        return (
            gs[PX + p, here, :]
            - x
            + spread(
                x, lambda step, part: cur[PX + p + step, part[0] : part[1], :], span, NY,
                lambda e: ws[e, PX + p, here, :],
            )
        )

    def coarse_blocks(deep):
        found = []
        for p in range(-deep, CX + deep):
            beyond = max(-p, p - CX + 1, 0)
            found.append((p, CX + p, (0, EYC) if beyond < deep else (0, CY)))
        return found

    def in_planes(p):
        return in_lo_x if p < 0 else in_hi_x if p >= CX else None

    def masked(value, mask):
        return value if mask is None else value * mask

    def place_coarse(f, field, inside, slots=(0, 1, 2)):
        def inner(below, above):
            return (below * in_lo_y, above * in_hi_y) if inside else (below, above)

        def join_rows(plane, below, above):
            field[plane, pl.ds(CY, 8), :] = jnp.where(chalf, above, below)
            field[plane + 1, pl.ds(CY, 8), :] = pltpu.roll(jnp.where(chalf, below, above), 4, 0)

        for k in slots:
            if k == 1:
                for q in range(0, CX, 2):
                    join_rows(CX + q, *inner(rkc[f, 0, q // 2], rkc[f, 1, q // 2]))
                continue
            ix = k // 2
            below, above = inner(rcc[f, ix, 0], rcc[f, ix, 1])
            join_rows(2 if ix == 0 else 2 * CX, below, above)
            low, high = (4, 3) if ix == 0 else (0, 7)
            field[1 if ix == 0 else 2 * CX + 2, pl.ds(CY, 8), :] = jnp.where(
                chalf,
                jnp.broadcast_to(above[high : high + 1], (8, CZ)),
                jnp.broadcast_to(below[low : low + 1], (8, CZ)),
            )

    def coarse_setup(own_only):
        for p, at_p, span in coarse_blocks(0 if own_only else 3):
            here = pl.ds(0, span[1])
            b = cab[1, at_p, here, :]
            b_up, b_down = along_y(b, lambda row: cab[1, at_p, row : row + 1, :], span, CY)
            b_right, b_left = z_beside(b)
            b_right = without_last(b_right)
            b_left = without_first(b_left)
            faces = [
                0.5 * (b + other)
                for other in (cab[1, at_p + 1, here, :], cab[1, at_p - 1, here, :], b_up, b_down, b_right, b_left)
            ]
            total = faces[0] + faces[1] + faces[2] + faces[3] + faces[4] + faces[5]
            whole = cab[0, at_p, here, :] + 0.25 * total
            if own_only:
                cdiag[p] = whole
                continue
            scale = masked(0.25 / whole, in_planes(p))
            if span == (0, EYC):
                scale = in_rows(scale, CY)
            w = [scale * face for face in faces]
            w[4] = without_last(w[4])
            w[5] = without_first(w[5])
            for e in range(6):
                cw[e, at_p, here, :] = w[e]

    def later_step(step, p, span):
        cur, other = (xb, xa) if step % 2 == 1 else (xa, xb)
        first, second = terms[step - 1]
        here = pl.ds(span[0], span[1] - span[0])
        update = first * ds[PX + p, here, :] + second * residual(cur, p, span)
        ds[PX + p, here, :] = update
        other[PX + p, here, :] = cur[PX + p, here, :] + update

    def fine_step(step, chosen):
        for p, span in fine_blocks(DEPTH - 1 - step):
            if p in (step, NX - 1 - step):
                later_step(step, p, (0, NY) if chosen else (NY, EY))
            elif (step < p < NX - 1 - step) == chosen:
                later_step(step, p, span)

    for side in (0, 1):
        wait_for(y_waits[0][side : side + 1])
        pass_on(side, False)
    slots = [pl.ds(k * CX, CX) for k in range(3)]
    ab_waits = exchange_coarse(
        pl.ds(0, 2), cab.at[:, slots[1], pl.ds(0, CY)],
        [cab.at[:, slot, pl.ds(0, CY)] for slot in slots], sab_sem, rab_sem,
    )
    for side in (0, 1):
        wait_for(y_waits[1][side : side + 1])
        pass_on(side, True)
    place_rows()
    wait_for(x_waits)
    fill_edges()
    for p in range(NX):
        first_step(p, (0, NY))
    wait_for(y_waits[2])
    for p in range(1, NX - 1):
        first_step(p, (NY, EY))
    for step in range(1, DEGREE):
        fine_step(step, True)
    for relay, arrives, *_ in corners:
        pl.when(arrives)(relay.wait_recv)
    place_corners()
    for p, span in fine_blocks(DEPTH - 1):
        if not 0 <= p < NX:
            first_step(p, span)
        elif p in (0, NX - 1):
            first_step(p, (NY, EY))
    for step in range(1, DEGREE):
        fine_step(step, False)
    cur = xa if DEGREE % 2 == 0 else xb
    own = (0, NY)
    wait_for(ab_waits[4:])
    place_coarse(1, cab.at[1], True, (1,))
    for p in (-1, CX):
        cab[1, CX + p, 0:CY] = cab[1, CX + p, 0:CY] * in_planes(p)
    coarse_setup(True)
    for q in range(CX):
        a = diag[2 * q] * residual(cur, 2 * q, own)
        b = diag[2 * q + 1] * residual(cur, 2 * q + 1, own)
        cg[CX + q, 0:CY] = 0.125 * restrict_pair(a, b) / cdiag[q]

    pack_coarse(2, lambda q: cg[CX + q, 0:CY])
    g_waits = exchange_coarse(
        2, cg.at[slots[1], pl.ds(0, CY)], [cg.at[slot, pl.ds(0, CY)] for slot in slots], sg_sem, rg_sem
    )
    wait_for(ab_waits[:4])
    place_coarse(0, cab.at[0], False)
    place_coarse(1, cab.at[1], True, (0, 2))
    for p in (*range(-CX, 0), *range(CX, 2 * CX)):
        cab[1, CX + p] = cab[1, CX + p] * in_planes(p)
    coarse_setup(False)
    wait_for(g_waits)
    place_coarse(2, cg, True)

    for p, at_p, span in coarse_blocks(4):
        here = pl.ds(0, span[1])
        g = masked(cg[at_p, here, :], in_planes(p))
        if in_planes(p) is not None:
            cg[at_p, here, :] = g
        update = g * (1.0 / THETA)
        cxs[0, at_p, here, :] = update
        cds[at_p, here, :] = update

    def coarse_residual(now, at_p, span):
        here = pl.ds(0, span[1])
        x = cxs[now, at_p, here, :]
        return (
            cg[at_p, here, :]
            - x
            + spread(
                x, lambda step, part: cxs[now, at_p + step, part[0] : part[1], :], span, CY,
                lambda e: cw[e, at_p, here, :],
            )
        )

    now = 0
    for step, (first, second) in enumerate(terms):
        for p, at_p, span in coarse_blocks(3 - step):
            here = pl.ds(0, span[1])
            update = first * cds[at_p, here, :] + second * coarse_residual(now, at_p, span)
            cds[at_p, here, :] = update
            cxs[1 - now, at_p, here, :] = cxs[now, at_p, here, :] + update
        now = 1 - now

    quarter = []
    for q in range(CX):
        quarter.append(cdiag[q] * coarse_residual(now, CX + q, (0, CY)))
    for h in range(CX // 2):
        both = quarter[2 * h] + quarter[2 * h + 1]
        for t in range(2):
            pair[t, 0:CY, :] = both[:, t * 128 : (t + 1) * 128]
        summed = jnp.concatenate(
            [pair[t, pl.ds(0, CY // 2, 2), :] + pair[t, pl.ds(1, CY // 2, 2), :] for t in range(2)], axis=1
        )
        coarsest[0, h] = 0.125 * halve_z(summed)
    earlier = len(sent)
    l_waits = [
        send(coarsest.at[0], coarsest.at[dx], sl_sem.at[dx], rl_sem.at[dx], dx, 0) for dx in (4, 5, 3, 6, 2, 7, 1)
    ]

    for q in range(CX):
        fine = double_z(cxs[now, CX + q, 0:CY])
        for t in range(4):
            part = fine[:, t * 128 : (t + 1) * 128]
            wide[t, pl.ds(0, CY, 2), :] = part
            wide[t, pl.ds(1, CY, 2), :] = part
        full = jnp.concatenate([wide[t] for t in range(4)], axis=1)
        for p in (2 * q, 2 * q + 1):
            out_ref[p] = cur[PX + p, own_y, :] + full

    for copy, dy in sent[:earlier]:
        when(beside[dy], copy.wait_send)
    for relay, arrives, *_ in corners:
        pl.when(arrives)(relay.wait_send)
    wait_for(l_waits)
    for dx in range(8):
        owner = lax.rem(gx + ngx - dx, ngx)
        last_ref[pl.ds(2 * owner, 2)] = coarsest[dx]
    for copy, _ in l_waits:
        copy.wait_send()


def store(field, last, field_out, last_out, sem):
    copies = [pltpu.make_async_copy(field, field_out, sem.at[0]), pltpu.make_async_copy(last, last_out, sem.at[1])]
    for copy in copies:
        copy.start()
    for copy in copies:
        copy.wait()


def on_device(guess, rhs, alpha, beta):
    vmem = pltpu.VMEM
    dma = pltpu.SemaphoreType.DMA
    fine = (NX, NY, NZ)
    wide = (EX, EY, NZ)
    coarse = (EXC, EYC, CZ)
    scratch = [
        vmem(wide, F32), vmem(wide, F32), vmem(wide, F32), vmem(wide, F32), vmem(wide, F32), vmem(wide, F32),
        vmem(wide, F32), vmem(fine, F32), vmem((6, *wide), F32),
        vmem((2, 18, 8, NZ), F32), vmem((2, 18, 8, NZ), F32), vmem((2, 2, 4, 8, NZ), F32), vmem((2, 2, 4, 8, NZ), F32),
        vmem((4, NY, 128), F32), vmem((4, NY, 128), F32),
        vmem((2, *coarse), F32), vmem(coarse, F32), vmem((3, 2, CX // 2, 8, CZ), F32),
        vmem((3, 2, CX // 2, 8, CZ), F32), vmem((3, 2, 2, 8, CZ), F32), vmem((3, 2, 2, 8, CZ), F32),
        vmem((6, *coarse), F32),
        vmem((2, *coarse), F32), vmem(coarse, F32), vmem((CX, CY, CZ), F32),
        vmem((8, 2, CY // 2, CZ // 2), F32),
        dma((4,)), dma((4, 2)), dma((4, 2)), dma((2, 3)), dma((2, 3)), dma((2, 2)), dma((2, 2)),
        dma((8,)), dma((8,)), dma((8,)), dma((8,)), dma((8,)), dma((8,)),
    ]
    placed = [pltpu.with_memory_space_constraint(x, pltpu.HBM) for x in (guess, rhs, alpha, beta)]
    results = pl.pallas_call(
        kernel,
        out_shape=(
            jax.ShapeDtypeStruct(fine, F32),
            jax.ShapeDtypeStruct((16, CY // 2, CZ // 2), F32),
        ),
        in_specs=[pl.BlockSpec(memory_space=pltpu.HBM)] * 4,
        out_specs=(pl.BlockSpec(memory_space=vmem), pl.BlockSpec(memory_space=vmem)),
        scratch_shapes=scratch,
        compiler_params=pltpu.CompilerParams(
            collective_id=0, has_side_effects=True, vmem_limit_bytes=40 << 20
        ),
        name="vcycle",
    )(*placed)
    return pl.pallas_call(
        store,
        out_shape=(
            jax.ShapeDtypeStruct(fine, F32),
            jax.ShapeDtypeStruct((16, CY // 2, CZ // 2), F32),
        ),
        in_specs=[pl.BlockSpec(memory_space=vmem)] * 2,
        out_specs=(pl.BlockSpec(memory_space=pltpu.HBM), pl.BlockSpec(memory_space=pltpu.HBM)),
        scratch_shapes=[dma((2,))],
        compiler_params=pltpu.CompilerParams(vmem_limit_bytes=4 << 20),
        name="store",
    )(*results)


def solution(mesh):
    placed = (P("gx", "yz", None),) * 4
    return jax.shard_map(
        on_device,
        mesh=mesh,
        in_specs=placed,
        out_specs=(P("gx", "yz", None), P(None, "yz", None)),
        check_vma=False,
    )
```
